128 devices in a mesh: section: 2 (over core), dp: 16 (over y, x), mp: 4 (over z).
Axes of the slice: x: 4, y: 4, z: 4, core: 2. Of those that a mesh axis runs over, the one named last changes fastest.
Arguments:
- patches: bfloat16 [8192, 1280], P(('section', 'dp', 'mp')), may hold values from -6 to 6
- image_units: int32 [128, 3], P(('section', 'dp', 'mp')), may hold values from 1 to 8, 16 in all within a row
- v_gain: float32 [1280], replicated, may hold values from 0.5 to 1.5
- v_qkv: bfloat16 [1280, 3840], replicated, may hold values from -0.15625 to 0.15625
- v_out: bfloat16 [1280, 1280], replicated, may hold values from -0.15625 to 0.15625
- merge_gain: float32 [1280], replicated, may hold values from 0.5 to 1.5
- w_merge: bfloat16 [5120, 8192], P('dp', 'mp'), may hold values from -0.078125 to 0.078125
- routes: int32 [2048, 1], P(('section', 'dp', 'mp')), may hold values from 0 to 15; in each aligned block of 1024 rows (0 to 1023, 1024 to 2047, ...) at most 128 rows name the same one
- text: bfloat16 [4096, 8192], P(('section', 'dp'), 'mp'), may hold values from -6 to 6
- seq_lengths: int32 [32, 3], P(('section', 'dp')), may hold values from 1 to 64, 128 in all within a row
- lang_gain: float32 [2, 8192], P('section'), may hold values from 0.5 to 1.5
- w_qkv: bfloat16 [2, 8192, 5120], P('section', 'dp', 'mp'), may hold values from -0.0625 to 0.0625
- wo_t: bfloat16 [2, 8192, 4096], P('section', 'dp', 'mp'), may hold values from -0.09375 to 0.09375
- row_grads: bfloat16 [4096, 8192], P(('section', 'dp'), 'mp'), may hold values from -6 to 6
Outputs:
- final_hidden: bfloat16 [4096, 8192], P(('section', 'dp'), 'mp')
- merged_grads: bfloat16 [2048, 8192], P(('section', 'dp', 'mp'))
The draws below stay inside these ranges and needn't reach their ends.
Inputs may be any that keep to these rules, and one draw needn't show every extreme that they name: `image_units`: each row sums to 16. `routes`: among the 1024 rows of one section index (aligned blocks), at most 128 name one group; in some section index one group is named by exactly 128. `seq_lengths`: each row sums to 128.
All inputs are finite; a program needn't handle non-finite values.
Results may differ from the reference program's by a relative error of at most 0.03.
Values may be sent and summed in bfloat16 or wider, within the bound.
A program may use at most 192 MiB of HBM per device.

```python
import math
import jax
import jax.numpy as jnp
import numpy as np
from jax import lax

D = 8192
QH = 32
KVH = 4
HD = 128
VD = 1280
VH = 16
VHD = 80
MERGE = 4
IMG_DEV = 3
SEQ_MB = 3
R_DEV = 16
MERGE_IN = 5120
QKV_W = 5120
TOK = 128
ROWS_SECTION = 1024
VROWS = 2048
PATCHES = 8192
LTOK = 4096
N_SECTION = 2
N_DP = 16
N_MP = 4


def block_scale(own_key, dims, shards, low, high):
    def one(axis_at, blocks):
        draws = jax.random.uniform(jax.random.fold_in(jax.random.fold_in(own_key, 6), axis_at), (blocks,), jnp.float32, low / len(shards), high / len(shards))
        return jnp.repeat(jnp.exp(draws), dims[axis_at] // blocks).reshape((-1,) + (1,) * (len(dims) - axis_at - 1))

    gain = one(*shards[0])
    for cut in shards[1:]:
        gain = gain * one(*cut)
    return gain


def profile(number_of, total, bound, lean):
    portions = [(1 << 20) // math.isqrt(standing ** lean) + 1 for standing in range(2, number_of + 1)]
    spare, given = total - bound - (number_of - 1), [1] * (number_of - 1)
    while spare > 0:
        movable = [i for i in range(number_of - 1) if given[i] < bound]
        pool, left = sum([portions[i] for i in movable]), spare
        for i in movable:
            addition = min(bound - given[i], max(1, left * portions[i] // pool), spare)
            given[i] = given[i] + addition
            spare = spare - addition
    return np.array([bound] + given)


def uneven(rng, count, total, most, skew):
    if count == 2:
        one = jax.random.randint(rng, (), max(1, total - most), min(most, total - 1) + 1)
        return jnp.stack([one, total - one])
    tallies = jnp.asarray(profile(count, total, most, skew), jnp.int32)
    pairs = (count - 1) // 2
    source_of, taker = tallies[1:1 + 2 * pairs:2], tallies[2:2 + 2 * pairs:2]
    margin = jnp.minimum(source_of - 1, most - taker)
    passed = jax.random.randint(jax.random.fold_in(rng, 1), (pairs,), 0, 1 << 20) % (margin + 1)
    tallies = tallies.at[1:1 + 2 * pairs:2].set(source_of - passed).at[2:2 + 2 * pairs:2].set(taker + passed)
    return tallies[jax.random.permutation(jax.random.fold_in(rng, 2), count)]


def assign_block(own_key, own, number, rows, count, top, reach, slope):
    sequence = jax.random.permutation(own_key, count)
    packed, usual = portions_of(count, rows * top, reach, slope, True), portions_of(count, rows * top, reach, slope, False)
    places = jnp.arange(count)

    def named(sizes, offset_by):
        used = int((sizes > 0).sum())
        fixed = max(1, used // 4)
        shifted = fixed + (places - fixed + offset_by * (used - fixed)) % max(1, count - fixed)
        return jnp.zeros((count,), jnp.int32).at[sequence[jnp.where(places < fixed, places, shifted)]].set(jnp.asarray(sizes, jnp.int32))

    sizes = jnp.where(number % 4 == 0, named(packed, number // 4), named(usual, number - number // 4 - 1))
    mixed = jax.random.permutation(jax.random.fold_in(own, 3), count)
    source_of, receiver = mixed[0:count // 2 * 2:2], mixed[1:count // 2 * 2:2]
    slack = jnp.minimum(sizes[source_of] - 1, reach - sizes[receiver]) // 2
    slack = jnp.where((source_of == sequence[0]) | (receiver == sequence[0]) | (sizes[receiver] == 0), 0, jnp.maximum(slack, 0))
    shifted = jax.random.randint(jax.random.fold_in(own, 4), (count // 2,), 0, 1 << 20) % (slack + 1)
    sizes = sizes.at[source_of].add(-shifted).at[receiver].add(shifted)
    labels = jnp.searchsorted(jnp.cumsum(sizes), jnp.arange(rows * top), side="right").astype(jnp.int32)
    table = labels.reshape(top, rows).T
    table = table[jax.random.permutation(jax.random.fold_in(own, 1), rows)]
    offset_by = jax.random.randint(jax.random.fold_in(own, 2), (rows, 1), 0, top)
    return jnp.take_along_axis(table, (jnp.arange(top)[None, :] + offset_by) % top, axis=1)


def portions_of(number_of, total, most, slope, full):
    portions = [(1 << 20) // math.isqrt(grade ** slope) + 1 for grade in range(1, number_of + 1)]
    largest = most if full else min(most, max(-(-total // number_of), total * portions[0] // sum(portions)))
    least = 1 if total - largest >= number_of - 1 else 0
    holding, surplus = [largest] + [least] * (number_of - 1), total - largest - least * (number_of - 1)
    while surplus > 0:
        movable = [i for i in range(1, number_of) if holding[i] < largest] or [i for i in range(1, number_of) if holding[i] < most]
        mass, remaining = sum([portions[i] for i in movable]), surplus
        for i in movable:
            extra = min(most - holding[i], max(1, remaining * portions[i] // mass), surplus)
            holding[i] = holding[i] + extra
            surplus = surplus - extra
    return np.array(holding)


def scatter_about(key, shape, scale, bound, pieces=(), kind=jnp.bfloat16):
    array = jax.random.normal(key, shape, jnp.float32) * scale
    if len(pieces) > 0:
        array = block_scale(key, shape, pieces, -0.22, 0.18) * array
    return jnp.clip(array, min=-bound, max=bound).astype(kind)


def setup_inputs(seed: int = 0) -> dict:
    key_list = jax.random.split(jax.random.key(seed), 15)
    patches = scatter_about(key_list[0], (PATCHES, VD), 1.0, 6.0, ((0, 128),))
    image_units = jax.vmap(lambda own: uneven(own, IMG_DEV, R_DEV, R_DEV // 2, 2))(jax.random.split(key_list[1], (N_SECTION * N_DP * N_MP))).reshape((N_SECTION * N_DP * N_MP, IMG_DEV)).astype(jnp.int32)
    v_gain = jnp.clip(1.0 + 0.1 * jax.random.normal(key_list[2], (VD,), jnp.float32), 0.5, 1.5)
    v_qkv = scatter_about(key_list[3], (VD, 3 * VD), VD ** -0.5, 0.15625)
    v_out = scatter_about(key_list[4], (VD, VD), VD ** -0.5, 0.15625)
    merge_gain = jnp.clip(1.0 + 0.1 * jax.random.normal(key_list[5], (VD,), jnp.float32), 0.5, 1.5)
    w_merge = scatter_about(key_list[6], (MERGE_IN, D), MERGE_IN ** -0.5, 0.078125, ((0, 16), (1, 4)))
    routes_keys = jax.random.split(jax.random.fold_in(key_list[7], 1), VROWS // ROWS_SECTION)
    routes_turns = jax.random.permutation(jax.random.fold_in(key_list[7], 3), VROWS // ROWS_SECTION)
    routes = jax.vmap(lambda own, number: assign_block(jax.random.fold_in(key_list[7], 2), own, number, ROWS_SECTION, N_DP, 1, TOK, 2))(routes_keys, routes_turns).reshape((VROWS, 1))
    text = scatter_about(key_list[8], (LTOK, D), 1.0, 6.0, ((0, 32), (1, 4)))
    seq_lengths = jax.vmap(lambda own: uneven(own, SEQ_MB, TOK, TOK // 2, 2))(jax.random.split(key_list[9], (N_SECTION * N_DP))).reshape((N_SECTION * N_DP, SEQ_MB)).astype(jnp.int32)
    lang_gain = jnp.clip(1.0 + 0.1 * jax.random.normal(key_list[10], (N_SECTION, D), jnp.float32), 0.5, 1.5)
    w_qkv = scatter_about(key_list[11], (N_SECTION, D, QKV_W), D ** -0.5, 0.0625, ((0, 2), (1, 16), (2, 4)))
    wo_t = scatter_about(key_list[12], (N_SECTION, D, QH * HD), (QH * HD) ** -0.5, 0.09375, ((0, 2), (1, 16), (2, 4)))
    row_grads = scatter_about(key_list[13], (LTOK, D), 1.0, 6.0, ((0, 32), (1, 4)))
    return dict(patches=patches, image_units=image_units, v_gain=v_gain, v_qkv=v_qkv, v_out=v_out, merge_gain=merge_gain, w_merge=w_merge, routes=routes, text=text, seq_lengths=seq_lengths, lang_gain=lang_gain, w_qkv=w_qkv, wo_t=wo_t, row_grads=row_grads)


EPSILON = 1e-06

def layer_norm(values, norm_gain):
    values = values.astype(jnp.float32)
    centre = lax.optimization_barrier(jnp.mean(values, axis=-1, keepdims=True))
    centred = values - centre
    variance = lax.optimization_barrier(jnp.mean(centred * centred, axis=-1, keepdims=True))
    return centred * lax.rsqrt(variance + EPSILON) * norm_gain.astype(jnp.float32)

def rms_norm(values, norm_gain):
    values = values.astype(jnp.float32)
    return values * lax.rsqrt(lax.optimization_barrier(jnp.mean(values * values, axis=-1, keepdims=True)) + EPSILON) * norm_gain.astype(jnp.float32)

def segment_of(lengths, amount):
    boundary = jnp.cumsum(lengths.astype(jnp.int32))
    positions = jnp.arange(amount, dtype=jnp.int32)
    return lax.optimization_barrier(jnp.sum((positions[:, None] >= boundary[None, :]).astype(jnp.int32), axis=1))

def vision_block(patches, units, v_gain, v_qkv, v_out, merge_gain):
    amount = patches.shape[0]
    merged_count = amount // MERGE
    unit_image = segment_of(units, merged_count)
    image_ids = jnp.broadcast_to(unit_image[:, None], (merged_count, MERGE)).reshape(amount)
    v_normed = layer_norm(patches, v_gain).astype(jnp.bfloat16)
    projected = jnp.dot(v_normed, v_qkv, preferred_element_type=jnp.float32).astype(jnp.bfloat16)
    projected = projected.reshape(amount, 3, VH, VHD).astype(jnp.float32)
    scores = jnp.einsum('qhd,khd->hqk', projected[:, 0], projected[:, 1]) / math.sqrt(VHD)
    allowed = image_ids[:, None] == image_ids[None, :]
    scores = jnp.where(allowed[None], scores, -1e+30)
    weights = jax.nn.softmax(scores, axis=-1).astype(jnp.bfloat16)
    attended = jnp.einsum('hqk,khd->qhd', weights.astype(jnp.float32), projected[:, 2]).astype(jnp.bfloat16).reshape(amount, VD)
    update = jnp.dot(attended, v_out, preferred_element_type=jnp.float32)
    v_hidden = (patches.astype(jnp.float32) + update).astype(jnp.bfloat16)
    merged = layer_norm(v_hidden, merge_gain).astype(jnp.bfloat16)
    return merged.reshape(merged_count, MERGE * VD)

def attend(projected, lengths):
    seq_rows = projected.shape[0]
    group_size = QH // KVH
    kv_here = projected.shape[1] // ((group_size + 2) * HD)
    heads_view = projected.reshape(seq_rows, kv_here, group_size + 2, HD).astype(jnp.float32)
    scores = jnp.einsum('tkgd,skd->kgts', heads_view[:, :, :group_size], heads_view[:, :, group_size]) * (1.0 / math.sqrt(HD))
    seq_ids = segment_of(lengths, seq_rows)
    positions = jnp.arange(seq_rows, dtype=jnp.int32)
    allowed = (seq_ids[:, None] == seq_ids[None, :]) & (positions[:, None] >= positions[None, :])
    scores = jnp.where(allowed[None, None], scores, -1e+30)
    weights = jax.nn.softmax(scores, axis=-1).astype(jnp.bfloat16)
    attended = jnp.einsum('kgts,skd->tkgd', weights.astype(jnp.float32), heads_view[:, :, group_size + 1]).astype(jnp.bfloat16)
    return attended.reshape(seq_rows, kv_here * group_size * HD)

def language_layer(hidden, norm_gain, w_qkv, wo_t, lengths):
    normed = rms_norm(hidden, norm_gain).astype(jnp.bfloat16)
    projected = jnp.dot(normed, w_qkv, preferred_element_type=jnp.float32).astype(jnp.bfloat16)
    attended = attend(projected, lengths)
    width = QH * HD // N_MP
    summed = jnp.zeros((hidden.shape[0], D), jnp.float32)
    for group_index in range(N_MP):
        partial_value = jnp.dot(attended[:, group_index * width:(group_index + 1) * width], wo_t[:, group_index * width:(group_index + 1) * width].T, preferred_element_type=jnp.float32)
        rounded = lax.optimization_barrier(partial_value.astype(jnp.bfloat16))
        summed = summed + rounded.astype(jnp.float32)
    return (hidden.astype(jnp.float32) + summed).astype(jnp.bfloat16)

def reference(patches, image_units, v_gain, v_qkv, v_out, merge_gain, w_merge, routes, text, seq_lengths, lang_gain, w_qkv, wo_t, row_grads):
    devices_all = image_units.shape[0]
    per_device = patches.shape[0] // devices_all
    blocks = patches.reshape(devices_all, per_device, VD)

    def encode(block_item):
        return vision_block(block_item[0], block_item[1], v_gain, v_qkv, v_out, merge_gain)
    merged = lax.map(encode, (blocks, image_units)).reshape(VROWS, MERGE_IN)
    rows = jnp.dot(merged, w_merge, preferred_element_type=jnp.float32).astype(jnp.bfloat16)
    target = routes[:, 0].reshape(N_SECTION, ROWS_SECTION)
    row_order = jnp.arange(ROWS_SECTION, dtype=jnp.int32)
    matching = target[:, :, None] == target[:, None, :]
    position = lax.optimization_barrier(jnp.sum((matching & (row_order[:, None] > row_order[None, :])[None]).astype(jnp.int32), axis=2))
    section_ids = jnp.arange(N_SECTION, dtype=jnp.int32)[:, None]
    slot_index = ((section_ids * N_DP + target) * TOK + position).reshape(VROWS)
    start_rows = text.at[slot_index].set(rows)
    merged_grads = row_grads[slot_index]
    sequences = start_rows.reshape(N_SECTION * N_DP, TOK, D)

    def run_layers(block_item):
        hidden, lengths = block_item
        for layer_index in range(N_SECTION):
            hidden = language_layer(hidden, lang_gain[layer_index], w_qkv[layer_index], wo_t[layer_index], lengths)
        return hidden
    final_hidden = lax.map(run_layers, (sequences, seq_lengths)).reshape(LTOK, D)
    return (final_hidden, merged_grads)
```

```python
import functools
import math

import jax
import jax.numpy as jnp
from jax import lax
from jax.experimental import pallas as pl
from jax.experimental.pallas import tpu as pltpu
from jax.sharding import PartitionSpec as P

QH = 32
KVH = 4
HD = 128
VD = 1280
VH = 16
VHD = 80
MERGE = 4
SIDE = 4
TOK = 128
FB = 512
HEADS = QH // KVH
QW = HEADS * HD
PW = QW + 2 * HD
PT = PW + HD
D = 8192
EPSILON = 1e-06
VMEM_LIMIT = 56 * 1024 * 1024
BF = jnp.bfloat16
F32 = jnp.float32


def layer_norm(values, norm_gain):
    values = values.astype(F32)
    centre = jnp.mean(values, axis=-1, keepdims=True)
    centred = values - centre
    variance = jnp.mean(centred * centred, axis=-1, keepdims=True)
    return centred * lax.rsqrt(variance + EPSILON) * norm_gain


def segment_of(lengths, amount):
    boundary = jnp.cumsum(lengths.astype(jnp.int32))
    positions = jnp.arange(amount, dtype=jnp.int32)
    return jnp.sum((positions[:, None] >= boundary[None, :]).astype(jnp.int32), axis=1)


def vision_rows(patches, units, v_gain, v_qkv, v_out, merge_gain):
    amount = patches.shape[0]
    merged_count = amount // MERGE
    unit_image = segment_of(units, merged_count)
    image_ids = jnp.broadcast_to(unit_image[:, None], (merged_count, MERGE)).reshape(amount)
    v_normed = layer_norm(patches, v_gain).astype(BF)
    projected = jnp.dot(v_normed, v_qkv, preferred_element_type=F32).astype(BF)
    projected = projected.reshape(amount, 3, VH, VHD)
    scores = jnp.einsum(
        "qhd,khd->hqk", projected[:, 0], projected[:, 1], preferred_element_type=F32
    ) / math.sqrt(VHD)
    allowed = image_ids[:, None] == image_ids[None, :]
    scores = jnp.where(allowed[None], scores, -1e30)
    weights = jax.nn.softmax(scores, axis=-1).astype(BF)
    attended = (
        jnp.einsum("hqk,khd->qhd", weights, projected[:, 2], preferred_element_type=F32)
        .astype(BF)
        .reshape(amount, VD)
    )
    update = jnp.dot(attended, v_out, preferred_element_type=F32)
    v_hidden = (patches.astype(F32) + update).astype(BF)
    merged = layer_norm(v_hidden, merge_gain).astype(BF)
    return merged.reshape(merged_count, MERGE * VD)


def push(src, dst, send_sem, recv_sem, where):
    copy = pltpu.make_async_remote_copy(
        src_ref=src,
        dst_ref=dst,
        send_sem=send_sem,
        recv_sem=recv_sem,
        device_id=where,
        device_id_type=pl.DeviceIdType.MESH,
    )
    copy.start()
    return copy


def greet(partners):
    barrier = pltpu.get_barrier_semaphore()
    for where in partners:
        pl.semaphore_signal(
            barrier, inc=1, device_id=where, device_id_type=pl.DeviceIdType.MESH
        )
    pl.semaphore_wait(barrier, len(partners))


def along(index, step):
    return lax.rem(index + step, SIDE)


def behind(index, step):
    return lax.rem(index + SIDE - step, SIDE)


def merge_kernel(
    pieces, wm, text, lslot, gslot, grads,
    h0, mg,
    wmv, xbuf, part, psend, rbuf, ybuf, tbuf, pick, gbuf, gsend, grec, gz, mz,
    w_sem, s_pl, r_pl, s_x, r_x, s_y, r_y, s_t, r_t, s_g, r_g, s_gy, r_gy, s_gz, r_gz,
):
    x = lax.axis_index("x")
    y = lax.axis_index("y")
    z = lax.axis_index("mp")
    plane = [(dx, dz) for dx in range(SIDE) for dz in range(SIDE) if dx or dz]
    steps = (1, 3, 2)

    loads = []
    for dx in range(SIDE):
        xt = along(x, dx)
        load = pltpu.make_async_copy(
            wm.at[:, pl.ds(pl.multiple_of(xt * FB, FB), FB)], wmv.at[dx], w_sem.at[dx]
        )
        load.start()
        loads.append(load)

    greet(
        [{"x": along(x, dx), "mp": along(z, dz)} for dx, dz in plane]
        + [{"y": along(y, dy)} for dy in steps]
    )
    plane_copies = []
    for dx, dz in plane:
        xt = along(x, dx)
        plane_copies.append(
            push(
                pieces.at[xt], xbuf.at[x * SIDE + z],
                s_pl.at[dx * SIDE + dz], r_pl.at[dx * SIDE + dz],
                {"x": xt, "mp": along(z, dz)},
            )
        )
    xbuf[x * SIDE + z] = pieces[x]
    text_copies, grad_copies = [], []
    for dx in steps:
        xt = along(x, dx)
        text_copies.append(
            push(
                text.at[:, pl.ds(pl.multiple_of(xt * FB, FB), FB)], tbuf.at[x],
                s_t.at[dx], r_t.at[dx], {"x": xt},
            )
        )
    tbuf[x] = text[:, pl.ds(pl.multiple_of(x * FB, FB), FB)]
    for dx in steps:
        grad_copies.append(
            push(grads, gbuf.at[x], s_g.at[dx], r_g.at[dx], {"x": along(x, dx)})
        )
    gbuf[x] = grads[...]

    slots = lslot[...]
    for block in range(SIDE):
        wanted = lax.broadcasted_iota(jnp.int32, (TOK, slots.shape[1]), 0) + block * TOK
        pick[pl.ds(block * TOK, TOK), :] = jnp.where(wanted == slots, 1.0, 0.0).astype(BF)

    for load in loads:
        load.wait()
    for copy in plane_copies:
        copy.wait()

    rows = xbuf[...].reshape(SIDE * SIDE * 16, VD)
    x_copies = []
    for dx in steps:
        psend[dx] = jnp.dot(rows, wmv[dx], preferred_element_type=F32).astype(BF)
        x_copies.append(
            push(psend.at[dx], rbuf.at[dx], s_x.at[dx], r_x.at[dx], {"x": along(x, dx)})
        )
    part[...] = jnp.dot(rows, wmv[0], preferred_element_type=F32)
    for copy in x_copies:
        copy.wait()
    total = part[...]
    for dx in steps:
        total = total + rbuf[dx].astype(F32)
    ybuf[y] = total.astype(BF)
    y_copies = [
        push(ybuf.at[y], ybuf.at[y], s_y.at[dy], r_y.at[dy], {"y": along(y, dy)})
        for dy in steps
    ]

    for copy in grad_copies:
        copy.wait()
    given = gbuf[...].reshape(SIDE * TOK, grads.shape[1])
    gy_copies = []
    for dy in (1, 3, 2, 0):
        yt = along(y, dy)
        mine = gslot[pl.ds(pl.multiple_of(yt * 64, 64), 64), :]
        lanes = lax.broadcasted_iota(jnp.int32, (64, SIDE * TOK), 1)
        chosen = jnp.where(lanes == mine, 1.0, 0.0).astype(BF)
        gsend[dy] = jnp.dot(chosen, given, preferred_element_type=F32).astype(BF)
        if dy:
            gy_copies.append(
                push(gsend.at[dy], grec.at[dy], s_gy.at[dy], r_gy.at[dy], {"y": yt})
            )

    for copy in text_copies:
        copy.wait()
    for copy in y_copies:
        copy.wait()
    chosen = pick[...]
    picked = jnp.dot(
        chosen, ybuf[...].reshape(SIDE * 256, FB), preferred_element_type=F32
    ).astype(BF)
    present = jnp.dot(chosen, jnp.ones((SIDE * 256, 128), BF), preferred_element_type=F32)
    texts = tbuf[...].reshape(SIDE * TOK, FB)
    for tile in range(FB // 128):
        cols = slice(tile * 128, (tile + 1) * 128)
        h0[:, cols] = jnp.where(present > 0.5, picked[:, cols], texts[:, cols])

    for copy in gy_copies:
        copy.wait()
    found = gsend[0].astype(F32)
    for dy in steps:
        found = found + grec[dy].astype(F32)
    gz[...] = found.astype(BF).reshape(SIDE, 16, grads.shape[1])
    gz_copies = []
    for dz in steps:
        zt = along(z, dz)
        gz_copies.append(push(gz.at[zt], mz.at[z], s_gz.at[dz], r_gz.at[dz], {"mp": zt}))
    mz[z] = gz[z]
    for copy in gz_copies:
        copy.wait()
    width = grads.shape[1]
    for block in range(SIDE):
        mg[:, block * width : (block + 1) * width] = mz[block]


def merge_call(pieces, wm, text, lslot, gslot, grads):
    vmem = pl.BlockSpec(memory_space=pltpu.VMEM)
    dma = pltpu.SemaphoreType.DMA
    width = grads.shape[1]
    return pl.pallas_call(
        merge_kernel,
        out_shape=(
            jax.ShapeDtypeStruct((SIDE * TOK, FB), BF),
            jax.ShapeDtypeStruct((16, SIDE * width), BF),
        ),
        in_specs=[vmem, pl.BlockSpec(memory_space=pl.ANY), vmem, vmem, vmem, vmem],
        out_specs=(vmem, vmem),
        scratch_shapes=[
            pltpu.VMEM((SIDE, VD, FB), BF),
            pltpu.VMEM((SIDE * SIDE, 16, VD), BF),
            pltpu.VMEM((256, FB), F32),
            pltpu.VMEM((SIDE, 256, FB), BF),
            pltpu.VMEM((SIDE, 256, FB), BF),
            pltpu.VMEM((SIDE, 256, FB), BF),
            pltpu.VMEM((SIDE, TOK, FB), BF),
            pltpu.VMEM((SIDE * TOK, 1024), BF),
            pltpu.VMEM((SIDE, TOK, width), BF),
            pltpu.VMEM((SIDE, 64, width), BF),
            pltpu.VMEM((SIDE, 64, width), BF),
            pltpu.VMEM((SIDE, 16, width), BF),
            pltpu.VMEM((SIDE, 16, width), BF),
            dma((SIDE,)),
            dma((16,)), dma((16,)),
            dma((SIDE,)), dma((SIDE,)),
            dma((SIDE,)), dma((SIDE,)),
            dma((SIDE,)), dma((SIDE,)),
            dma((SIDE,)), dma((SIDE,)),
            dma((SIDE,)), dma((SIDE,)),
            dma((SIDE,)), dma((SIDE,)),
        ],
        compiler_params=pltpu.CompilerParams(
            collective_id=1, has_side_effects=True, vmem_limit_bytes=VMEM_LIMIT
        ),
        name="merge",
    )(pieces, wm, text, lslot, gslot, grads)


def layer_kernel(
    layer, last,
    h, wqa, wqb, woa, wob, mask,
    out,
    wq, wo, zbuf, acc, squares, psend, rbuf, abuf, osend, orec, obuf,
    w_sem, s_z, r_z, s_x, r_x, s_a, r_a, s_o, r_o, s_e, r_e,
):
    x = lax.axis_index("x")
    z = lax.axis_index("mp")
    section = lax.axis_index("section")
    steps = (1, 3, 2)

    @pl.when(section == layer)
    def _():
        pltpu.make_async_copy(wqa, wq, w_sem.at[0]).start()
        pltpu.make_async_copy(woa, wo, w_sem.at[1]).start()

    @pl.when(section != layer)
    def _():
        pltpu.make_async_copy(wqb, wq, w_sem.at[0]).start()
        pltpu.make_async_copy(wob, wo, w_sem.at[1]).start()

    zbuf[z] = h[...]
    greet([{"x": along(x, d)} for d in steps] + [{"mp": along(z, d)} for d in steps])
    z_copies = {
        dz: push(zbuf.at[z], zbuf.at[z], s_z.at[dz], r_z.at[dz], {"mp": along(z, dz)})
        for dz in steps
    }
    pltpu.make_async_copy(wqa, wq, w_sem.at[0]).wait()
    for dz in (0, 1, 3, 2):
        zs = behind(z, dz)
        if dz:
            z_copies[dz].wait_recv()
        block = zbuf[zs]
        wide = block.astype(F32)
        wide = wide * wide
        squared = jnp.sum(wide, axis=1, keepdims=True)
        if dz:
            squares[...] += jnp.broadcast_to(squared, squares.shape)
        else:
            squares[...] = jnp.broadcast_to(squared, squares.shape)

        @pl.loop(0, PW // 256)
        def _(tile):
            cols = pl.ds(pl.multiple_of(tile * 256, 256), 256)
            product = jnp.dot(zbuf[zs], wq[zs, :, cols], preferred_element_type=F32)
            if dz:
                acc[:, cols] += product
            else:
                acc[:, cols] = product

    lane = lax.broadcasted_iota(jnp.int32, (TOK, HD), 1)
    x_copies = []
    for dx in steps:
        xt = along(x, dx)
        span = pl.ds(pl.multiple_of(xt * TOK, TOK), TOK)
        psend[dx, :, :PW] = acc[span, :].astype(BF)
        sq = squares[span, :]
        high = sq.astype(BF)
        low = (sq - high.astype(F32)).astype(BF)
        psend[dx, :, PW:] = jnp.where(lane < 64, high, low)
        x_copies.append(
            push(psend.at[dx], rbuf.at[dx], s_x.at[dx], r_x.at[dx], {"x": xt})
        )
    own = pl.ds(pl.multiple_of(x * TOK, TOK), TOK)
    total = acc[own, :]
    sq = squares[own, :][:, :1]
    for copy in x_copies:
        copy.wait()
    for dx in steps:
        total = total + rbuf[dx, :, :PW].astype(F32)
        tail = rbuf[dx, :, PW:].astype(F32)
        sq = sq + tail[:, :1] + tail[:, 64:65]
    scale = lax.rsqrt(sq / D + EPSILON)
    projected = (total * scale).astype(BF)
    keys = projected[:, QW : QW + HD]
    values = projected[:, QW + HD :]
    allowed = mask[...] > 0.5
    for head in range(HEADS):
        cols = slice(head * HD, (head + 1) * HD)
        scores = lax.dot_general(
            projected[:, cols], keys, (((1,), (1,)), ((), ())), preferred_element_type=F32
        ) * (1.0 / math.sqrt(HD))
        scores = jnp.where(allowed, scores, -1e30)
        top = jnp.max(scores, axis=1, keepdims=True)
        weights = jnp.exp(scores - top)
        weights = (weights / jnp.sum(weights, axis=1, keepdims=True)).astype(BF)
        abuf[x, :, cols] = jnp.dot(weights, values, preferred_element_type=F32).astype(BF)
    a_copies = [
        push(abuf.at[x], abuf.at[x], s_a.at[dx], r_a.at[dx], {"x": along(x, dx)})
        for dx in steps
    ]
    pltpu.make_async_copy(woa, wo, w_sem.at[1]).wait()
    for copy in a_copies:
        copy.wait()
    o_copies = []
    for dz in (1, 3, 2, 0):
        zt = along(z, dz)

        @pl.loop(0, FB // 256)
        def _(tile):
            cols = pl.ds(pl.multiple_of(tile * 256, 256), 256)
            osend[dz, :, cols] = lax.dot_general(
                abuf[...].reshape(SIDE * TOK, QW), wo[zt, cols, :],
                (((1,), (1,)), ((), ())), preferred_element_type=F32,
            ).astype(BF)

        if dz:
            o_copies.append(
                push(osend.at[dz], orec.at[dz], s_o.at[dz], r_o.at[dz], {"mp": zt})
            )
    for copy in z_copies.values():
        copy.wait_send()
    update = osend[0].astype(F32)
    for copy in o_copies:
        copy.wait()
    for dz in steps:
        update = update + orec[dz].astype(F32)
    fresh = (h[...].astype(F32) + update).astype(BF)
    if not last:
        out[...] = fresh
        return
    zbuf[0] = fresh
    e_copies = []
    for dx in steps:
        xt = along(x, dx)
        e_copies.append(
            push(
                zbuf.at[0, pl.ds(pl.multiple_of(xt * TOK, TOK), TOK), :], obuf.at[x],
                s_e.at[dx], r_e.at[dx], {"x": xt},
            )
        )
    obuf[x] = zbuf[0, own, :]
    for copy in e_copies:
        copy.wait()
    for block in range(SIDE):
        out[:, block * FB : (block + 1) * FB] = obuf[block]


def layer_call(layer, last, h, wqa, wqb, woa, wob, mask):
    vmem = pl.BlockSpec(memory_space=pltpu.VMEM)
    hbm = pl.BlockSpec(memory_space=pl.ANY)
    dma = pltpu.SemaphoreType.DMA
    rows = SIDE * TOK
    return pl.pallas_call(
        functools.partial(layer_kernel, layer, last),
        out_shape=jax.ShapeDtypeStruct((TOK, SIDE * FB) if last else (rows, FB), BF),
        in_specs=[vmem, hbm, hbm, hbm, hbm, vmem],
        out_specs=vmem,
        scratch_shapes=[
            pltpu.VMEM((SIDE, FB, PW), BF),
            pltpu.VMEM((SIDE, FB, QW), BF),
            pltpu.VMEM((SIDE, rows, FB), BF),
            pltpu.VMEM((rows, PW), F32),
            pltpu.VMEM((rows, HD), F32),
            pltpu.VMEM((SIDE, TOK, PT), BF),
            pltpu.VMEM((SIDE, TOK, PT), BF),
            pltpu.VMEM((SIDE, TOK, QW), BF),
            pltpu.VMEM((SIDE, rows, FB), BF),
            pltpu.VMEM((SIDE, rows, FB), BF),
            pltpu.VMEM((SIDE, TOK, FB), BF),
            dma((2,)),
            dma((SIDE,)), dma((SIDE,)),
            dma((SIDE,)), dma((SIDE,)),
            dma((SIDE,)), dma((SIDE,)),
            dma((SIDE,)), dma((SIDE,)),
            dma((SIDE,)), dma((SIDE,)),
        ],
        compiler_params=pltpu.CompilerParams(
            collective_id=2 + layer, has_side_effects=True, vmem_limit_bytes=VMEM_LIMIT
        ),
        name="layer%d" % layer,
    )(h, wqa, wqb, woa, wob, mask)


def shards(
    patches,
    image_units,
    v_gain,
    v_qkv,
    v_out,
    merge_gain,
    w_merge,
    routes,
    text,
    seq_lengths,
    lang_gain,
    w_qkv,
    wo_t,
    row_grads,
):
    x = lax.axis_index("x")
    y = lax.axis_index("y")
    swap = [(0, 1), (1, 0)]

    wm = lax.all_gather(w_merge, "y", axis=0, tiled=True)
    gain = lax.dynamic_slice_in_dim(lang_gain[0], (y * SIDE + x) * FB, FB, 0)
    scaled = (w_qkv[0].astype(F32) * gain[:, None]).astype(BF)
    wq_here = lax.all_gather(scaled, "y", axis=0, tiled=False)
    wo_here = lax.all_gather(wo_t[0], "y", axis=0, tiled=False)
    wq_there = lax.ppermute(wq_here, "section", swap)
    wo_there = lax.ppermute(wo_here, "section", swap)

    target = lax.all_gather(routes, ("y", "x", "mp"), axis=0, tiled=True)[:, 0]
    count = target.shape[0]
    order = jnp.arange(count, dtype=jnp.int32)
    position = jnp.sum(
        ((target[:, None] == target[None, :]) & (order[:, None] > order[None, :])).astype(jnp.int32),
        axis=1,
    )
    local = (target - y * SIDE) * TOK + position
    gslot = lax.dynamic_index_in_dim(local.reshape(SIDE, SIDE, 64), x, 1, keepdims=False)

    merged = vision_rows(patches, image_units[0], v_gain, v_qkv, v_out, merge_gain)
    pieces = merged.reshape(16, MERGE, SIDE, 320).transpose(2, 0, 1, 3).reshape(SIDE, 16, VD)

    hidden, merged_grads = merge_call(
        pieces, wm, text, local[None, :], gslot.reshape(256, 1), row_grads
    )
    seq = segment_of(seq_lengths[0], TOK)
    at = jnp.arange(TOK, dtype=jnp.int32)
    mask = ((seq[:, None] == seq[None, :]) & (at[:, None] >= at[None, :])).astype(F32)
    hidden = layer_call(0, False, hidden, wq_here, wq_there, wo_here, wo_there, mask)
    final_hidden = layer_call(1, True, hidden, wq_here, wq_there, wo_here, wo_there, mask)
    return (final_hidden, merged_grads)


def solution(mesh):
    grid = jax.sharding.Mesh(
        mesh.devices.reshape(2, SIDE, SIDE, SIDE), ("section", "y", "x", "mp")
    )
    every = ("section", "y", "x", "mp")
    home = P(("section", "y", "x"), "mp")
    in_specs = (
        P(every, None),
        P(every, None),
        P(),
        P(),
        P(),
        P(),
        P(("y", "x"), "mp"),
        P(every, None),
        home,
        P(("section", "y", "x"), None),
        P("section", None),
        P("section", ("y", "x"), "mp"),
        P("section", ("y", "x"), "mp"),
        home,
    )
    out_specs = (home, P(every, None))
    return jax.shard_map(shards, mesh=grid, in_specs=in_specs, out_specs=out_specs, check_vma=False)
```

```python
import functools
import math

import jax
import jax.numpy as jnp
from jax import lax
from jax.experimental import pallas as pl
from jax.experimental.pallas import tpu as pltpu
from jax.sharding import PartitionSpec as P

QH = 32
KVH = 4
HD = 128
VD = 1280
VH = 16
VHD = 80
MERGE = 4
SIDE = 4
TOK = 128
FB = 512
HALF = TOK // 2
STEPS = (1, 3, 2)
HEADS = QH // KVH
QW = HEADS * HD
PW = QW + 2 * HD
PT = PW + HD
D = 8192
EPSILON = 1e-06
VMEM_LIMIT = 60 * 1024 * 1024
BF = jnp.bfloat16
F32 = jnp.float32


def layer_norm(values, norm_gain):
    values = values.astype(F32)
    centre = jnp.mean(values, axis=-1, keepdims=True)
    centred = values - centre
    variance = jnp.mean(centred * centred, axis=-1, keepdims=True)
    return centred * lax.rsqrt(variance + EPSILON) * norm_gain


def segment_of(lengths, amount):
    boundary = jnp.cumsum(lengths.astype(jnp.int32))
    positions = jnp.arange(amount, dtype=jnp.int32)
    return jnp.sum((positions[:, None] >= boundary[None, :]).astype(jnp.int32), axis=1)


def vision_rows(patches, units, v_gain, v_qkv, v_out, merge_gain):
    amount = patches.shape[0]
    merged_count = amount // MERGE
    unit_image = segment_of(units, merged_count)
    image_ids = jnp.broadcast_to(unit_image[:, None], (merged_count, MERGE)).reshape(amount)
    v_normed = layer_norm(patches, v_gain).astype(BF)
    projected = jnp.dot(v_normed, v_qkv, preferred_element_type=F32).astype(BF)
    projected = projected.reshape(amount, 3, VH, VHD)
    scores = jnp.einsum(
        "qhd,khd->hqk", projected[:, 0], projected[:, 1], preferred_element_type=F32
    ) / math.sqrt(VHD)
    allowed = image_ids[:, None] == image_ids[None, :]
    scores = jnp.where(allowed[None], scores, -1e30)
    weights = jax.nn.softmax(scores, axis=-1).astype(BF)
    attended = (
        jnp.einsum("hqk,khd->qhd", weights, projected[:, 2], preferred_element_type=F32)
        .astype(BF)
        .reshape(amount, VD)
    )
    update = jnp.dot(attended, v_out, preferred_element_type=F32)
    v_hidden = (patches.astype(F32) + update).astype(BF)
    merged = layer_norm(v_hidden, merge_gain).astype(BF)
    return merged.reshape(merged_count, MERGE * VD)


def push(src, dst, send_sem, recv_sem, where):
    copy = pltpu.make_async_remote_copy(
        src_ref=src,
        dst_ref=dst,
        send_sem=send_sem,
        recv_sem=recv_sem,
        device_id=where,
        device_id_type=pl.DeviceIdType.MESH,
    )
    copy.start()
    return copy


def greet(partners):
    barrier = pltpu.get_barrier_semaphore()
    for where in partners:
        pl.semaphore_signal(
            barrier, inc=1, device_id=where, device_id_type=pl.DeviceIdType.MESH
        )
    pl.semaphore_wait(barrier, len(partners))


def along(index, step):
    return lax.rem(index + step, SIDE)


def behind(index, step):
    return lax.rem(index + SIDE - step, SIDE)


def merge_kernel(
    pieces, wm, text, lslot,
    h0,
    wmv, xbuf, part, psend, rbuf, ybuf, tbuf, pick,
    w_sem, s_w, r_w, s_pl, r_pl, s_x, r_x, s_y, r_y, s_t, r_t,
):
    section = lax.axis_index("section")
    x = lax.axis_index("x")
    y = lax.axis_index("y")
    z = lax.axis_index("mp")
    plane = [(dx, dz) for dx in range(SIDE) for dz in range(SIDE) if dx or dz]
    half = wm.shape[1]

    for block in range(SIDE):
        pltpu.make_async_copy(wm.at[block], wmv.at[block, section], w_sem.at[block]).start()
    greet(
        [{"x": along(x, dx), "mp": along(z, dz)} for dx, dz in plane]
        + [{"y": along(y, dy)} for dy in STEPS]
        + [{"section": 1 - section}]
    )
    plane_copies = []
    for dx, dz in plane:
        xt = along(x, dx)
        plane_copies.append(
            push(
                pieces.at[xt], xbuf.at[x * SIDE + z],
                s_pl.at[dx * SIDE + dz], r_pl.at[dx * SIDE + dz],
                {"x": xt, "mp": along(z, dz)},
            )
        )
    xbuf[x * SIDE + z] = pieces[x]
    twin_copies = [
        push(
            wm.at[block], wmv.at[block, section], s_w.at[block], r_w.at[block],
            {"section": 1 - section},
        )
        for block in range(SIDE)
    ]
    text_copies = []
    for dx in STEPS:
        xt = along(x, dx)
        text_copies.append(
            push(
                text.at[:, pl.ds(pl.multiple_of(xt * FB, FB), FB)], tbuf.at[x],
                s_t.at[dx], r_t.at[dx], {"x": xt},
            )
        )
    tbuf[x] = text[:, pl.ds(pl.multiple_of(x * FB, FB), FB)]

    slots = lslot[...]
    for block in range(SIDE):
        wanted = lax.broadcasted_iota(jnp.int32, (TOK, slots.shape[1]), 0) + block * TOK
        pick[pl.ds(block * TOK, TOK), :] = jnp.where(wanted == slots, 1.0, 0.0).astype(BF)

    for block in range(SIDE):
        pltpu.make_async_copy(wm.at[block], wmv.at[block, section], w_sem.at[block]).wait()
    for copy in twin_copies:
        copy.wait()
    for copy in plane_copies:
        copy.wait()

    def product(dx):
        cols = pl.ds(pl.multiple_of(along(x, dx) * FB, FB), FB)
        rows = xbuf[...].reshape(SIDE * SIDE * 16, VD)
        weights = wmv[:, :, :, cols].reshape(SIDE * 2 * half, FB)
        return jnp.dot(rows, weights, preferred_element_type=F32)

    x_copies = []
    for dx in STEPS:
        psend[dx] = product(dx).astype(BF)
        x_copies.append(
            push(psend.at[dx], rbuf.at[dx], s_x.at[dx], r_x.at[dx], {"x": along(x, dx)})
        )
    part[...] = product(0)
    for copy in x_copies:
        copy.wait()
    total = part[...]
    for dx in STEPS:
        total = total + rbuf[dx].astype(F32)
    ybuf[y] = total.astype(BF)
    y_copies = [
        push(ybuf.at[y], ybuf.at[y], s_y.at[dy], r_y.at[dy], {"y": along(y, dy)})
        for dy in STEPS
    ]
    chosen = pick[...]
    present = jnp.dot(chosen, jnp.ones((SIDE * 256, 128), BF), preferred_element_type=F32)
    for copy in text_copies:
        copy.wait()
    for copy in y_copies:
        copy.wait()
    picked = jnp.dot(
        chosen, ybuf[...].reshape(SIDE * 256, FB), preferred_element_type=F32
    ).astype(BF)
    for group in range(SIDE):
        for part_of in range(2):
            rows = slice(group * TOK + part_of * HALF, group * TOK + (part_of + 1) * HALF)
            to = slice(group * HALF, (group + 1) * HALF)
            inside = slice(part_of * HALF, (part_of + 1) * HALF)
            for tile in range(FB // 128):
                cols = slice(tile * 128, (tile + 1) * 128)
                h0[part_of, to, cols] = jnp.where(
                    present[rows, :] > 0.5, picked[rows, cols], tbuf[group, inside, cols]
                )


def merge_call(pieces, wm, text, lslot):
    vmem = pl.BlockSpec(memory_space=pltpu.VMEM)
    dma = pltpu.SemaphoreType.DMA
    half = wm.shape[1]
    return pl.pallas_call(
        merge_kernel,
        out_shape=jax.ShapeDtypeStruct((2, SIDE * HALF, FB), BF),
        in_specs=[vmem, pl.BlockSpec(memory_space=pl.ANY), vmem, vmem],
        out_specs=vmem,
        scratch_shapes=[
            pltpu.VMEM((SIDE, 2, half, SIDE * FB), BF),
            pltpu.VMEM((SIDE * SIDE, 16, VD), BF),
            pltpu.VMEM((256, FB), F32),
            pltpu.VMEM((SIDE, 256, FB), BF),
            pltpu.VMEM((SIDE, 256, FB), BF),
            pltpu.VMEM((SIDE, 256, FB), BF),
            pltpu.VMEM((SIDE, TOK, FB), BF),
            pltpu.VMEM((SIDE * TOK, 1024), BF),
            dma((SIDE,)),
            dma((SIDE,)), dma((SIDE,)),
            dma((16,)), dma((16,)),
            dma((SIDE,)), dma((SIDE,)),
            dma((SIDE,)), dma((SIDE,)),
            dma((SIDE,)), dma((SIDE,)),
        ],
        compiler_params=pltpu.CompilerParams(
            collective_id=1, has_side_effects=True, vmem_limit_bytes=VMEM_LIMIT
        ),
        name="merge",
    )(pieces, wm, text, lslot)


def layers_kernel(
    h, w_first, w_mine, mask, gslot, grads,
    out, mg,
    w, zbuf, acc, squares, kv, psend, rbuf, abuf, osend, orec, obuf,
    gbuf, gsend, grec, gz, mz,
    w_sem, s_w0, r_w0, s_w1, r_w1, s_w2, r_w2,
    s_z, r_z, s_x, r_x, s_a, r_a, s_o, r_o, s_e, r_e,
    s_g, r_g, s_gx, r_gx, s_gz, r_gz,
):
    section = lax.axis_index("section")
    x = lax.axis_index("x")
    y = lax.axis_index("y")
    z = lax.axis_index("mp")
    twin = {"section": 1 - section}
    rows = SIDE * HALF
    half = FB // 2
    width = grads.shape[1]
    mine = pl.ds(pl.multiple_of(section * half, half), half)

    own_load = pltpu.make_async_copy(w_first, w.at[0, :, mine, :], w_sem.at[0])
    own_load.start()
    own_shard = pltpu.make_async_copy(w_mine, w.at[1, y], w_sem.at[1])
    for part in range(2):
        zbuf[0, part, z] = h[part]
    greet(
        [{"x": along(x, d)} for d in STEPS]
        + [{"mp": along(z, d)} for d in STEPS]
        + [{"y": along(y, d)} for d in STEPS]
        + [twin]
    )

    z_copies, x_copies, a_copies, o_copies, e_copies = {}, {}, {}, {}, []

    def spread(layer, part):
        z_copies[layer, part] = {
            dz: push(
                zbuf.at[layer, part, z], zbuf.at[layer, part, z],
                s_z.at[layer, part, dz], r_z.at[layer, part, dz], {"mp": along(z, dz)},
            )
            for dz in STEPS
        }

    def project(layer, part):
        for dz in (0, 1, 3, 2):
            zs = behind(z, dz)
            if dz:
                z_copies[layer, part][dz].wait()
            wide = zbuf[layer, part, zs].astype(F32)
            squared = jnp.sum(wide * wide, axis=1, keepdims=True)
            if dz:
                squares[part] += jnp.broadcast_to(squared, (rows, HD))
            else:
                squares[part] = jnp.broadcast_to(squared, (rows, HD))

            @pl.loop(0, PW // 256)
            def _(tile):
                cols = pl.ds(pl.multiple_of(tile * 256, 256), 256)
                product = jnp.dot(
                    zbuf[layer, part, zs], w[layer, zs, :, cols], preferred_element_type=F32
                )
                if dz:
                    acc[part, :, cols] += product
                else:
                    acc[part, :, cols] = product

        lane = lax.broadcasted_iota(jnp.int32, (HALF, HD), 1)
        copies = []
        for dx in STEPS:
            xt = along(x, dx)
            span = pl.ds(pl.multiple_of(xt * HALF, HALF), HALF)
            psend[layer, part, dx, :, :PW] = acc[part, span, :].astype(BF)
            sq = squares[part, span, :]
            high = sq.astype(BF)
            low = (sq - high.astype(F32)).astype(BF)
            psend[layer, part, dx, :, PW:] = jnp.where(lane < 64, high, low)
            copies.append(
                push(
                    psend.at[layer, part, dx], rbuf.at[layer, part, dx],
                    s_x.at[layer, part, dx], r_x.at[layer, part, dx], {"x": xt},
                )
            )
        x_copies[layer, part] = copies

    def attend(layer, part):
        own = pl.ds(pl.multiple_of(x * HALF, HALF), HALF)
        total = acc[part, own, :]
        sq = squares[part, own, :][:, :1]
        for copy in x_copies[layer, part]:
            copy.wait()
        for dx in STEPS:
            total = total + rbuf[layer, part, dx, :, :PW].astype(F32)
            tail = rbuf[layer, part, dx, :, PW:].astype(F32)
            sq = sq + tail[:, :1] + tail[:, 64:65]
        projected = (total * lax.rsqrt(sq / D + EPSILON)).astype(BF)
        kv[part * HALF : (part + 1) * HALF, :] = projected[:, QW:]
        seen = (part + 1) * HALF
        keys = kv[:seen, :HD]
        values = kv[:seen, HD:]
        queries = jnp.concatenate(
            [projected[:, head * HD : (head + 1) * HD] for head in range(HEADS)], axis=0
        )
        allowed = mask[part * HALF : (part + 1) * HALF, :seen]
        allowed = jnp.concatenate([allowed] * HEADS, axis=0) > 0.5
        scores = lax.dot_general(
            queries, keys, (((1,), (1,)), ((), ())), preferred_element_type=F32
        ) * (1.0 / math.sqrt(HD))
        scores = jnp.where(allowed, scores, -1e30)
        top = jnp.max(scores, axis=1, keepdims=True)
        weights = jnp.exp(scores - top)
        weights = (weights / jnp.sum(weights, axis=1, keepdims=True)).astype(BF)
        mixed = jnp.dot(weights, values, preferred_element_type=F32).astype(BF)
        for head in range(HEADS):
            abuf[layer, part, x, :, head * HD : (head + 1) * HD] = mixed[
                head * HALF : (head + 1) * HALF, :
            ]
        a_copies[layer, part] = [
            push(
                abuf.at[layer, part, x], abuf.at[layer, part, x],
                s_a.at[layer, part, dx], r_a.at[layer, part, dx], {"x": along(x, dx)},
            )
            for dx in STEPS
        ]

    def output(layer, part):
        for copy in a_copies[layer, part]:
            copy.wait()
        copies = []
        for dz in (1, 3, 2, 0):
            zt = along(z, dz)

            @pl.loop(0, FB // 256)
            def _(tile):
                cols = pl.ds(pl.multiple_of(tile * 256, 256), 256)
                osend[layer, part, dz, :, cols] = lax.dot_general(
                    abuf[layer, part].reshape(rows, QW), w[layer, zt, cols, PW:],
                    (((1,), (1,)), ((), ())), preferred_element_type=F32,
                ).astype(BF)

            if dz:
                copies.append(
                    push(
                        osend.at[layer, part, dz], orec.at[layer, part, dz],
                        s_o.at[layer, part, dz], r_o.at[layer, part, dz], {"mp": zt},
                    )
                )
        o_copies[layer, part] = copies

    def finish(layer, part):
        update = osend[layer, part, 0].astype(F32)
        for copy in o_copies[layer, part]:
            copy.wait()
        for dz in STEPS:
            update = update + orec[layer, part, dz].astype(F32)
        fresh = (zbuf[layer, part, z].astype(F32) + update).astype(BF)
        if layer == 0:
            zbuf[1, part, z] = fresh
            return
        osend[layer, part, 0] = fresh
        for dx in STEPS:
            xt = along(x, dx)
            e_copies.append(
                push(
                    osend.at[layer, part, 0, pl.ds(pl.multiple_of(xt * HALF, HALF), HALF), :],
                    obuf.at[x, part],
                    s_e.at[part, dx], r_e.at[part, dx], {"x": xt},
                )
            )
        obuf[x, part] = osend[
            layer, part, 0, pl.ds(pl.multiple_of(x * HALF, HALF), HALF), :
        ]

    spread(0, 0)
    spread(0, 1)
    twin_copy = push(w_first, w.at[0, :, mine, :], s_w0.at[0], r_w0.at[0], twin)

    def shard_copy(dy):
        return pltpu.make_async_remote_copy(
            src_ref=w_mine, dst_ref=w.at[1, y], send_sem=s_w1.at[dy], recv_sem=r_w1.at[dy],
            device_id={"y": along(y, dy)}, device_id_type=pl.DeviceIdType.MESH,
        )

    def forward_copy(dy):
        ys = behind(y, dy)
        return pltpu.make_async_remote_copy(
            src_ref=w.at[1, ys], dst_ref=w.at[1, ys], send_sem=s_w2.at[dy],
            recv_sem=r_w2.at[dy], device_id=twin, device_id_type=pl.DeviceIdType.MESH,
        )

    @pl.when(section == 1)
    def _():
        for dy in STEPS:
            shard_copy(dy).start()
        own_shard.start()

    own_load.wait()
    twin_copy.wait()
    project(0, 0)
    project(0, 1)
    attend(0, 0)
    attend(0, 1)
    g_copies = [
        push(grads, gbuf.at[y], s_g.at[dy], r_g.at[dy], {"y": along(y, dy)}) for dy in STEPS
    ]
    gbuf[y] = grads[...]
    output(0, 0)
    output(0, 1)

    @pl.when(section == 1)
    def _():
        own_shard.wait()
        forward_copy(0).start()
        for dy in STEPS:
            shard_copy(dy).wait()
            forward_copy(dy).start()

    finish(0, 0)
    spread(1, 0)
    finish(0, 1)
    spread(1, 1)

    @pl.when(section == 0)
    def _():
        for dy in range(SIDE):
            forward_copy(dy).wait_recv()

    project(1, 0)
    project(1, 1)
    attend(1, 0)
    attend(1, 1)

    for copy in g_copies:
        copy.wait()
    gx_copies = []
    for dx in (1, 3, 2, 0):
        xt = along(x, dx)
        wanted = gslot[pl.ds(pl.multiple_of(xt * 64, 64), 64), :]
        lanes = lax.broadcasted_iota(jnp.int32, (64, SIDE * TOK), 1)
        chosen = jnp.where(lanes == wanted, 1.0, 0.0).astype(BF)
        gsend[dx] = jnp.dot(
            chosen, gbuf[...].reshape(SIDE * TOK, width), preferred_element_type=F32
        ).astype(BF)
        if dx:
            gx_copies.append(
                push(gsend.at[dx], grec.at[dx], s_gx.at[dx], r_gx.at[dx], {"x": xt})
            )

    output(1, 0)
    output(1, 1)
    for copy in gx_copies:
        copy.wait()
    found = gsend[0].astype(F32)
    for dx in STEPS:
        found = found + grec[dx].astype(F32)
    gz[...] = found.astype(BF).reshape(SIDE, 16, width)
    gz_copies = []
    for dz in STEPS:
        zt = along(z, dz)
        gz_copies.append(push(gz.at[zt], mz.at[z], s_gz.at[dz], r_gz.at[dz], {"mp": zt}))
    mz[z] = gz[z]

    finish(1, 0)
    finish(1, 1)
    for copy in gz_copies:
        copy.wait()
    for block in range(SIDE):
        mg[:, block * width : (block + 1) * width] = mz[block]
    for copy in e_copies:
        copy.wait()
    for block in range(SIDE):
        for part in range(2):
            out[part * HALF : (part + 1) * HALF, block * FB : (block + 1) * FB] = obuf[block, part]

    @pl.when(section == 1)
    def _():
        for dy in range(SIDE):
            forward_copy(dy).wait_send()


def layers_call(h, w_first, w_mine, mask, gslot, grads):
    vmem = pl.BlockSpec(memory_space=pltpu.VMEM)
    hbm = pl.BlockSpec(memory_space=pl.ANY)
    dma = pltpu.SemaphoreType.DMA
    rows = SIDE * HALF
    width = grads.shape[1]
    stage = dma((2, 2, SIDE))
    return pl.pallas_call(
        layers_kernel,
        out_shape=(
            jax.ShapeDtypeStruct((TOK, SIDE * FB), BF),
            jax.ShapeDtypeStruct((16, SIDE * width), BF),
        ),
        in_specs=[vmem, hbm, hbm, vmem, vmem, vmem],
        out_specs=(vmem, vmem),
        scratch_shapes=[
            pltpu.VMEM((2, SIDE, FB, PW + QW), BF),
            pltpu.VMEM((2, 2, SIDE, rows, FB), BF),
            pltpu.VMEM((2, rows, PW), F32),
            pltpu.VMEM((2, rows, HD), F32),
            pltpu.VMEM((TOK, 2 * HD), BF),
            pltpu.VMEM((2, 2, SIDE, HALF, PT), BF),
            pltpu.VMEM((2, 2, SIDE, HALF, PT), BF),
            pltpu.VMEM((2, 2, SIDE, HALF, QW), BF),
            pltpu.VMEM((2, 2, SIDE, rows, FB), BF),
            pltpu.VMEM((2, 2, SIDE, rows, FB), BF),
            pltpu.VMEM((SIDE, 2, HALF, FB), BF),
            pltpu.VMEM((SIDE, TOK, width), BF),
            pltpu.VMEM((SIDE, 64, width), BF),
            pltpu.VMEM((SIDE, 64, width), BF),
            pltpu.VMEM((SIDE, 16, width), BF),
            pltpu.VMEM((SIDE, 16, width), BF),
            dma((2,)),
            dma((1,)), dma((1,)),
            dma((SIDE,)), dma((SIDE,)),
            dma((SIDE,)), dma((SIDE,)),
            stage, stage,
            stage, stage,
            stage, stage,
            stage, stage,
            dma((2, SIDE)), dma((2, SIDE)),
            dma((SIDE,)), dma((SIDE,)),
            dma((SIDE,)), dma((SIDE,)),
            dma((SIDE,)), dma((SIDE,)),
        ],
        compiler_params=pltpu.CompilerParams(
            collective_id=2, has_side_effects=True, vmem_limit_bytes=VMEM_LIMIT
        ),
        name="layers",
    )(h, w_first, w_mine, mask, gslot, grads)


def shards(
    patches,
    image_units,
    v_gain,
    v_qkv,
    v_out,
    merge_gain,
    w_merge,
    routes,
    text,
    seq_lengths,
    lang_gain,
    w_qkv,
    wo_t,
    row_grads,
):
    section = lax.axis_index("section")
    x = lax.axis_index("x")
    y = lax.axis_index("y")

    sent = lax.optimization_barrier(jnp.broadcast_to(routes, (routes.shape[0], 128)))
    target = lax.optimization_barrier(
        lax.all_gather(sent, ("y", "x", "mp"), axis=0, tiled=True)
    )[:, 0]
    part = w_merge.shape[0] // 2
    wm = lax.all_gather(
        lax.dynamic_slice_in_dim(w_merge, section * part, part, 0), "y", axis=0, tiled=False
    )
    gain = lax.dynamic_slice_in_dim(lang_gain[0], (y * SIDE + x) * FB, FB, 0)
    scaled = (w_qkv[0].astype(F32) * gain[:, None]).astype(BF)
    w_mine = jnp.concatenate([scaled, wo_t[0]], axis=1)
    swapped = lax.ppermute(w_mine[FB // 2 :], "section", [(0, 1)])
    w_half = jnp.where(section == 0, w_mine[: FB // 2], swapped)
    w_first = lax.all_gather(w_half, "y", axis=0, tiled=False)

    count = target.shape[0]
    order = jnp.arange(count, dtype=jnp.int32)
    position = jnp.sum(
        ((target[:, None] == target[None, :]) & (order[:, None] > order[None, :])).astype(jnp.int32),
        axis=1,
    )
    lslot = (target - y * SIDE) * TOK + position
    gslot = jnp.where(target % SIDE == x, (target // SIDE) * TOK + position, -1)
    gslot = lax.dynamic_slice_in_dim(gslot, y * 256, 256, 0)

    merged = vision_rows(patches, image_units[0], v_gain, v_qkv, v_out, merge_gain)
    pieces = merged.reshape(16, MERGE, SIDE, 320).transpose(2, 0, 1, 3).reshape(SIDE, 16, VD)
    seq = segment_of(seq_lengths[0], TOK)
    at = jnp.arange(TOK, dtype=jnp.int32)
    mask = ((seq[:, None] == seq[None, :]) & (at[:, None] >= at[None, :])).astype(F32)

    hidden = merge_call(pieces, wm, text, lslot[None, :])
    return layers_call(hidden, w_first, w_mine, mask, gslot[:, None], row_grads)


def solution(mesh):
    grid = jax.sharding.Mesh(
        mesh.devices.reshape(2, SIDE, SIDE, SIDE), ("section", "y", "x", "mp")
    )
    every = ("section", "y", "x", "mp")
    home = P(("section", "y", "x"), "mp")
    in_specs = (
        P(every, None),
        P(every, None),
        P(),
        P(),
        P(),
        P(),
        P(("y", "x"), "mp"),
        P(every, None),
        home,
        P(("section", "y", "x"), None),
        P("section", None),
        P("section", ("y", "x"), "mp"),
        P("section", ("y", "x"), "mp"),
        home,
    )
    out_specs = (home, P(every, None))
    return jax.shard_map(shards, mesh=grid, in_specs=in_specs, out_specs=out_specs, check_vma=False)
```

```python
import functools
import math

import jax
import jax.numpy as jnp
from jax import lax
from jax.experimental import pallas as pl
from jax.experimental.pallas import tpu as pltpu
from jax.sharding import PartitionSpec as P

QH = 32
KVH = 4
HD = 128
VD = 1280
VH = 16
VHD = 80
MERGE = 4
SIDE = 4
TOK = 128
FB = 512
HALF = TOK // 2
STEPS = (1, 3, 2)
HEADS = QH // KVH
QW = HEADS * HD
PW = QW + 2 * HD
PT = PW + HD
D = 8192
EPSILON = 1e-06
VMEM_LIMIT = 60 * 1024 * 1024
BF = jnp.bfloat16
F32 = jnp.float32


def layer_norm(values, norm_gain):
    values = values.astype(F32)
    centre = jnp.mean(values, axis=-1, keepdims=True)
    centred = values - centre
    variance = jnp.mean(centred * centred, axis=-1, keepdims=True)
    return centred * lax.rsqrt(variance + EPSILON) * norm_gain


def segment_of(lengths, amount):
    boundary = jnp.cumsum(lengths.astype(jnp.int32))
    positions = jnp.arange(amount, dtype=jnp.int32)
    return jnp.sum((positions[:, None] >= boundary[None, :]).astype(jnp.int32), axis=1)


def vision_rows(patches, units, v_gain, v_qkv, v_out, merge_gain):
    amount = patches.shape[0]
    merged_count = amount // MERGE
    unit_image = segment_of(units, merged_count)
    image_ids = jnp.broadcast_to(unit_image[:, None], (merged_count, MERGE)).reshape(amount)
    v_normed = layer_norm(patches, v_gain).astype(BF)
    projected = jnp.dot(v_normed, v_qkv, preferred_element_type=F32).astype(BF)
    projected = projected.reshape(amount, 3, VH, VHD)
    scores = jnp.einsum(
        "qhd,khd->hqk", projected[:, 0], projected[:, 1], preferred_element_type=F32
    ) / math.sqrt(VHD)
    allowed = image_ids[:, None] == image_ids[None, :]
    scores = jnp.where(allowed[None], scores, -1e30)
    weights = jax.nn.softmax(scores, axis=-1).astype(BF)
    attended = (
        jnp.einsum("hqk,khd->qhd", weights, projected[:, 2], preferred_element_type=F32)
        .astype(BF)
        .reshape(amount, VD)
    )
    update = jnp.dot(attended, v_out, preferred_element_type=F32)
    v_hidden = (patches.astype(F32) + update).astype(BF)
    merged = layer_norm(v_hidden, merge_gain).astype(BF)
    return merged.reshape(merged_count, MERGE * VD)


def push(src, dst, send_sem, recv_sem, where):
    copy = pltpu.make_async_remote_copy(
        src_ref=src,
        dst_ref=dst,
        send_sem=send_sem,
        recv_sem=recv_sem,
        device_id=where,
        device_id_type=pl.DeviceIdType.MESH,
    )
    copy.start()
    return copy


def greet(partners):
    barrier = pltpu.get_barrier_semaphore()
    for where in partners:
        pl.semaphore_signal(
            barrier, inc=1, device_id=where, device_id_type=pl.DeviceIdType.MESH
        )
    pl.semaphore_wait(barrier, len(partners))


def along(index, step):
    return lax.rem(index + step, SIDE)


def behind(index, step):
    return lax.rem(index + SIDE - step, SIDE)


def merge_kernel(
    pieces, wm, text, placed,
    h0, gslot,
    wmv, xbuf, part, psend, rbuf, ybuf, tbuf, pick, rt, ry, tri, line,
    w_sem, s_w, r_w, s_pl, r_pl, s_x, r_x, s_y, r_y, s_t, r_t, s_rt, r_rt, s_ry, r_ry,
):
    section = lax.axis_index("section")
    x = lax.axis_index("x")
    y = lax.axis_index("y")
    z = lax.axis_index("mp")
    plane = [(dx, dz) for dx in range(SIDE) for dz in range(SIDE) if dx or dz]
    half = wm.shape[1]

    for block in range(SIDE):
        pltpu.make_async_copy(wm.at[block], wmv.at[block, section], w_sem.at[block]).start()
    greet(
        [{"x": along(x, dx), "mp": along(z, dz)} for dx, dz in plane]
        + [{"y": along(y, dy)} for dy in STEPS]
        + [{"section": 1 - section}]
    )
    route_copies = [
        push(
            placed, rt.at[x * SIDE + z], s_rt.at[dx * SIDE + dz], r_rt.at[dx * SIDE + dz],
            {"x": along(x, dx), "mp": along(z, dz)},
        )
        for dx, dz in plane
    ]
    rt[x * SIDE + z] = placed[...]
    plane_copies = []
    for dx, dz in plane:
        xt = along(x, dx)
        plane_copies.append(
            push(
                pieces.at[xt], xbuf.at[x * SIDE + z],
                s_pl.at[dx * SIDE + dz], r_pl.at[dx * SIDE + dz],
                {"x": xt, "mp": along(z, dz)},
            )
        )
    xbuf[x * SIDE + z] = pieces[x]
    twin_copies = [
        push(
            wm.at[block], wmv.at[block, section], s_w.at[block], r_w.at[block],
            {"section": 1 - section},
        )
        for block in range(SIDE)
    ]
    text_copies = []
    for dx in STEPS:
        xt = along(x, dx)
        text_copies.append(
            push(
                text.at[:, pl.ds(pl.multiple_of(xt * FB, FB), FB)], tbuf.at[x],
                s_t.at[dx], r_t.at[dx], {"x": xt},
            )
        )
    tbuf[x] = text[:, pl.ds(pl.multiple_of(x * FB, FB), FB)]

    count = tri.shape[0]
    for block in range(SIDE):
        before = lax.broadcasted_iota(jnp.int32, (256, count), 0) + block * 256
        after = lax.broadcasted_iota(jnp.int32, (256, count), 1)
        tri[block * 256 : (block + 1) * 256, :] = jnp.where(before < after, 1.0, 0.0).astype(BF)
    for copy in route_copies:
        copy.wait()
    known = rt[0]
    for source in range(1, SIDE * SIDE):
        known = known + rt[source]
    ry[y] = known
    ry_copies = [
        push(ry.at[y], ry.at[y], s_ry.at[dy], r_ry.at[dy], {"y": along(y, dy)})
        for dy in STEPS
    ]

    for block in range(SIDE):
        pltpu.make_async_copy(wm.at[block], wmv.at[block, section], w_sem.at[block]).wait()
    for copy in twin_copies:
        copy.wait()
    for copy in plane_copies:
        copy.wait()

    def product(dx):
        cols = pl.ds(pl.multiple_of(along(x, dx) * FB, FB), FB)
        rows = xbuf[...].reshape(SIDE * SIDE * 16, VD)
        weights = wmv[:, :, :, cols].reshape(SIDE * 2 * half, FB)
        return jnp.dot(rows, weights, preferred_element_type=F32)

    x_copies = []
    for dx in STEPS:
        psend[dx] = product(dx).astype(BF)
        x_copies.append(
            push(psend.at[dx], rbuf.at[dx], s_x.at[dx], r_x.at[dx], {"x": along(x, dx)})
        )
    part[...] = product(0)

    for copy in ry_copies:
        copy.wait()
    target = ry[0] + ry[1] + ry[2] + ry[3]
    groups = lax.broadcasted_iota(jnp.int32, (SIDE * SIDE, count), 0)
    named = jnp.where(groups == target, 1.0, 0.0)
    earlier = jnp.dot(named.astype(BF), tri[...], preferred_element_type=F32)
    position = jnp.sum(named * earlier, axis=0, keepdims=True).astype(jnp.int32)
    slots = (target - y * SIDE) * TOK + position
    for block in range(SIDE):
        wanted = lax.broadcasted_iota(jnp.int32, (TOK, count), 0) + block * TOK
        pick[pl.ds(block * TOK, TOK), :] = jnp.where(wanted == slots, 1.0, 0.0).astype(BF)
    line[...] = jnp.where((target & 3) == x, (target >> 2) * TOK + position + 1, 0)
    returned = line[:, pl.ds(pl.multiple_of(y * 256, 256), 256)]
    across = lax.broadcasted_iota(jnp.int32, (256, 256), 1)
    down = lax.broadcasted_iota(jnp.int32, (256, 256), 0)
    same = jnp.where(across == down, 1.0, 0.0).astype(BF)

    def upright(row):
        wide = jnp.broadcast_to(row.astype(F32), (128, 256)).astype(BF)
        return lax.dot_general(
            same, wide, (((1,), (1,)), ((), ())), preferred_element_type=F32
        )

    gslot[...] = (16.0 * upright(returned >> 4) + upright(returned & 15)).astype(jnp.int32) - 1

    for copy in x_copies:
        copy.wait()
    total = part[...]
    for dx in STEPS:
        total = total + rbuf[dx].astype(F32)
    ybuf[y] = total.astype(BF)
    y_copies = [
        push(ybuf.at[y], ybuf.at[y], s_y.at[dy], r_y.at[dy], {"y": along(y, dy)})
        for dy in STEPS
    ]
    chosen = pick[...]
    present = jnp.dot(chosen, jnp.ones((SIDE * 256, 128), BF), preferred_element_type=F32)
    for copy in text_copies:
        copy.wait()
    for copy in y_copies:
        copy.wait()
    picked = jnp.dot(
        chosen, ybuf[...].reshape(SIDE * 256, FB), preferred_element_type=F32
    ).astype(BF)
    for group in range(SIDE):
        for part_of in range(2):
            rows = slice(group * TOK + part_of * HALF, group * TOK + (part_of + 1) * HALF)
            to = slice(group * HALF, (group + 1) * HALF)
            inside = slice(part_of * HALF, (part_of + 1) * HALF)
            for tile in range(FB // 128):
                cols = slice(tile * 128, (tile + 1) * 128)
                h0[part_of, to, cols] = jnp.where(
                    present[rows, :] > 0.5, picked[rows, cols], tbuf[group, inside, cols]
                )


def merge_call(pieces, wm, text, placed):
    vmem = pl.BlockSpec(memory_space=pltpu.VMEM)
    dma = pltpu.SemaphoreType.DMA
    half = wm.shape[1]
    return pl.pallas_call(
        merge_kernel,
        out_shape=(
            jax.ShapeDtypeStruct((2, SIDE * HALF, FB), BF),
            jax.ShapeDtypeStruct((256, 128), jnp.int32),
        ),
        in_specs=[vmem, pl.BlockSpec(memory_space=pl.ANY), vmem, vmem],
        out_specs=(vmem, vmem),
        scratch_shapes=[
            pltpu.VMEM((SIDE, 2, half, SIDE * FB), BF),
            pltpu.VMEM((SIDE * SIDE, 16, VD), BF),
            pltpu.VMEM((256, FB), F32),
            pltpu.VMEM((SIDE, 256, FB), BF),
            pltpu.VMEM((SIDE, 256, FB), BF),
            pltpu.VMEM((SIDE, 256, FB), BF),
            pltpu.VMEM((SIDE, TOK, FB), BF),
            pltpu.VMEM((SIDE * TOK, 1024), BF),
            pltpu.VMEM((SIDE * SIDE, 1, 1024), jnp.int32),
            pltpu.VMEM((SIDE, 1, 1024), jnp.int32),
            pltpu.VMEM((1024, 1024), BF),
            pltpu.VMEM((1, 1024), jnp.int32),
            dma((SIDE,)),
            dma((SIDE,)), dma((SIDE,)),
            dma((16,)), dma((16,)),
            dma((SIDE,)), dma((SIDE,)),
            dma((SIDE,)), dma((SIDE,)),
            dma((SIDE,)), dma((SIDE,)),
            dma((16,)), dma((16,)),
            dma((SIDE,)), dma((SIDE,)),
        ],
        compiler_params=pltpu.CompilerParams(
            collective_id=1, has_side_effects=True, vmem_limit_bytes=VMEM_LIMIT
        ),
        name="merge",
    )(pieces, wm, text, placed)


def layers_kernel(
    h, w_first, w_mine, mask, gslot, grads,
    out, mg,
    w, zbuf, acc, squares, kv, psend, rbuf, abuf, osend, orec, obuf,
    gbuf, gsend, grec, gz, mz,
    w_sem, s_w0, r_w0, s_w1, r_w1, s_w2, r_w2,
    s_z, r_z, s_x, r_x, s_a, r_a, s_o, r_o, s_e, r_e,
    s_g, r_g, s_gx, r_gx, s_gz, r_gz,
):
    section = lax.axis_index("section")
    x = lax.axis_index("x")
    y = lax.axis_index("y")
    z = lax.axis_index("mp")
    twin = {"section": 1 - section}
    rows = SIDE * HALF
    half = FB // 2
    width = grads.shape[1]
    mine = pl.ds(pl.multiple_of(section * half, half), half)

    own_load = pltpu.make_async_copy(w_first, w.at[0, :, mine, :], w_sem.at[0])
    own_load.start()
    own_shard = pltpu.make_async_copy(w_mine, w.at[1, y], w_sem.at[1])
    for part in range(2):
        zbuf[0, part, z] = h[part]
    greet(
        [{"x": along(x, d)} for d in STEPS]
        + [{"mp": along(z, d)} for d in STEPS]
        + [{"y": along(y, d)} for d in STEPS]
        + [twin]
    )

    z_copies, x_copies, a_copies, o_copies, e_copies = {}, {}, {}, {}, []

    def spread(layer, part):
        z_copies[layer, part] = {
            dz: push(
                zbuf.at[layer, part, z], zbuf.at[layer, part, z],
                s_z.at[layer, part, dz], r_z.at[layer, part, dz], {"mp": along(z, dz)},
            )
            for dz in STEPS
        }

    def project(layer, part):
        for dz in (0, 1, 3, 2):
            zs = behind(z, dz)
            if dz:
                z_copies[layer, part][dz].wait()
            wide = zbuf[layer, part, zs].astype(F32)
            squared = jnp.sum(wide * wide, axis=1, keepdims=True)
            if dz:
                squares[part] += jnp.broadcast_to(squared, (rows, HD))
            else:
                squares[part] = jnp.broadcast_to(squared, (rows, HD))

            @pl.loop(0, PW // 256)
            def _(tile):
                cols = pl.ds(pl.multiple_of(tile * 256, 256), 256)
                product = jnp.dot(
                    zbuf[layer, part, zs], w[layer, zs, :, cols], preferred_element_type=F32
                )
                if dz:
                    acc[part, :, cols] += product
                else:
                    acc[part, :, cols] = product

        lane = lax.broadcasted_iota(jnp.int32, (HALF, HD), 1)
        copies = []
        for dx in STEPS:
            xt = along(x, dx)
            span = pl.ds(pl.multiple_of(xt * HALF, HALF), HALF)
            psend[layer, part, dx, :, :PW] = acc[part, span, :].astype(BF)
            sq = squares[part, span, :]
            high = sq.astype(BF)
            low = (sq - high.astype(F32)).astype(BF)
            psend[layer, part, dx, :, PW:] = jnp.where(lane < 64, high, low)
            copies.append(
                push(
                    psend.at[layer, part, dx], rbuf.at[layer, part, dx],
                    s_x.at[layer, part, dx], r_x.at[layer, part, dx], {"x": xt},
                )
            )
        x_copies[layer, part] = copies

    def attend(layer, part):
        own = pl.ds(pl.multiple_of(x * HALF, HALF), HALF)
        total = acc[part, own, :]
        sq = squares[part, own, :][:, :1]
        for copy in x_copies[layer, part]:
            copy.wait()
        for dx in STEPS:
            total = total + rbuf[layer, part, dx, :, :PW].astype(F32)
            tail = rbuf[layer, part, dx, :, PW:].astype(F32)
            sq = sq + tail[:, :1] + tail[:, 64:65]
        projected = (total * lax.rsqrt(sq / D + EPSILON)).astype(BF)
        kv[part * HALF : (part + 1) * HALF, :] = projected[:, QW:]
        seen = (part + 1) * HALF
        keys = kv[:seen, :HD]
        values = kv[:seen, HD:]
        queries = jnp.concatenate(
            [projected[:, head * HD : (head + 1) * HD] for head in range(HEADS)], axis=0
        )
        allowed = mask[part * HALF : (part + 1) * HALF, :seen]
        allowed = jnp.concatenate([allowed] * HEADS, axis=0) > 0.5
        scores = lax.dot_general(
            queries, keys, (((1,), (1,)), ((), ())), preferred_element_type=F32
        ) * (1.0 / math.sqrt(HD))
        scores = jnp.where(allowed, scores, -1e30)
        top = jnp.max(scores, axis=1, keepdims=True)
        weights = jnp.exp(scores - top)
        weights = (weights / jnp.sum(weights, axis=1, keepdims=True)).astype(BF)
        mixed = jnp.dot(weights, values, preferred_element_type=F32).astype(BF)
        for head in range(HEADS):
            abuf[layer, part, x, :, head * HD : (head + 1) * HD] = mixed[
                head * HALF : (head + 1) * HALF, :
            ]
        a_copies[layer, part] = [
            push(
                abuf.at[layer, part, x], abuf.at[layer, part, x],
                s_a.at[layer, part, dx], r_a.at[layer, part, dx], {"x": along(x, dx)},
            )
            for dx in STEPS
        ]

    def output(layer, part):
        for copy in a_copies[layer, part]:
            copy.wait()
        copies = []
        for dz in (1, 3, 2, 0):
            zt = along(z, dz)

            @pl.loop(0, FB // 256)
            def _(tile):
                cols = pl.ds(pl.multiple_of(tile * 256, 256), 256)
                osend[layer, part, dz, :, cols] = lax.dot_general(
                    abuf[layer, part].reshape(rows, QW), w[layer, zt, cols, PW:],
                    (((1,), (1,)), ((), ())), preferred_element_type=F32,
                ).astype(BF)

            if dz:
                copies.append(
                    push(
                        osend.at[layer, part, dz], orec.at[layer, part, dz],
                        s_o.at[layer, part, dz], r_o.at[layer, part, dz], {"mp": zt},
                    )
                )
        o_copies[layer, part] = copies

    def finish(layer, part):
        update = osend[layer, part, 0].astype(F32)
        for copy in o_copies[layer, part]:
            copy.wait()
        for dz in STEPS:
            update = update + orec[layer, part, dz].astype(F32)
        fresh = (zbuf[layer, part, z].astype(F32) + update).astype(BF)
        if layer == 0:
            zbuf[1, part, z] = fresh
            return
        osend[layer, part, 0] = fresh
        for dx in STEPS:
            xt = along(x, dx)
            e_copies.append(
                push(
                    osend.at[layer, part, 0, pl.ds(pl.multiple_of(xt * HALF, HALF), HALF), :],
                    obuf.at[x, part],
                    s_e.at[part, dx], r_e.at[part, dx], {"x": xt},
                )
            )
        obuf[x, part] = osend[
            layer, part, 0, pl.ds(pl.multiple_of(x * HALF, HALF), HALF), :
        ]

    spread(0, 0)
    spread(0, 1)
    twin_copy = push(w_first, w.at[0, :, mine, :], s_w0.at[0], r_w0.at[0], twin)

    def shard_copy(dy):
        return pltpu.make_async_remote_copy(
            src_ref=w_mine, dst_ref=w.at[1, y], send_sem=s_w1.at[dy], recv_sem=r_w1.at[dy],
            device_id={"y": along(y, dy)}, device_id_type=pl.DeviceIdType.MESH,
        )

    def forward_copy(dy):
        ys = behind(y, dy)
        return pltpu.make_async_remote_copy(
            src_ref=w.at[1, ys], dst_ref=w.at[1, ys], send_sem=s_w2.at[dy],
            recv_sem=r_w2.at[dy], device_id=twin, device_id_type=pl.DeviceIdType.MESH,
        )

    @pl.when(section == 1)
    def _():
        for dy in STEPS:
            shard_copy(dy).start()
        own_shard.start()

    own_load.wait()
    twin_copy.wait()
    project(0, 0)
    project(0, 1)
    attend(0, 0)
    attend(0, 1)
    g_copies = [
        push(grads, gbuf.at[y], s_g.at[dy], r_g.at[dy], {"y": along(y, dy)}) for dy in STEPS
    ]
    gbuf[y] = grads[...]
    output(0, 0)
    output(0, 1)

    @pl.when(section == 1)
    def _():
        own_shard.wait()
        forward_copy(0).start()
        for dy in STEPS:
            shard_copy(dy).wait()
            forward_copy(dy).start()

    finish(0, 0)
    spread(1, 0)
    finish(0, 1)
    spread(1, 1)

    @pl.when(section == 0)
    def _():
        for dy in range(SIDE):
            forward_copy(dy).wait_recv()

    project(1, 0)
    project(1, 1)
    attend(1, 0)
    attend(1, 1)

    for copy in g_copies:
        copy.wait()
    gx_copies = []
    for dx in (1, 3, 2, 0):
        xt = along(x, dx)
        wanted = gslot[pl.ds(pl.multiple_of(xt * 64, 64), 64), :1]
        lanes = lax.broadcasted_iota(jnp.int32, (64, SIDE * TOK), 1)
        chosen = jnp.where(lanes == wanted, 1.0, 0.0).astype(BF)
        gsend[dx] = jnp.dot(
            chosen, gbuf[...].reshape(SIDE * TOK, width), preferred_element_type=F32
        ).astype(BF)
        if dx:
            gx_copies.append(
                push(gsend.at[dx], grec.at[dx], s_gx.at[dx], r_gx.at[dx], {"x": xt})
            )

    output(1, 0)
    output(1, 1)
    for copy in gx_copies:
        copy.wait()
    found = gsend[0].astype(F32)
    for dx in STEPS:
        found = found + grec[dx].astype(F32)
    gz[...] = found.astype(BF).reshape(SIDE, 16, width)
    gz_copies = []
    for dz in STEPS:
        zt = along(z, dz)
        gz_copies.append(push(gz.at[zt], mz.at[z], s_gz.at[dz], r_gz.at[dz], {"mp": zt}))
    mz[z] = gz[z]

    finish(1, 0)
    finish(1, 1)
    for copy in gz_copies:
        copy.wait()
    for block in range(SIDE):
        mg[:, block * width : (block + 1) * width] = mz[block]
    for copy in e_copies:
        copy.wait()
    for block in range(SIDE):
        for part in range(2):
            out[part * HALF : (part + 1) * HALF, block * FB : (block + 1) * FB] = obuf[block, part]

    @pl.when(section == 1)
    def _():
        for dy in range(SIDE):
            forward_copy(dy).wait_send()


def layers_call(h, w_first, w_mine, mask, gslot, grads):
    vmem = pl.BlockSpec(memory_space=pltpu.VMEM)
    hbm = pl.BlockSpec(memory_space=pl.ANY)
    dma = pltpu.SemaphoreType.DMA
    rows = SIDE * HALF
    width = grads.shape[1]
    stage = dma((2, 2, SIDE))
    return pl.pallas_call(
        layers_kernel,
        out_shape=(
            jax.ShapeDtypeStruct((TOK, SIDE * FB), BF),
            jax.ShapeDtypeStruct((16, SIDE * width), BF),
        ),
        in_specs=[vmem, hbm, hbm, vmem, vmem, vmem],
        out_specs=(vmem, vmem),
        scratch_shapes=[
            pltpu.VMEM((2, SIDE, FB, PW + QW), BF),
            pltpu.VMEM((2, 2, SIDE, rows, FB), BF),
            pltpu.VMEM((2, rows, PW), F32),
            pltpu.VMEM((2, rows, HD), F32),
            pltpu.VMEM((TOK, 2 * HD), BF),
            pltpu.VMEM((2, 2, SIDE, HALF, PT), BF),
            pltpu.VMEM((2, 2, SIDE, HALF, PT), BF),
            pltpu.VMEM((2, 2, SIDE, HALF, QW), BF),
            pltpu.VMEM((2, 2, SIDE, rows, FB), BF),
            pltpu.VMEM((2, 2, SIDE, rows, FB), BF),
            pltpu.VMEM((SIDE, 2, HALF, FB), BF),
            pltpu.VMEM((SIDE, TOK, width), BF),
            pltpu.VMEM((SIDE, 64, width), BF),
            pltpu.VMEM((SIDE, 64, width), BF),
            pltpu.VMEM((SIDE, 16, width), BF),
            pltpu.VMEM((SIDE, 16, width), BF),
            dma((2,)),
            dma((1,)), dma((1,)),
            dma((SIDE,)), dma((SIDE,)),
            dma((SIDE,)), dma((SIDE,)),
            stage, stage,
            stage, stage,
            stage, stage,
            stage, stage,
            dma((2, SIDE)), dma((2, SIDE)),
            dma((SIDE,)), dma((SIDE,)),
            dma((SIDE,)), dma((SIDE,)),
            dma((SIDE,)), dma((SIDE,)),
        ],
        compiler_params=pltpu.CompilerParams(
            collective_id=2, has_side_effects=True, vmem_limit_bytes=VMEM_LIMIT
        ),
        name="layers",
    )(h, w_first, w_mine, mask, gslot, grads)


def shards(
    patches,
    image_units,
    v_gain,
    v_qkv,
    v_out,
    merge_gain,
    w_merge,
    routes,
    text,
    seq_lengths,
    lang_gain,
    w_qkv,
    wo_t,
    row_grads,
):
    section = lax.axis_index("section")
    x = lax.axis_index("x")
    y = lax.axis_index("y")

    part = w_merge.shape[0] // 2
    wm = lax.all_gather(
        lax.dynamic_slice_in_dim(w_merge, section * part, part, 0), "y", axis=0, tiled=False
    )
    gain = lax.dynamic_slice_in_dim(lang_gain[0], (y * SIDE + x) * FB, FB, 0)
    scaled = (w_qkv[0].astype(F32) * gain[:, None]).astype(BF)
    w_mine = jnp.concatenate([scaled, wo_t[0]], axis=1)
    swapped = lax.ppermute(w_mine[FB // 2 :], "section", [(0, 1)])
    w_half = jnp.where(section == 0, w_mine[: FB // 2], swapped)
    w_first = lax.all_gather(w_half, "y", axis=0, tiled=False)

    z = lax.axis_index("mp")
    place = jnp.arange(1024, dtype=jnp.int32)
    repeated = jnp.broadcast_to(routes[:, 0][None, :], (64, 16)).reshape(1024)
    placed = jnp.where(place // 16 == (y * SIDE + x) * SIDE + z, repeated, 0)[None, :]

    merged = vision_rows(patches, image_units[0], v_gain, v_qkv, v_out, merge_gain)
    pieces = merged.reshape(16, MERGE, SIDE, 320).transpose(2, 0, 1, 3).reshape(SIDE, 16, VD)
    seq = segment_of(seq_lengths[0], TOK)
    at = jnp.arange(TOK, dtype=jnp.int32)
    mask = ((seq[:, None] == seq[None, :]) & (at[:, None] >= at[None, :])).astype(F32)

    hidden, gslot = merge_call(pieces, wm, text, placed)
    return layers_call(hidden, w_first, w_mine, mask, gslot, row_grads)


def solution(mesh):
    grid = jax.sharding.Mesh(
        mesh.devices.reshape(2, SIDE, SIDE, SIDE), ("section", "y", "x", "mp")
    )
    every = ("section", "y", "x", "mp")
    home = P(("section", "y", "x"), "mp")
    in_specs = (
        P(every, None),
        P(every, None),
        P(),
        P(),
        P(),
        P(),
        P(("y", "x"), "mp"),
        P(every, None),
        home,
        P(("section", "y", "x"), None),
        P("section", None),
        P("section", ("y", "x"), "mp"),
        P("section", ("y", "x"), "mp"),
        home,
    )
    out_specs = (home, P(every, None))
    return jax.shard_map(shards, mesh=grid, in_specs=in_specs, out_specs=out_specs, check_vma=False)
```

```python
import functools
import math

import jax
import jax.numpy as jnp
from jax import lax
from jax.experimental import pallas as pl
from jax.experimental.pallas import tpu as pltpu
from jax.sharding import PartitionSpec as P

QH = 32
KVH = 4
HD = 128
VD = 1280
VH = 16
VHD = 80
MERGE = 4
SIDE = 4
TOK = 128
FB = 512
HALF = TOK // 2
STEPS = (1, 3, 2)
HEADS = QH // KVH
QW = HEADS * HD
PW = QW + 2 * HD
PT = PW + HD
D = 8192
EPSILON = 1e-06
VMEM_LIMIT = 60 * 1024 * 1024
BF = jnp.bfloat16
F32 = jnp.float32


def layer_norm(values, norm_gain):
    values = values.astype(F32)
    centre = jnp.mean(values, axis=-1, keepdims=True)
    centred = values - centre
    variance = jnp.mean(centred * centred, axis=-1, keepdims=True)
    return centred * lax.rsqrt(variance + EPSILON) * norm_gain


def segment_of(lengths, amount):
    boundary = jnp.cumsum(lengths.astype(jnp.int32))
    positions = jnp.arange(amount, dtype=jnp.int32)
    return jnp.sum((positions[:, None] >= boundary[None, :]).astype(jnp.int32), axis=1)


def vision_rows(patches, units, v_gain, v_qkv, v_out, merge_gain):
    amount = patches.shape[0]
    merged_count = amount // MERGE
    unit_image = segment_of(units, merged_count)
    image_ids = jnp.broadcast_to(unit_image[:, None], (merged_count, MERGE)).reshape(amount)
    v_normed = layer_norm(patches, v_gain).astype(BF)
    projected = jnp.dot(v_normed, v_qkv, preferred_element_type=F32).astype(BF)
    projected = projected.reshape(amount, 3, VH, VHD)
    scores = jnp.einsum(
        "qhd,khd->hqk", projected[:, 0], projected[:, 1], preferred_element_type=F32
    ) / math.sqrt(VHD)
    allowed = image_ids[:, None] == image_ids[None, :]
    scores = jnp.where(allowed[None], scores, -1e30)
    weights = jax.nn.softmax(scores, axis=-1).astype(BF)
    attended = (
        jnp.einsum("hqk,khd->qhd", weights, projected[:, 2], preferred_element_type=F32)
        .astype(BF)
        .reshape(amount, VD)
    )
    update = jnp.dot(attended, v_out, preferred_element_type=F32)
    v_hidden = (patches.astype(F32) + update).astype(BF)
    merged = layer_norm(v_hidden, merge_gain).astype(BF)
    return merged.reshape(merged_count, MERGE * VD)


def push(src, dst, send_sem, recv_sem, where):
    copy = pltpu.make_async_remote_copy(
        src_ref=src,
        dst_ref=dst,
        send_sem=send_sem,
        recv_sem=recv_sem,
        device_id=where,
        device_id_type=pl.DeviceIdType.MESH,
    )
    copy.start()
    return copy


def greet(partners):
    barrier = pltpu.get_barrier_semaphore()
    for where in partners:
        pl.semaphore_signal(
            barrier, inc=1, device_id=where, device_id_type=pl.DeviceIdType.MESH
        )
    pl.semaphore_wait(barrier, len(partners))


def along(index, step):
    return lax.rem(index + step, SIDE)


def behind(index, step):
    return lax.rem(index + SIDE - step, SIDE)


def merge_kernel(
    pieces, wm, text, placed,
    h0, gslot,
    wmv, xbuf, part, psend, rbuf, ybuf, tbuf, pick, rt, ry, tri, line,
    w_sem, s_w, r_w, s_pl, r_pl, s_x, r_x, s_y, r_y, s_t, r_t, s_rt, r_rt, s_ry, r_ry,
):
    section = lax.axis_index("section")
    x = lax.axis_index("x")
    y = lax.axis_index("y")
    z = lax.axis_index("mp")
    plane = [(dx, dz) for dx in range(SIDE) for dz in range(SIDE) if dx or dz]
    half = wm.shape[1]

    for block in range(SIDE):
        pltpu.make_async_copy(wm.at[block], wmv.at[block, section], w_sem.at[block]).start()
    greet(
        [{"x": along(x, dx), "mp": along(z, dz)} for dx, dz in plane]
        + [{"y": along(y, dy)} for dy in STEPS]
        + [{"section": 1 - section}]
    )
    route_copies = [
        push(
            placed, rt.at[x * SIDE + z], s_rt.at[dx * SIDE + dz], r_rt.at[dx * SIDE + dz],
            {"x": along(x, dx), "mp": along(z, dz)},
        )
        for dx, dz in plane
    ]
    rt[x * SIDE + z] = placed[...]
    plane_copies = []
    for dx, dz in plane:
        xt = along(x, dx)
        plane_copies.append(
            push(
                pieces.at[xt], xbuf.at[x * SIDE + z],
                s_pl.at[dx * SIDE + dz], r_pl.at[dx * SIDE + dz],
                {"x": xt, "mp": along(z, dz)},
            )
        )
    xbuf[x * SIDE + z] = pieces[x]
    twin_copies = [
        push(
            wm.at[block], wmv.at[block, section], s_w.at[block], r_w.at[block],
            {"section": 1 - section},
        )
        for block in range(SIDE)
    ]
    text_copies = []
    for dx in STEPS:
        xt = along(x, dx)
        text_copies.append(
            push(
                text.at[:, pl.ds(pl.multiple_of(xt * FB, FB), FB)], tbuf.at[x],
                s_t.at[dx], r_t.at[dx], {"x": xt},
            )
        )
    tbuf[x] = text[:, pl.ds(pl.multiple_of(x * FB, FB), FB)]

    count = tri.shape[0]
    for block in range(SIDE):
        before = lax.broadcasted_iota(jnp.int32, (256, count), 0) + block * 256
        after = lax.broadcasted_iota(jnp.int32, (256, count), 1)
        tri[block * 256 : (block + 1) * 256, :] = jnp.where(before < after, 1.0, 0.0).astype(BF)
    for copy in route_copies:
        copy.wait()
    known = rt[0]
    for source in range(1, SIDE * SIDE):
        known = known + rt[source]
    ry[y] = known
    ry_copies = [
        push(ry.at[y], ry.at[y], s_ry.at[dy], r_ry.at[dy], {"y": along(y, dy)})
        for dy in STEPS
    ]

    for block in range(SIDE):
        pltpu.make_async_copy(wm.at[block], wmv.at[block, section], w_sem.at[block]).wait()
    for copy in twin_copies:
        copy.wait()
    for copy in plane_copies:
        copy.wait()

    def product(dx):
        cols = pl.ds(pl.multiple_of(along(x, dx) * FB, FB), FB)
        rows = xbuf[...].reshape(SIDE * SIDE * 16, VD)
        weights = wmv[:, :, :, cols].reshape(SIDE * 2 * half, FB)
        return jnp.dot(rows, weights, preferred_element_type=F32)

    x_copies = []
    for dx in STEPS:
        psend[dx] = product(dx).astype(BF)
        x_copies.append(
            push(psend.at[dx], rbuf.at[dx], s_x.at[dx], r_x.at[dx], {"x": along(x, dx)})
        )
    part[...] = product(0)

    for copy in ry_copies:
        copy.wait()
    target = ry[0] + ry[1] + ry[2] + ry[3]
    groups = lax.broadcasted_iota(jnp.int32, (SIDE * SIDE, count), 0)
    named = jnp.where(groups == target, 1.0, 0.0)
    earlier = jnp.dot(named.astype(BF), tri[...], preferred_element_type=F32)
    position = jnp.sum(named * earlier, axis=0, keepdims=True).astype(jnp.int32)
    slots = (target - y * SIDE) * TOK + position
    for block in range(SIDE):
        wanted = lax.broadcasted_iota(jnp.int32, (TOK, count), 0) + block * TOK
        pick[pl.ds(block * TOK, TOK), :] = jnp.where(wanted == slots, 1.0, 0.0).astype(BF)
    line[...] = jnp.where((target & 3) == x, (target >> 2) * TOK + position + 1, 0)
    returned = line[:, pl.ds(pl.multiple_of(y * 256, 256), 256)]
    across = lax.broadcasted_iota(jnp.int32, (256, 256), 1)
    down = lax.broadcasted_iota(jnp.int32, (256, 256), 0)
    same = jnp.where(across == down, 1.0, 0.0).astype(BF)

    def upright(row):
        wide = jnp.broadcast_to(row.astype(F32), (128, 256)).astype(BF)
        return lax.dot_general(
            same, wide, (((1,), (1,)), ((), ())), preferred_element_type=F32
        )

    gslot[...] = (16.0 * upright(returned >> 4) + upright(returned & 15)).astype(jnp.int32) - 1

    for copy in x_copies:
        copy.wait()
    total = part[...]
    for dx in STEPS:
        total = total + rbuf[dx].astype(F32)
    ybuf[y] = total.astype(BF)
    y_copies = [
        push(ybuf.at[y], ybuf.at[y], s_y.at[dy], r_y.at[dy], {"y": along(y, dy)})
        for dy in STEPS
    ]
    chosen = pick[...]
    present = jnp.dot(chosen, jnp.ones((SIDE * 256, 128), BF), preferred_element_type=F32)
    for copy in text_copies:
        copy.wait()
    for copy in y_copies:
        copy.wait()
    picked = jnp.dot(
        chosen, ybuf[...].reshape(SIDE * 256, FB), preferred_element_type=F32
    ).astype(BF)
    for group in range(SIDE):
        for part_of in range(2):
            rows = slice(group * TOK + part_of * HALF, group * TOK + (part_of + 1) * HALF)
            to = slice(group * HALF, (group + 1) * HALF)
            inside = slice(part_of * HALF, (part_of + 1) * HALF)
            for tile in range(FB // 128):
                cols = slice(tile * 128, (tile + 1) * 128)
                h0[part_of, to, cols] = jnp.where(
                    present[rows, :] > 0.5, picked[rows, cols], tbuf[group, inside, cols]
                )


def merge_call(pieces, wm, text, placed):
    vmem = pl.BlockSpec(memory_space=pltpu.VMEM)
    dma = pltpu.SemaphoreType.DMA
    half = wm.shape[1]
    return pl.pallas_call(
        merge_kernel,
        out_shape=(
            jax.ShapeDtypeStruct((2, SIDE * HALF, FB), BF),
            jax.ShapeDtypeStruct((256, 128), jnp.int32),
        ),
        in_specs=[vmem, pl.BlockSpec(memory_space=pl.ANY), vmem, vmem],
        out_specs=(vmem, vmem),
        scratch_shapes=[
            pltpu.VMEM((SIDE, 2, half, SIDE * FB), BF),
            pltpu.VMEM((SIDE * SIDE, 16, VD), BF),
            pltpu.VMEM((256, FB), F32),
            pltpu.VMEM((SIDE, 256, FB), BF),
            pltpu.VMEM((SIDE, 256, FB), BF),
            pltpu.VMEM((SIDE, 256, FB), BF),
            pltpu.VMEM((SIDE, TOK, FB), BF),
            pltpu.VMEM((SIDE * TOK, 1024), BF),
            pltpu.VMEM((SIDE * SIDE, 1, 1024), jnp.int32),
            pltpu.VMEM((SIDE, 1, 1024), jnp.int32),
            pltpu.VMEM((1024, 1024), BF),
            pltpu.VMEM((1, 1024), jnp.int32),
            dma((SIDE,)),
            dma((SIDE,)), dma((SIDE,)),
            dma((16,)), dma((16,)),
            dma((SIDE,)), dma((SIDE,)),
            dma((SIDE,)), dma((SIDE,)),
            dma((SIDE,)), dma((SIDE,)),
            dma((16,)), dma((16,)),
            dma((SIDE,)), dma((SIDE,)),
        ],
        compiler_params=pltpu.CompilerParams(
            collective_id=1, has_side_effects=True, vmem_limit_bytes=VMEM_LIMIT
        ),
        name="merge",
    )(pieces, wm, text, placed)


def layers_kernel(
    h, w_first, w_mine, mask, gslot, grads,
    out, mg,
    w, zbuf, acc, squares, kv, psend, rbuf, abuf, osend, orec, orel, obuf,
    gbuf, gsend, grec, gz, mz,
    w_sem, s_w0, r_w0, s_w1, r_w1, s_w2, r_w2, s_v1, r_v1, s_v2, r_v2,
    s_z, r_z, s_x, r_x, s_a, r_a, s_o, r_o, s_e, r_e,
    s_g, r_g, s_gx, r_gx, s_gz, r_gz,
):
    section = lax.axis_index("section")
    x = lax.axis_index("x")
    y = lax.axis_index("y")
    z = lax.axis_index("mp")
    twin = {"section": 1 - section}
    rows = SIDE * HALF
    half = FB // 2
    width = grads.shape[1]
    mine = pl.ds(pl.multiple_of(section * half, half), half)

    left = slice(0, rows // 2)
    right = slice(rows // 2, rows)
    first_cols = pl.ds(0, PW)
    last_cols = pl.ds(PW, QW)
    own_load = pltpu.make_async_copy(w_first, w.at[0, :, mine, first_cols], w_sem.at[0])
    own_load.start()
    own_shard = pltpu.make_async_copy(w_mine, w.at[1, y], w_sem.at[1])
    own_out = pltpu.make_async_copy(
        w_mine.at[:, last_cols], w.at[0, y, :, last_cols], w_sem.at[2]
    )
    for part in range(2):
        zbuf[0, part, z] = h[part]
    greet(
        [{"x": along(x, d)} for d in STEPS]
        + [{"mp": along(z, d)} for d in STEPS]
        + [{"y": along(y, d)} for d in STEPS]
        + [twin]
    )

    z_copies, f_copies, x_copies, a_copies, o_copies, e_copies = {}, {}, {}, {}, {}, []

    def spread(layer, part):
        z_copies[layer, part] = {
            dz: push(
                zbuf.at[layer, part, z], zbuf.at[layer, part, z],
                s_z.at[layer, part, dz], r_z.at[layer, part, dz], {"mp": along(z, dz)},
            )
            for dz in (1, 3)
        }

    def times(layer, part, dz):
        zs = behind(z, dz)
        wide = zbuf[layer, part, zs].astype(F32)
        squared = jnp.sum(wide * wide, axis=1, keepdims=True)
        if dz:
            squares[part] += jnp.broadcast_to(squared, (rows, HD))
        else:
            squares[part] = jnp.broadcast_to(squared, (rows, HD))

        @pl.loop(0, PW // 256)
        def _(tile):
            cols = pl.ds(pl.multiple_of(tile * 256, 256), 256)
            product = jnp.dot(
                zbuf[layer, part, zs], w[layer, zs, :, cols], preferred_element_type=F32
            )
            if dz:
                acc[part, :, cols] += product
            else:
                acc[part, :, cols] = product

    def passed(layer, part):
        copies = z_copies[layer, part]
        copies[1].wait()
        zs = behind(z, 1)
        f_copies[layer, part] = [
            push(
                zbuf.at[layer, part, zs, left], zbuf.at[layer, part, zs, left],
                s_z.at[layer, part, 0], r_z.at[layer, part, 0], {"mp": along(z, 1)},
            )
        ]
        copies[3].wait()
        zs = along(z, 1)
        f_copies[layer, part].append(
            push(
                zbuf.at[layer, part, zs, right], zbuf.at[layer, part, zs, right],
                s_z.at[layer, part, 2], r_z.at[layer, part, 2], {"mp": along(z, 3)},
            )
        )

    def own_part(layer, part):
        times(layer, part, 0)

    def project(layer, part):
        times(layer, part, 1)
        times(layer, part, 3)
        for copy in f_copies[layer, part]:
            copy.wait()
        times(layer, part, 2)
        lane = lax.broadcasted_iota(jnp.int32, (HALF, HD), 1)
        copies = []
        for dx in STEPS:
            xt = along(x, dx)
            span = pl.ds(pl.multiple_of(xt * HALF, HALF), HALF)
            psend[layer, part, dx, :, :PW] = acc[part, span, :].astype(BF)
            sq = squares[part, span, :]
            high = sq.astype(BF)
            low = (sq - high.astype(F32)).astype(BF)
            psend[layer, part, dx, :, PW:] = jnp.where(lane < 64, high, low)
            copies.append(
                push(
                    psend.at[layer, part, dx], rbuf.at[layer, part, dx],
                    s_x.at[layer, part, dx], r_x.at[layer, part, dx], {"x": xt},
                )
            )
        x_copies[layer, part] = copies

    def attend(layer, part):
        own = pl.ds(pl.multiple_of(x * HALF, HALF), HALF)
        total = acc[part, own, :]
        sq = squares[part, own, :][:, :1]
        for copy in x_copies[layer, part]:
            copy.wait()
        for dx in STEPS:
            total = total + rbuf[layer, part, dx, :, :PW].astype(F32)
            tail = rbuf[layer, part, dx, :, PW:].astype(F32)
            sq = sq + tail[:, :1] + tail[:, 64:65]
        projected = (total * lax.rsqrt(sq / D + EPSILON)).astype(BF)
        kv[part * HALF : (part + 1) * HALF, :] = projected[:, QW:]
        seen = (part + 1) * HALF
        keys = kv[:seen, :HD]
        values = kv[:seen, HD:]
        queries = jnp.concatenate(
            [projected[:, head * HD : (head + 1) * HD] for head in range(HEADS)], axis=0
        )
        allowed = mask[part * HALF : (part + 1) * HALF, :seen]
        allowed = jnp.concatenate([allowed] * HEADS, axis=0) > 0.5
        scores = lax.dot_general(
            queries, keys, (((1,), (1,)), ((), ())), preferred_element_type=F32
        ) * (1.0 / math.sqrt(HD))
        scores = jnp.where(allowed, scores, -1e30)
        top = jnp.max(scores, axis=1, keepdims=True)
        weights = jnp.exp(scores - top)
        weights = (weights / jnp.sum(weights, axis=1, keepdims=True)).astype(BF)
        mixed = jnp.dot(weights, values, preferred_element_type=F32).astype(BF)
        for head in range(HEADS):
            abuf[layer, part, x, :, head * HD : (head + 1) * HD] = mixed[
                head * HALF : (head + 1) * HALF, :
            ]
        a_copies[layer, part] = [
            push(
                abuf.at[layer, part, x], abuf.at[layer, part, x],
                s_a.at[layer, part, dx], r_a.at[layer, part, dx], {"x": along(x, dx)},
            )
            for dx in STEPS
        ]

    def output(layer, part):
        for copy in a_copies[layer, part]:
            copy.wait()
        copies = {}

        def send(name, src, dst, dz):
            copies[name] = push(
                src, dst, s_o.at[layer, part, name], r_o.at[layer, part, name],
                {"mp": along(z, dz)},
            )

        for dz in (2, 1, 3, 0):
            zt = along(z, dz)

            @pl.loop(0, FB // 256)
            def _(tile):
                cols = pl.ds(pl.multiple_of(tile * 256, 256), 256)
                osend[layer, part, dz, :, cols] = lax.dot_general(
                    abuf[layer, part].reshape(rows, QW), w[layer, zt, cols, PW:],
                    (((1,), (1,)), ((), ())), preferred_element_type=F32,
                ).astype(BF)

            if dz == 2:
                send(0, osend.at[layer, part, 2, left], orel.at[layer, part, 0], 1)
                send(1, osend.at[layer, part, 2, right], orel.at[layer, part, 1], 3)
            elif dz == 1:
                send(2, osend.at[layer, part, 1, right], orec.at[layer, part, 0, right], 1)
            elif dz == 3:
                send(3, osend.at[layer, part, 3, left], orec.at[layer, part, 1, left], 3)
        o_copies[layer, part] = copies, send

    def relay(layer, part):
        copies, send = o_copies[layer, part]
        copies[0].wait()
        osend[layer, part, 1, left] = (
            osend[layer, part, 1, left].astype(F32) + orel[layer, part, 0].astype(F32)
        ).astype(BF)
        send(4, osend.at[layer, part, 1, left], orec.at[layer, part, 0, left], 1)
        copies[1].wait()
        osend[layer, part, 3, right] = (
            osend[layer, part, 3, right].astype(F32) + orel[layer, part, 1].astype(F32)
        ).astype(BF)
        send(5, osend.at[layer, part, 3, right], orec.at[layer, part, 1, right], 3)

    def finish(layer, part):
        update = osend[layer, part, 0].astype(F32)
        copies, _ = o_copies[layer, part]
        for name in (2, 3, 4, 5):
            copies[name].wait()
        for side in range(2):
            update = update + orec[layer, part, side].astype(F32)
        fresh = (zbuf[layer, part, z].astype(F32) + update).astype(BF)
        if layer == 0:
            zbuf[1, part, z] = fresh
            return
        osend[layer, part, 0] = fresh
        for dx in STEPS:
            xt = along(x, dx)
            e_copies.append(
                push(
                    osend.at[layer, part, 0, pl.ds(pl.multiple_of(xt * HALF, HALF), HALF), :],
                    obuf.at[x, part],
                    s_e.at[part, dx], r_e.at[part, dx], {"x": xt},
                )
            )
        obuf[x, part] = osend[
            layer, part, 0, pl.ds(pl.multiple_of(x * HALF, HALF), HALF), :
        ]

    spread(0, 0)
    twin_copy = push(w_first, w.at[0, :, mine, first_cols], s_w0.at[0], r_w0.at[0], twin)

    def shard_copy(dy):
        return pltpu.make_async_remote_copy(
            src_ref=w_mine, dst_ref=w.at[1, y], send_sem=s_w1.at[dy], recv_sem=r_w1.at[dy],
            device_id={"y": along(y, dy)}, device_id_type=pl.DeviceIdType.MESH,
        )

    def forward_copy(dy):
        ys = behind(y, dy)
        return pltpu.make_async_remote_copy(
            src_ref=w.at[1, ys], dst_ref=w.at[1, ys], send_sem=s_w2.at[dy],
            recv_sem=r_w2.at[dy], device_id=twin, device_id_type=pl.DeviceIdType.MESH,
        )

    def out_copy(dy):
        return pltpu.make_async_remote_copy(
            src_ref=w_mine.at[:, last_cols], dst_ref=w.at[0, y, :, last_cols],
            send_sem=s_v1.at[dy], recv_sem=r_v1.at[dy],
            device_id={"y": along(y, dy)}, device_id_type=pl.DeviceIdType.MESH,
        )

    def out_forward(dy):
        ys = behind(y, dy)
        return pltpu.make_async_remote_copy(
            src_ref=w.at[0, ys, :, last_cols], dst_ref=w.at[0, ys, :, last_cols],
            send_sem=s_v2.at[dy], recv_sem=r_v2.at[dy], device_id=twin,
            device_id_type=pl.DeviceIdType.MESH,
        )

    @pl.when(section == 0)
    def _():
        for dy in STEPS:
            out_copy(dy).start()
        own_out.start()

    def start_last(layer, part):
        @pl.when(section == 1)
        def _():
            for dy in STEPS:
                shard_copy(dy).start()
            own_shard.start()

    def share_out(layer, part):
        @pl.when(section == 0)
        def _():
            own_out.wait()
            out_forward(0).start()
            for dy in STEPS:
                out_copy(dy).wait()
                out_forward(dy).start()

        @pl.when(section == 1)
        def _():
            for dy in range(SIDE):
                out_forward(dy).wait_recv()

    g_copies, gx_copies, gz_copies = [], [], []

    def ready(layer, part):
        if layer == 0:
            own_load.wait()
            twin_copy.wait()
            return

        @pl.when(section == 0)
        def _():
            for dy in range(SIDE):
                forward_copy(dy).wait_recv()

    def forward(layer, part):
        @pl.when(section == 1)
        def _():
            own_shard.wait()
            forward_copy(0).start()
            for dy in STEPS:
                shard_copy(dy).wait()
                forward_copy(dy).start()

    def give(layer, part):
        gbuf[y] = grads[...]
        for dy in STEPS:
            g_copies.append(
                push(grads, gbuf.at[y], s_g.at[dy], r_g.at[dy], {"y": along(y, dy)})
            )

    def choose(layer, part):
        for copy in g_copies:
            copy.wait()
        for dx in (1, 3, 2, 0):
            xt = along(x, dx)
            wanted = gslot[pl.ds(pl.multiple_of(xt * 64, 64), 64), :1]
            lanes = lax.broadcasted_iota(jnp.int32, (64, SIDE * TOK), 1)
            chosen = jnp.where(lanes == wanted, 1.0, 0.0).astype(BF)
            gsend[dx] = jnp.dot(
                chosen, gbuf[...].reshape(SIDE * TOK, width), preferred_element_type=F32
            ).astype(BF)
            if dx:
                gx_copies.append(
                    push(gsend.at[dx], grec.at[dx], s_gx.at[dx], r_gx.at[dx], {"x": xt})
                )

    def hand(layer, part):
        for copy in gx_copies:
            copy.wait()
        found = gsend[0].astype(F32)
        for dx in STEPS:
            found = found + grec[dx].astype(F32)
        gz[...] = found.astype(BF).reshape(SIDE, 16, width)
        for dz in STEPS:
            zt = along(z, dz)
            gz_copies.append(
                push(gz.at[zt], mz.at[z], s_gz.at[dz], r_gz.at[dz], {"mp": zt})
            )
        mz[z] = gz[z]

    for stage, layer, part in (
        (ready, 0, 0),
        (own_part, 0, 0),
        (passed, 0, 0),
        (spread, 0, 1),
        (project, 0, 0),
        (own_part, 0, 1),
        (attend, 0, 0),
        (start_last, 0, 0),
        (passed, 0, 1),
        (project, 0, 1),
        (share_out, 0, 0),
        (output, 0, 0),
        (attend, 0, 1),
        (relay, 0, 0),
        (output, 0, 1),
        (finish, 0, 0),
        (spread, 1, 0),
        (relay, 0, 1),
        (forward, 0, 0),
        (ready, 1, 0),
        (own_part, 1, 0),
        (give, 0, 0),
        (finish, 0, 1),
        (passed, 1, 0),
        (spread, 1, 1),
        (project, 1, 0),
        (own_part, 1, 1),
        (attend, 1, 0),
        (passed, 1, 1),
        (project, 1, 1),
        (output, 1, 0),
        (attend, 1, 1),
        (relay, 1, 0),
        (output, 1, 1),
        (choose, 1, 0),
        (finish, 1, 0),
        (relay, 1, 1),
        (hand, 1, 0),
        (finish, 1, 1),
    ):
        stage(layer, part)

    for copy in gz_copies:
        copy.wait()
    for block in range(SIDE):
        mg[:, block * width : (block + 1) * width] = mz[block]
    for copy in e_copies:
        copy.wait()
    for block in range(SIDE):
        for part in range(2):
            out[part * HALF : (part + 1) * HALF, block * FB : (block + 1) * FB] = obuf[block, part]

    @pl.when(section == 1)
    def _():
        for dy in range(SIDE):
            forward_copy(dy).wait_send()

    @pl.when(section == 0)
    def _():
        for dy in range(SIDE):
            out_forward(dy).wait_send()


def layers_call(h, w_first, w_mine, mask, gslot, grads):
    vmem = pl.BlockSpec(memory_space=pltpu.VMEM)
    hbm = pl.BlockSpec(memory_space=pl.ANY)
    dma = pltpu.SemaphoreType.DMA
    rows = SIDE * HALF
    width = grads.shape[1]
    stage = dma((2, 2, SIDE))
    return pl.pallas_call(
        layers_kernel,
        out_shape=(
            jax.ShapeDtypeStruct((TOK, SIDE * FB), BF),
            jax.ShapeDtypeStruct((16, SIDE * width), BF),
        ),
        in_specs=[vmem, hbm, hbm, vmem, vmem, vmem],
        out_specs=(vmem, vmem),
        scratch_shapes=[
            pltpu.VMEM((2, SIDE, FB, PW + QW), BF),
            pltpu.VMEM((2, 2, SIDE, rows, FB), BF),
            pltpu.VMEM((2, rows, PW), F32),
            pltpu.VMEM((2, rows, HD), F32),
            pltpu.VMEM((TOK, 2 * HD), BF),
            pltpu.VMEM((2, 2, SIDE, HALF, PT), BF),
            pltpu.VMEM((2, 2, SIDE, HALF, PT), BF),
            pltpu.VMEM((2, 2, SIDE, HALF, QW), BF),
            pltpu.VMEM((2, 2, SIDE, rows, FB), BF),
            pltpu.VMEM((2, 2, 2, rows, FB), BF),
            pltpu.VMEM((2, 2, 2, rows // 2, FB), BF),
            pltpu.VMEM((SIDE, 2, HALF, FB), BF),
            pltpu.VMEM((SIDE, TOK, width), BF),
            pltpu.VMEM((SIDE, 64, width), BF),
            pltpu.VMEM((SIDE, 64, width), BF),
            pltpu.VMEM((SIDE, 16, width), BF),
            pltpu.VMEM((SIDE, 16, width), BF),
            dma((3,)),
            dma((1,)), dma((1,)),
            dma((SIDE,)), dma((SIDE,)),
            dma((SIDE,)), dma((SIDE,)),
            dma((SIDE,)), dma((SIDE,)),
            dma((SIDE,)), dma((SIDE,)),
            stage, stage,
            stage, stage,
            stage, stage,
            dma((2, 2, 6)), dma((2, 2, 6)),
            dma((2, SIDE)), dma((2, SIDE)),
            dma((SIDE,)), dma((SIDE,)),
            dma((SIDE,)), dma((SIDE,)),
            dma((SIDE,)), dma((SIDE,)),
        ],
        compiler_params=pltpu.CompilerParams(
            collective_id=2, has_side_effects=True, vmem_limit_bytes=VMEM_LIMIT
        ),
        name="layers",
    )(h, w_first, w_mine, mask, gslot, grads)


def shards(
    patches,
    image_units,
    v_gain,
    v_qkv,
    v_out,
    merge_gain,
    w_merge,
    routes,
    text,
    seq_lengths,
    lang_gain,
    w_qkv,
    wo_t,
    row_grads,
):
    section = lax.axis_index("section")
    x = lax.axis_index("x")
    y = lax.axis_index("y")

    part = w_merge.shape[0] // 2
    wm = lax.all_gather(
        lax.dynamic_slice_in_dim(w_merge, section * part, part, 0), "y", axis=0, tiled=False
    )
    gain = lax.dynamic_slice_in_dim(lang_gain[0], (y * SIDE + x) * FB, FB, 0)
    scaled = (w_qkv[0].astype(F32) * gain[:, None]).astype(BF)
    w_mine = jnp.concatenate([scaled, wo_t[0]], axis=1)
    swapped = lax.ppermute(scaled[FB // 2 :], "section", [(0, 1)])
    w_half = jnp.where(section == 0, scaled[: FB // 2], swapped)
    w_first = lax.all_gather(w_half, "y", axis=0, tiled=False)

    z = lax.axis_index("mp")
    place = jnp.arange(1024, dtype=jnp.int32)
    repeated = jnp.broadcast_to(routes[:, 0][None, :], (64, 16)).reshape(1024)
    placed = jnp.where(place // 16 == (y * SIDE + x) * SIDE + z, repeated, 0)[None, :]

    merged = vision_rows(patches, image_units[0], v_gain, v_qkv, v_out, merge_gain)
    pieces = merged.reshape(16, MERGE, SIDE, 320).transpose(2, 0, 1, 3).reshape(SIDE, 16, VD)
    seq = segment_of(seq_lengths[0], TOK)
    at = jnp.arange(TOK, dtype=jnp.int32)
    mask = ((seq[:, None] == seq[None, :]) & (at[:, None] >= at[None, :])).astype(F32)

    hidden, gslot = merge_call(pieces, wm, text, placed)
    return layers_call(hidden, w_first, w_mine, mask, gslot, row_grads)


def solution(mesh):
    grid = jax.sharding.Mesh(
        mesh.devices.reshape(2, SIDE, SIDE, SIDE), ("section", "y", "x", "mp")
    )
    every = ("section", "y", "x", "mp")
    home = P(("section", "y", "x"), "mp")
    in_specs = (
        P(every, None),
        P(every, None),
        P(),
        P(),
        P(),
        P(),
        P(("y", "x"), "mp"),
        P(every, None),
        home,
        P(("section", "y", "x"), None),
        P("section", None),
        P("section", ("y", "x"), "mp"),
        P("section", ("y", "x"), "mp"),
        home,
    )
    out_specs = (home, P(every, None))
    return jax.shard_map(shards, mesh=grid, in_specs=in_specs, out_specs=out_specs, check_vma=False)
```

```python
import functools
import math

import jax
import jax.numpy as jnp
from jax import lax
from jax.experimental import pallas as pl
from jax.experimental.pallas import tpu as pltpu
from jax.sharding import PartitionSpec as P

QH = 32
KVH = 4
HD = 128
VD = 1280
VH = 16
VHD = 80
SIDE = 4
TOK = 128
HALF = TOK // 2
STEPS = (1, 3, 2)
FB = 512
HEADS = QH // KVH
QW = HEADS * HD
PW = QW + 2 * HD
PT = PW + HD
D = 8192
PATCH = 64
UNITS = 16
PIECE = VD // SIDE
PADDED = 384
COUNT = 1024
TILE = 256
SLOTS = 6
EPSILON = 1e-06
VMEM_LIMIT = 62 * 1024 * 1024
BF = jnp.bfloat16
F32 = jnp.float32
MESH = pl.DeviceIdType.MESH


def layer_norm(values, norm_gain):
    centre = jnp.mean(values, axis=-1, keepdims=True)
    centred = values - centre
    variance = jnp.mean(centred * centred, axis=-1, keepdims=True)
    return centred * lax.rsqrt(variance + EPSILON) * norm_gain


def remote(src, dst, send_sem, recv_sem, where):
    return pltpu.make_async_remote_copy(
        src_ref=src, dst_ref=dst, send_sem=send_sem, recv_sem=recv_sem,
        device_id=where, device_id_type=MESH,
    )


def push(src, dst, send_sem, recv_sem, where):
    copy = remote(src, dst, send_sem, recv_sem, where)
    copy.start()
    return copy


def greet(partners):
    barrier = pltpu.get_barrier_semaphore()
    for where in partners:
        pl.semaphore_signal(barrier, inc=1, device_id=where, device_id_type=MESH)
    pl.semaphore_wait(barrier, len(partners))


def along(index, step):
    return lax.rem(index + step, SIDE)


def behind(index, step):
    return lax.rem(index + SIDE - step, SIDE)


def one_hot(condition):
    return jnp.where(condition, 1.0, 0.0).astype(BF)


def iota(shape, dimension):
    return lax.broadcasted_iota(jnp.int32, shape, dimension)


def segments(index, lengths):
    first = lengths[0, 0]
    second = first + lengths[0, 1]
    return jnp.where(index >= first, 1, 0) + jnp.where(index >= second, 1, 0)


def whole_kernel(
    patches, units, v_gain, v_qkv, v_out, merge_gain, w_merge, routes, text, lengths,
    lang_gain, w_qkv, wo_t, grads,
    out, mg,
    ring, wraw, wmv, w, v_proj, v_scores, v_weights, v_att, v_hidden, pieces, xbuf, part, msend, mrecv, ybuf, tbuf, pick,
    placed, rt, ry, tri, line, gslot,
    zbuf, acc, squares, kv, psend, rbuf, abuf, osend, orec, orel, obuf,
    gbuf, gsend, grec, gz, mz,
    v_sem, l_sem, s_w, r_w, s_rt, r_rt, s_ry, r_ry, s_pl, r_pl, s_mx, r_mx, s_my, r_my, s_t, r_t,
    s_z, r_z, s_x, r_x, s_a, r_a, s_o, r_o, s_e, r_e,
    s_g, r_g, s_gy, r_gy, s_gz, r_gz,
):
    section = lax.axis_index("section")
    x = lax.axis_index("x")
    y = lax.axis_index("y")
    z = lax.axis_index("mp")
    twin = {"section": 1 - section}
    rows = SIDE * HALF
    width = grads.shape[1]
    half = wmv.shape[2]
    plane = [(dx, dz) for dx in range(SIDE) for dz in range(SIDE) if dx or dz]
    left = slice(0, rows // 2)
    right = slice(rows // 2, rows)

    own_merge = pltpu.make_async_copy(
        w_merge.at[pl.ds(pl.multiple_of(section * half, half), half), :],
        wmv.at[y, section], l_sem.at[0],
    )
    own_merge.start()
    v_tiles = [
        pltpu.make_async_copy(
            (v_qkv if tile < 15 else v_out).at[:, pl.ds((tile if tile < 15 else tile - 15) * TILE, TILE)],
            ring.at[tile % SLOTS], v_sem.at[tile % SLOTS],
        )
        for tile in range(20)
    ]
    for tile in range(SLOTS):
        v_tiles[tile].start()
    raw_load = pltpu.make_async_copy(w_qkv.at[0], wraw, l_sem.at[1])
    raw_load.start()
    own_out = pltpu.make_async_copy(
        wo_t.at[0], w.at[section, y, :, pl.ds(PW, QW)], l_sem.at[2]
    )
    own_out.start()
    own_text = pltpu.make_async_copy(
        text.at[:, pl.ds(pl.multiple_of(x * FB, FB), FB)], tbuf.at[x], l_sem.at[3]
    )
    own_text.start()
    own_grads = pltpu.make_async_copy(grads, gbuf.at[x], l_sem.at[4])
    own_grads.start()

    lane = iota((1, COUNT), 1)
    base = ((y * SIDE + x) * SIDE + z) * UNITS
    row = jnp.zeros((1, COUNT), jnp.int32)
    for unit in range(UNITS):
        row = jnp.where(lane == base + unit, routes[unit, 0], row)
    placed[...] = row
    rt[x * SIDE + z] = row

    greet(
        [{"x": along(x, dx), "mp": along(z, dz)} for dx, dz in plane]
        + [{"y": along(y, dy)} for dy in STEPS]
        + [twin]
    )

    def shared(number, block, low, high):
        def own_copy(dy):
            return remote(
                block(y), block(y), s_w.at[number, dy], r_w.at[number, dy], {"y": along(y, dy)}
            )

        def up_copy():
            ref = low(behind(y, 1))
            return remote(ref, ref, s_w.at[number, 0], r_w.at[number, 0], {"y": along(y, 1)})

        def down_copy():
            ref = high(along(y, 1))
            return remote(ref, ref, s_w.at[number, 2], r_w.at[number, 2], {"y": along(y, 3)})

        def twin_copy(source):
            return remote(
                block(source), block(source), s_w.at[number, SIDE + source],
                r_w.at[number, SIDE + source], twin,
            )

        def begin():
            own_copy(1).start()
            own_copy(3).start()

        def middle():
            own_copy(1).wait()
            up_copy().start()
            own_copy(3).wait()
            down_copy().start()

        def end():
            up_copy().wait()
            down_copy().wait()
            for source in range(SIDE):
                twin_copy(source).start()

        def taken():
            for source in range(SIDE):
                twin_copy(source).wait_recv()

        def given():
            for source in range(SIDE):
                twin_copy(source).wait_send()

        return begin, middle, end, taken, given

    mid = wmv.shape[3] // 2
    merge_w = shared(
        0,
        lambda ys: wmv.at[ys, section],
        lambda ys: wmv.at[ys, section, :, pl.ds(0, mid)],
        lambda ys: wmv.at[ys, section, :, pl.ds(mid, mid)],
    )

    def layer_shard(number, layer, first, amount):
        cols = pl.ds(first, amount)
        return shared(
            number,
            lambda ys: w.at[layer, ys, :, cols],
            lambda ys: w.at[layer, ys, pl.ds(0, FB // 2), cols],
            lambda ys: w.at[layer, ys, pl.ds(FB // 2, FB // 2), cols],
        )

    qkv_w = layer_shard(1, 0, 0, PW)
    out_w = layer_shard(2, 0, PW, QW)
    last_w = layer_shard(3, 1, 0, PW + QW)

    def only(at, *actions):
        @pl.when(section == at)
        def _():
            for action in actions:
                action()

    own_merge.wait()
    merge_w[0]()
    route_copies = [
        push(
            placed, rt.at[x * SIDE + z], s_rt.at[dx * SIDE + dz], r_rt.at[dx * SIDE + dz],
            {"x": along(x, dx), "mp": along(z, dz)},
        )
        for dx, dz in plane
    ]
    text_copies = []
    for dx in STEPS:
        xt = along(x, dx)
        text_copies.append(
            push(
                text.at[:, pl.ds(pl.multiple_of(xt * FB, FB), FB)], tbuf.at[x],
                s_t.at[dx], r_t.at[dx], {"x": xt},
            )
        )
    grad_copies = [
        push(grads, gbuf.at[x], s_g.at[dx], r_g.at[dx], {"x": along(x, dx)}) for dx in STEPS
    ]

    order = iota((PATCH, PATCH), 0)
    swap = one_hot(iota((PATCH, PATCH), 1) == (order & 15) * SIDE + (order >> 4))
    patch = jnp.dot(swap, patches[...], preferred_element_type=F32)
    normed = layer_norm(patch, v_gain[...]).astype(BF)
    for tile in range(15):
        v_tiles[tile].wait()
        v_proj[:, tile * TILE : (tile + 1) * TILE] = jnp.dot(
            normed, ring[tile % SLOTS], preferred_element_type=F32
        ).astype(BF)
        if tile + SLOTS < 20:
            v_tiles[tile + SLOTS].start()

    windows = []
    for head in range(VH):
        start = min(head * VHD // 128 * 128, VD - 256)
        lanes = iota((PATCH, 256), 1) + start
        windows.append((start, (lanes >= head * VHD) & (lanes < (head + 1) * VHD)))
    for head, (start, inside) in enumerate(windows):
        query = v_proj[:, start : start + 256].astype(F32)
        query = jnp.where(inside, query, 0.0).astype(BF)
        key = v_proj[:, VD + start : VD + start + 256]
        v_scores[head * PATCH : (head + 1) * PATCH, :] = lax.dot_general(
            query, key, (((1,), (1,)), ((), ())), preferred_element_type=F32
        )
    image_q = segments(iota((VH * PATCH, PATCH), 0) & 15, units)
    image_k = segments(iota((VH * PATCH, PATCH), 1) & 15, units)
    scores = jnp.where(image_q == image_k, v_scores[...] / math.sqrt(VHD), -1e30)
    top = jnp.max(scores, axis=1, keepdims=True)
    weights = jnp.exp(scores - top)
    v_weights[...] = (weights / jnp.sum(weights, axis=1, keepdims=True)).astype(BF)
    v_att[...] = jnp.zeros((PATCH, VD), F32)
    for head, (start, inside) in enumerate(windows):
        mixed = jnp.dot(
            v_weights[head * PATCH : (head + 1) * PATCH, :],
            v_proj[:, 2 * VD + start : 2 * VD + start + 256],
            preferred_element_type=F32,
        )
        v_att[:, start : start + 256] += jnp.where(inside, mixed, 0.0)
    attended = v_att[...].astype(BF)
    for tile in range(5):
        v_tiles[15 + tile].wait()
        cols = slice(tile * TILE, (tile + 1) * TILE)
        v_hidden[:, cols] = (
            patch[:, cols]
            + jnp.dot(attended, ring[(15 + tile) % SLOTS], preferred_element_type=F32)
        ).astype(BF).astype(F32)
    merged = layer_norm(v_hidden[...], merge_gain[...])
    for block in range(SIDE):
        pieces[block, :, :, :PIECE] = merged[:, block * PIECE : (block + 1) * PIECE].astype(BF).reshape(
            SIDE, UNITS, PIECE
        )
        pieces[block, :, :, PIECE:] = jnp.zeros((SIDE, UNITS, PADDED - PIECE), BF)
    plane_copies = []
    for dx, dz in plane:
        xt = along(x, dx)
        plane_copies.append(
            push(
                pieces.at[xt], xbuf.at[x * SIDE + z],
                s_pl.at[dx * SIDE + dz], r_pl.at[dx * SIDE + dz],
                {"x": xt, "mp": along(z, dz)},
            )
        )
    xbuf[x * SIDE + z] = pieces[x]

    merge_w[1]()
    raw_load.wait()
    shard = y * SIDE + x
    gain = lang_gain[:, pl.ds(pl.multiple_of(shard * FB, FB), FB)]
    gain = jnp.transpose(jnp.broadcast_to(gain, (128, FB)))
    for tile in range(PW // 128):
        cols = slice(tile * 128, (tile + 1) * 128)
        w[section, y, :, cols] = (wraw[:, cols].astype(F32) * gain).astype(BF)
    own_out.wait()
    only(0, qkv_w[0])

    for block in range(SIDE):
        before = iota((256, COUNT), 0) + block * 256
        tri[block * 256 : (block + 1) * 256, :] = one_hot(before < iota((256, COUNT), 1))
    for copy in route_copies:
        copy.wait()
    known = rt[0]
    for source in range(1, SIDE * SIDE):
        known = known + rt[source]
    ry[y] = known
    ry_copies = [
        push(ry.at[y], ry.at[y], s_ry.at[dy], r_ry.at[dy], {"y": along(y, dy)})
        for dy in STEPS
    ]
    for copy in plane_copies:
        copy.wait()
    merge_w[2]()
    merge_w[3]()

    def product(dx):
        cols = pl.ds(pl.multiple_of(along(x, dx) * FB, FB), FB)
        total = None
        for patch_at in range(SIDE):
            piece = xbuf[:, patch_at].reshape(SIDE * SIDE * UNITS, PADDED)[:, :PIECE]
            weights = wmv[patch_at, :, :, cols].reshape(PIECE, FB)
            term = jnp.dot(piece, weights, preferred_element_type=F32)
            total = term if total is None else total + term
        return total

    m_copies = []
    for dx in STEPS:
        msend[dx] = product(dx).astype(BF)
        m_copies.append(
            push(msend.at[dx], mrecv.at[dx], s_mx.at[dx], r_mx.at[dx], {"x": along(x, dx)})
        )
    part[...] = product(0)

    for copy in ry_copies:
        copy.wait()
    target = ry[0] + ry[1] + ry[2] + ry[3]
    named = jnp.where(iota((16, COUNT), 0) == target, 1.0, 0.0)
    earlier = jnp.dot(named.astype(BF), tri[...], preferred_element_type=F32)
    position = jnp.sum(named * earlier, axis=0, keepdims=True).astype(jnp.int32)
    slots = (target - y * SIDE) * TOK + position
    for block in range(SIDE):
        wanted = iota((TOK, COUNT), 0) + block * TOK
        pick[block * TOK : (block + 1) * TOK, :] = one_hot(wanted == slots)
    line[...] = jnp.where((target >> 2) == y, (target & 3) * TOK + position + 1, 0)
    down = iota((256, COUNT), 0)
    chosen_rows = one_hot(iota((256, COUNT), 1) == (down >> 6) * 256 + x * 64 + (down & 63))

    def upright(values):
        wide = jnp.broadcast_to(values.astype(F32), (128, COUNT)).astype(BF)
        return lax.dot_general(
            chosen_rows, wide, (((1,), (1,)), ((), ())), preferred_element_type=F32
        )

    slot_line = line[...]
    gslot[...] = (
        16.0 * upright(slot_line >> 4) + upright(slot_line & 15)
    ).astype(jnp.int32) - 1

    only(0, qkv_w[1], out_w[0])
    for copy in m_copies:
        copy.wait()
    total = part[...]
    for dx in STEPS:
        total = total + mrecv[dx].astype(F32)
    ybuf[y] = total.astype(BF)
    y_copies = [
        push(ybuf.at[y], ybuf.at[y], s_my.at[dy], r_my.at[dy], {"y": along(y, dy)})
        for dy in STEPS
    ]
    present = jnp.dot(pick[...], jnp.ones((COUNT, 128), BF), preferred_element_type=F32)
    own_text.wait()
    for copy in text_copies:
        copy.wait()
    for copy in y_copies:
        copy.wait()
    picked = jnp.dot(
        pick[...], ybuf[...].reshape(COUNT, FB), preferred_element_type=F32
    ).astype(BF)
    for group in range(SIDE):
        for part_of in range(2):
            span = slice(group * TOK + part_of * HALF, group * TOK + (part_of + 1) * HALF)
            to = slice(group * HALF, (group + 1) * HALF)
            inside = slice(part_of * HALF, (part_of + 1) * HALF)
            for tile in range(FB // 128):
                cols = slice(tile * 128, (tile + 1) * 128)
                zbuf[part_of, z, to, cols] = jnp.where(
                    present[span, :] > 0.5, picked[span, cols], tbuf[group, inside, cols]
                )

    z_copies, f_copies, x_copies, a_copies, o_copies, e_copies = {}, {}, {}, {}, {}, []

    def spread(layer, part):
        z_copies[layer, part] = {
            dz: push(
                zbuf.at[part, z], zbuf.at[part, z],
                s_z.at[layer, part, dz], r_z.at[layer, part, dz], {"mp": along(z, dz)},
            )
            for dz in (1, 3)
        }

    def times(layer, part, dz):
        zs = behind(z, dz)
        wide = zbuf[part, zs].astype(F32)
        squared = jnp.sum(wide * wide, axis=1, keepdims=True)
        if dz:
            squares[part] += jnp.broadcast_to(squared, (rows, HD))
        else:
            squares[part] = jnp.broadcast_to(squared, (rows, HD))

        @pl.loop(0, PW // 256)
        def _(tile):
            cols = pl.ds(pl.multiple_of(tile * 256, 256), 256)
            product = jnp.dot(
                zbuf[part, zs], w[layer, zs, :, cols], preferred_element_type=F32
            )
            if dz:
                acc[part, :, cols] += product
            else:
                acc[part, :, cols] = product

    def passed(layer, part):
        copies = z_copies[layer, part]
        copies[1].wait()
        zs = behind(z, 1)
        f_copies[layer, part] = [
            push(
                zbuf.at[part, zs, left], zbuf.at[part, zs, left],
                s_z.at[layer, part, 0], r_z.at[layer, part, 0], {"mp": along(z, 1)},
            )
        ]
        copies[3].wait()
        zs = along(z, 1)
        f_copies[layer, part].append(
            push(
                zbuf.at[part, zs, right], zbuf.at[part, zs, right],
                s_z.at[layer, part, 2], r_z.at[layer, part, 2], {"mp": along(z, 3)},
            )
        )

    def own_part(layer, part):
        times(layer, part, 0)

    def project(layer, part):
        times(layer, part, 1)
        times(layer, part, 3)
        for copy in f_copies[layer, part]:
            copy.wait()
        times(layer, part, 2)
        lane = lax.broadcasted_iota(jnp.int32, (HALF, HD), 1)
        copies = []
        for dx in STEPS:
            xt = along(x, dx)
            span = pl.ds(pl.multiple_of(xt * HALF, HALF), HALF)
            psend[part, dx, :, :PW] = acc[part, span, :].astype(BF)
            sq = squares[part, span, :]
            high = sq.astype(BF)
            low = (sq - high.astype(F32)).astype(BF)
            psend[part, dx, :, PW:] = jnp.where(lane < 64, high, low)
            copies.append(
                push(
                    psend.at[part, dx], rbuf.at[part, dx],
                    s_x.at[layer, part, dx], r_x.at[layer, part, dx], {"x": xt},
                )
            )
        x_copies[layer, part] = copies

    def attend(layer, part):
        own = pl.ds(pl.multiple_of(x * HALF, HALF), HALF)
        total = acc[part, own, :]
        sq = squares[part, own, :][:, :1]
        for copy in x_copies[layer, part]:
            copy.wait()
        for dx in STEPS:
            total = total + rbuf[part, dx, :, :PW].astype(F32)
            tail = rbuf[part, dx, :, PW:].astype(F32)
            sq = sq + tail[:, :1] + tail[:, 64:65]
        projected = (total * lax.rsqrt(sq / D + EPSILON)).astype(BF)
        kv[part * HALF : (part + 1) * HALF, :] = projected[:, QW:]
        seen = (part + 1) * HALF
        keys = kv[:seen, :HD]
        values = kv[:seen, HD:]
        queries = jnp.concatenate(
            [projected[:, head * HD : (head + 1) * HD] for head in range(HEADS)], axis=0
        )
        at = iota((HALF, seen), 0) + part * HALF
        key_at = iota((HALF, seen), 1)
        allowed = jnp.where(
            (segments(at, lengths) == segments(key_at, lengths)) & (at >= key_at), 1.0, 0.0
        )
        allowed = jnp.concatenate([allowed] * HEADS, axis=0) > 0.5
        scores = lax.dot_general(
            queries, keys, (((1,), (1,)), ((), ())), preferred_element_type=F32
        ) * (1.0 / math.sqrt(HD))
        scores = jnp.where(allowed, scores, -1e30)
        top = jnp.max(scores, axis=1, keepdims=True)
        weights = jnp.exp(scores - top)
        weights = (weights / jnp.sum(weights, axis=1, keepdims=True)).astype(BF)
        mixed = jnp.dot(weights, values, preferred_element_type=F32).astype(BF)
        for head in range(HEADS):
            abuf[part, x, :, head * HD : (head + 1) * HD] = mixed[
                head * HALF : (head + 1) * HALF, :
            ]
        a_copies[layer, part] = [
            push(
                abuf.at[part, x], abuf.at[part, x],
                s_a.at[layer, part, dx], r_a.at[layer, part, dx], {"x": along(x, dx)},
            )
            for dx in STEPS
        ]

    def output(layer, part):
        for copy in a_copies[layer, part]:
            copy.wait()
        copies = {}

        def send(name, src, dst, dz):
            copies[name] = push(
                src, dst, s_o.at[layer, part, name], r_o.at[layer, part, name],
                {"mp": along(z, dz)},
            )

        for dz in (2, 1, 3, 0):
            zt = along(z, dz)

            @pl.loop(0, FB // 256)
            def _(tile):
                cols = pl.ds(pl.multiple_of(tile * 256, 256), 256)
                osend[part, dz, :, cols] = lax.dot_general(
                    abuf[part].reshape(rows, QW), w[layer, zt, cols, PW:],
                    (((1,), (1,)), ((), ())), preferred_element_type=F32,
                ).astype(BF)

            if dz == 2:
                send(0, osend.at[part, 2, left], orel.at[part, 0], 1)
                send(1, osend.at[part, 2, right], orel.at[part, 1], 3)
            elif dz == 1:
                send(2, osend.at[part, 1, right], orec.at[part, 0, right], 1)
            elif dz == 3:
                send(3, osend.at[part, 3, left], orec.at[part, 1, left], 3)
        o_copies[layer, part] = copies, send

    def relay(layer, part):
        copies, send = o_copies[layer, part]
        copies[0].wait()
        osend[part, 1, left] = (
            osend[part, 1, left].astype(F32) + orel[part, 0].astype(F32)
        ).astype(BF)
        send(4, osend.at[part, 1, left], orec.at[part, 0, left], 1)
        copies[1].wait()
        osend[part, 3, right] = (
            osend[part, 3, right].astype(F32) + orel[part, 1].astype(F32)
        ).astype(BF)
        send(5, osend.at[part, 3, right], orec.at[part, 1, right], 3)

    def finish(layer, part):
        update = osend[part, 0].astype(F32)
        copies, _ = o_copies[layer, part]
        for name in (2, 3, 4, 5):
            copies[name].wait()
        for side in range(2):
            update = update + orec[part, side].astype(F32)
        fresh = (zbuf[part, z].astype(F32) + update).astype(BF)
        if layer == 0:
            zbuf[part, z] = fresh
            return
        osend[part, 0] = fresh
        for dx in STEPS:
            xt = along(x, dx)
            e_copies.append(
                push(
                    osend.at[part, 0, pl.ds(pl.multiple_of(xt * HALF, HALF), HALF), :],
                    obuf.at[x, part],
                    s_e.at[part, dx], r_e.at[part, dx], {"x": xt},
                )
            )
        obuf[x, part] = osend[part, 0, pl.ds(pl.multiple_of(x * HALF, HALF), HALF), :
        ]

    spread(0, 0)
    g_copies, gz_copies = [], []

    def ready_qkv(layer, part):
        only(0, qkv_w[2], out_w[1])
        only(1, last_w[0], qkv_w[3])

    def ready_out(layer, part):
        only(0, out_w[2])
        only(1, out_w[3])

    def pass_last(layer, part):
        only(1, last_w[1])

    def ready_last(layer, part):
        only(1, last_w[2])
        only(0, last_w[3])

    def choose(layer, part):
        own_grads.wait()
        for copy in grad_copies:
            copy.wait()
        for dy in (1, 3, 2, 0):
            yt = along(y, dy)
            wanted = gslot[pl.ds(pl.multiple_of(yt * 64, 64), 64), :1]
            chosen = one_hot(iota((64, SIDE * TOK), 1) == wanted)
            gsend[dy] = jnp.dot(
                chosen, gbuf[...].reshape(SIDE * TOK, width), preferred_element_type=F32
            ).astype(BF)
            if dy:
                g_copies.append(
                    push(gsend.at[dy], grec.at[dy], s_gy.at[dy], r_gy.at[dy], {"y": yt})
                )

    def hand(layer, part):
        for copy in g_copies:
            copy.wait()
        found = gsend[0].astype(F32)
        for dy in STEPS:
            found = found + grec[dy].astype(F32)
        gz[...] = found.astype(BF).reshape(SIDE, UNITS, width)
        for dz in STEPS:
            zt = along(z, dz)
            gz_copies.append(
                push(gz.at[zt], mz.at[z], s_gz.at[dz], r_gz.at[dz], {"mp": zt})
            )
        mz[z] = gz[z]

    for stage, layer, part_at in (
        (ready_qkv, 0, 0),
        (own_part, 0, 0),
        (passed, 0, 0),
        (spread, 0, 1),
        (project, 0, 0),
        (own_part, 0, 1),
        (attend, 0, 0),
        (passed, 0, 1),
        (project, 0, 1),
        (ready_out, 0, 0),
        (output, 0, 0),
        (attend, 0, 1),
        (relay, 0, 0),
        (output, 0, 1),
        (pass_last, 0, 0),
        (finish, 0, 0),
        (spread, 1, 0),
        (relay, 0, 1),
        (choose, 1, 0),
        (ready_last, 1, 0),
        (own_part, 1, 0),
        (finish, 0, 1),
        (passed, 1, 0),
        (spread, 1, 1),
        (project, 1, 0),
        (own_part, 1, 1),
        (attend, 1, 0),
        (passed, 1, 1),
        (project, 1, 1),
        (output, 1, 0),
        (attend, 1, 1),
        (relay, 1, 0),
        (output, 1, 1),
        (hand, 1, 0),
        (finish, 1, 0),
        (relay, 1, 1),
        (finish, 1, 1),
    ):
        stage(layer, part_at)

    for copy in gz_copies:
        copy.wait()
    for block in range(SIDE):
        mg[:, block * width : (block + 1) * width] = mz[block]
    for copy in e_copies:
        copy.wait()
    for block in range(SIDE):
        for part_of in range(2):
            out[part_of * HALF : (part_of + 1) * HALF, block * FB : (block + 1) * FB] = obuf[
                block, part_of
            ]
    merge_w[4]()
    only(0, qkv_w[4], out_w[4])
    only(1, last_w[4])


def shards(*arrays):
    vmem = pl.BlockSpec(memory_space=pltpu.VMEM)
    smem = pl.BlockSpec(memory_space=pltpu.SMEM)
    hbm = pl.BlockSpec(memory_space=pl.ANY)
    dma = pltpu.SemaphoreType.DMA
    rows = SIDE * HALF
    width = arrays[13].shape[1]
    half = arrays[6].shape[0] // 2
    stage = dma((2, 2, SIDE))
    four, plane = dma((SIDE,)), dma((SIDE * SIDE,))
    call = pl.pallas_call(
        whole_kernel,
        out_shape=(
            jax.ShapeDtypeStruct((TOK, SIDE * FB), BF),
            jax.ShapeDtypeStruct((UNITS, SIDE * width), BF),
        ),
        in_specs=[vmem, smem, vmem, hbm, hbm, vmem, hbm, smem, hbm, smem, vmem, hbm, hbm, hbm],
        out_specs=(vmem, vmem),
        scratch_shapes=[
            pltpu.VMEM((SLOTS, VD, TILE), BF),
            pltpu.VMEM((FB, PW), BF),
            pltpu.VMEM((SIDE, 2, half, SIDE * FB), BF),
            pltpu.VMEM((2, SIDE, FB, PW + QW), BF),
            pltpu.VMEM((PATCH, 3 * VD), BF),
            pltpu.VMEM((VH * PATCH, PATCH), F32),
            pltpu.VMEM((VH * PATCH, PATCH), BF),
            pltpu.VMEM((PATCH, VD), F32),
            pltpu.VMEM((PATCH, VD), F32),
            pltpu.VMEM((SIDE, SIDE, UNITS, PADDED), BF),
            pltpu.VMEM((SIDE * SIDE, SIDE, UNITS, PADDED), BF),
            pltpu.VMEM((256, FB), F32),
            pltpu.VMEM((SIDE, 256, FB), BF),
            pltpu.VMEM((SIDE, 256, FB), BF),
            pltpu.VMEM((SIDE, 256, FB), BF),
            pltpu.VMEM((SIDE, TOK, FB), BF),
            pltpu.VMEM((SIDE * TOK, COUNT), BF),
            pltpu.VMEM((1, COUNT), jnp.int32),
            pltpu.VMEM((SIDE * SIDE, 1, COUNT), jnp.int32),
            pltpu.VMEM((SIDE, 1, COUNT), jnp.int32),
            pltpu.VMEM((COUNT, COUNT), BF),
            pltpu.VMEM((1, COUNT), jnp.int32),
            pltpu.VMEM((256, 128), jnp.int32),
            pltpu.VMEM((2, SIDE, rows, FB), BF),
            pltpu.VMEM((2, rows, PW), F32),
            pltpu.VMEM((2, rows, HD), F32),
            pltpu.VMEM((TOK, 2 * HD), BF),
            pltpu.VMEM((2, SIDE, HALF, PT), BF),
            pltpu.VMEM((2, SIDE, HALF, PT), BF),
            pltpu.VMEM((2, SIDE, HALF, QW), BF),
            pltpu.VMEM((2, SIDE, rows, FB), BF),
            pltpu.VMEM((2, 2, rows, FB), BF),
            pltpu.VMEM((2, 2, rows // 2, FB), BF),
            pltpu.VMEM((SIDE, 2, HALF, FB), BF),
            pltpu.VMEM((SIDE, TOK, width), BF),
            pltpu.VMEM((SIDE, 64, width), BF),
            pltpu.VMEM((SIDE, 64, width), BF),
            pltpu.VMEM((SIDE, UNITS, width), BF),
            pltpu.VMEM((SIDE, UNITS, width), BF),
            dma((SLOTS,)), dma((5,)), dma((4, 8)), dma((4, 8)),
            plane, plane, four, four, plane, plane, four, four, four, four, four, four,
            stage, stage, stage, stage, stage, stage, dma((2, 2, 6)), dma((2, 2, 6)),
            dma((2, SIDE)), dma((2, SIDE)),
            four, four, four, four, four, four,
        ],
        compiler_params=pltpu.CompilerParams(
            collective_id=1, has_side_effects=True, vmem_limit_bytes=VMEM_LIMIT
        ),
        name="whole",
    )
    arrays = list(arrays)
    arrays[2] = arrays[2][None, :]
    arrays[5] = arrays[5][None, :]
    return call(*arrays)


def solution(mesh):
    grid = jax.sharding.Mesh(
        mesh.devices.reshape(2, SIDE, SIDE, SIDE), ("section", "y", "x", "mp")
    )
    every = ("section", "y", "x", "mp")
    home = P(("section", "y", "x"), "mp")
    in_specs = (
        P(every, None),
        P(every, None),
        P(),
        P(),
        P(),
        P(),
        P(("y", "x"), "mp"),
        P(every, None),
        home,
        P(("section", "y", "x"), None),
        P("section", None),
        P("section", ("y", "x"), "mp"),
        P("section", ("y", "x"), "mp"),
        home,
    )
    out_specs = (home, P(every, None))
    return jax.shard_map(shards, mesh=grid, in_specs=in_specs, out_specs=out_specs, check_vma=False)
```

```python
import functools
import math

import jax
import jax.numpy as jnp
from jax import lax
from jax.experimental import pallas as pl
from jax.experimental.pallas import tpu as pltpu
from jax.sharding import PartitionSpec as P

QH = 32
KVH = 4
HD = 128
VD = 1280
VH = 16
VHD = 80
SIDE = 4
TOK = 128
HALF = TOK // 2
STEPS = (1, 3, 2)
FB = 512
HEADS = QH // KVH
QW = HEADS * HD
PW = QW + 2 * HD
PT = PW + HD
D = 8192
PATCH = 64
UNITS = 16
PIECE = VD // SIDE
PADDED = 384
COUNT = 1024
TILE = 256
SLOTS = 6
EPSILON = 1e-06
VMEM_LIMIT = 62 * 1024 * 1024
BF = jnp.bfloat16
F32 = jnp.float32
MESH = pl.DeviceIdType.MESH


def layer_norm(values, norm_gain):
    centre = jnp.mean(values, axis=-1, keepdims=True)
    centred = values - centre
    variance = jnp.mean(centred * centred, axis=-1, keepdims=True)
    return centred * lax.rsqrt(variance + EPSILON) * norm_gain


def remote(src, dst, send_sem, recv_sem, where):
    return pltpu.make_async_remote_copy(
        src_ref=src, dst_ref=dst, send_sem=send_sem, recv_sem=recv_sem,
        device_id=where, device_id_type=MESH,
    )


def push(src, dst, send_sem, recv_sem, where):
    copy = remote(src, dst, send_sem, recv_sem, where)
    copy.start()
    return copy


def greet(partners):
    barrier = pltpu.get_barrier_semaphore()
    for where in partners:
        pl.semaphore_signal(barrier, inc=1, device_id=where, device_id_type=MESH)
    pl.semaphore_wait(barrier, len(partners))


def along(index, step):
    return lax.rem(index + step, SIDE)


def behind(index, step):
    return lax.rem(index + SIDE - step, SIDE)


def one_hot(condition):
    return jnp.where(condition, 1.0, 0.0).astype(BF)


def iota(shape, dimension):
    return lax.broadcasted_iota(jnp.int32, shape, dimension)


def segments(index, lengths):
    first = lengths[0, 0]
    second = first + lengths[0, 1]
    return jnp.where(index >= first, 1, 0) + jnp.where(index >= second, 1, 0)


def whole_kernel(
    patches, units, v_gain, v_qkv, v_out, merge_gain, w_merge, routes, text, lengths,
    lang_gain, w_qkv, wo_t, grads,
    out, mg,
    ring, wraw, wmv, w, v_proj, v_scores, v_weights, v_att, v_hidden, pieces, xbuf, part, msend, mrecv, ybuf, tbuf, pick,
    placed, rt, ry, tri, line, gslot,
    zbuf, acc, squares, kv, psend, rbuf, abuf, osend, orec, orel, obuf,
    gbuf, gsend, grec, gz, mz,
    v_sem, l_sem, s_w, r_w, s_rt, r_rt, s_ry, r_ry, s_pl, r_pl, s_mx, r_mx, s_my, r_my, s_t, r_t,
    s_z, r_z, s_x, r_x, s_a, r_a, s_o, r_o, s_e, r_e,
    s_g, r_g, s_gy, r_gy, s_gz, r_gz,
):
    section = lax.axis_index("section")
    x = lax.axis_index("x")
    y = lax.axis_index("y")
    z = lax.axis_index("mp")
    twin = {"section": 1 - section}
    rows = SIDE * HALF
    width = grads.shape[1]
    half = wmv.shape[2]
    plane = [(dx, dz) for dx in range(SIDE) for dz in range(SIDE) if dx or dz]
    left = slice(0, rows // 2)
    right = slice(rows // 2, rows)

    own_merge = pltpu.make_async_copy(
        w_merge.at[pl.ds(pl.multiple_of(section * half, half), half), :],
        wmv.at[y, section], l_sem.at[0],
    )
    own_merge.start()
    v_tiles = [
        pltpu.make_async_copy(
            (v_qkv if tile < 15 else v_out).at[:, pl.ds((tile if tile < 15 else tile - 15) * TILE, TILE)],
            ring.at[tile % SLOTS], v_sem.at[tile % SLOTS],
        )
        for tile in range(20)
    ]
    for tile in range(SLOTS):
        v_tiles[tile].start()
    raw_load = pltpu.make_async_copy(w_qkv.at[0], wraw, l_sem.at[1])
    raw_load.start()
    own_out = pltpu.make_async_copy(
        wo_t.at[0], w.at[section, y, :, pl.ds(PW, QW)], l_sem.at[2]
    )
    own_out.start()
    own_text = pltpu.make_async_copy(
        text.at[:, pl.ds(pl.multiple_of(x * FB, FB), FB)], tbuf.at[x], l_sem.at[3]
    )
    own_text.start()
    own_grads = pltpu.make_async_copy(grads, gbuf.at[x], l_sem.at[4])
    own_grads.start()

    lane = iota((1, COUNT), 1)
    base = ((y * SIDE + x) * SIDE + z) * UNITS
    row = jnp.zeros((1, COUNT), jnp.int32)
    for unit in range(UNITS):
        row = jnp.where(lane == base + unit, routes[unit, 0], row)
    placed[...] = row
    rt[x * SIDE + z] = row

    greet(
        [{"x": along(x, dx), "mp": along(z, dz)} for dx, dz in plane]
        + [{"y": along(y, dy)} for dy in STEPS]
        + [twin]
    )

    def shared(number, block, low, high):
        def own_copy(dy):
            return remote(
                block(y), block(y), s_w.at[number, dy], r_w.at[number, dy], {"y": along(y, dy)}
            )

        def up_copy():
            ref = low(behind(y, 1))
            return remote(ref, ref, s_w.at[number, 0], r_w.at[number, 0], {"y": along(y, 1)})

        def down_copy():
            ref = high(along(y, 1))
            return remote(ref, ref, s_w.at[number, 2], r_w.at[number, 2], {"y": along(y, 3)})

        def twin_copy(source):
            return remote(
                block(source), block(source), s_w.at[number, SIDE + source],
                r_w.at[number, SIDE + source], twin,
            )

        def begin():
            own_copy(1).start()
            own_copy(3).start()
            twin_copy(y).start()

        def middle():
            own_copy(1).wait()
            up_copy().start()
            own_copy(3).wait()
            down_copy().start()
            twin_copy(behind(y, 1)).start()
            twin_copy(along(y, 1)).start()

        def end():
            up_copy().wait()
            down_copy().wait()
            twin_copy(along(y, 2)).start()

        def taken():
            for source in range(SIDE):
                twin_copy(source).wait_recv()

        def given():
            for source in range(SIDE):
                twin_copy(source).wait_send()

        return begin, middle, end, taken, given

    mid = wmv.shape[3] // 2
    merge_w = shared(
        0,
        lambda ys: wmv.at[ys, section],
        lambda ys: wmv.at[ys, section, :, pl.ds(0, mid)],
        lambda ys: wmv.at[ys, section, :, pl.ds(mid, mid)],
    )

    def layer_shard(number, layer, first, amount):
        cols = pl.ds(first, amount)
        return shared(
            number,
            lambda ys: w.at[layer, ys, :, cols],
            lambda ys: w.at[layer, ys, pl.ds(0, FB // 2), cols],
            lambda ys: w.at[layer, ys, pl.ds(FB // 2, FB // 2), cols],
        )

    qkv_w = layer_shard(1, 0, 0, PW)
    out_w = layer_shard(2, 0, PW, QW)
    last_q = layer_shard(3, 1, 0, PW)
    last_o = layer_shard(4, 1, PW, QW)

    def only(at, *actions):
        @pl.when(section == at)
        def _():
            for action in actions:
                action()

    own_merge.wait()
    merge_w[0]()
    route_copies = [
        push(
            placed, rt.at[x * SIDE + z], s_rt.at[dx * SIDE + dz], r_rt.at[dx * SIDE + dz],
            {"x": along(x, dx), "mp": along(z, dz)},
        )
        for dx, dz in plane
    ]
    text_copies = []
    for dx in STEPS:
        xt = along(x, dx)
        text_copies.append(
            push(
                text.at[:, pl.ds(pl.multiple_of(xt * FB, FB), FB)], tbuf.at[x],
                s_t.at[dx], r_t.at[dx], {"x": xt},
            )
        )
    grad_copies = [
        push(grads, gbuf.at[x], s_g.at[dx], r_g.at[dx], {"x": along(x, dx)}) for dx in (1, 3)
    ]

    order = iota((PATCH, PATCH), 0)
    swap = one_hot(iota((PATCH, PATCH), 1) == (order & 15) * SIDE + (order >> 4))
    patch = jnp.dot(swap, patches[...], preferred_element_type=F32)
    normed = layer_norm(patch, v_gain[...]).astype(BF)
    for tile in range(15):
        v_tiles[tile].wait()
        v_proj[:, tile * TILE : (tile + 1) * TILE] = jnp.dot(
            normed, ring[tile % SLOTS], preferred_element_type=F32
        ).astype(BF)
        if tile + SLOTS < 20:
            v_tiles[tile + SLOTS].start()

    windows = []
    for head in range(VH):
        start = min(head * VHD // 128 * 128, VD - 256)
        lanes = iota((PATCH, 256), 1) + start
        windows.append((start, (lanes >= head * VHD) & (lanes < (head + 1) * VHD)))
    for head, (start, inside) in enumerate(windows):
        query = v_proj[:, start : start + 256].astype(F32)
        query = jnp.where(inside, query, 0.0).astype(BF)
        key = v_proj[:, VD + start : VD + start + 256]
        v_scores[head * PATCH : (head + 1) * PATCH, :] = lax.dot_general(
            query, key, (((1,), (1,)), ((), ())), preferred_element_type=F32
        )
    image_q = segments(iota((VH * PATCH, PATCH), 0) & 15, units)
    image_k = segments(iota((VH * PATCH, PATCH), 1) & 15, units)
    scores = jnp.where(image_q == image_k, v_scores[...] / math.sqrt(VHD), -1e30)
    top = jnp.max(scores, axis=1, keepdims=True)
    weights = jnp.exp(scores - top)
    v_weights[...] = (weights / jnp.sum(weights, axis=1, keepdims=True)).astype(BF)
    v_att[...] = jnp.zeros((PATCH, VD), F32)
    for head, (start, inside) in enumerate(windows):
        mixed = jnp.dot(
            v_weights[head * PATCH : (head + 1) * PATCH, :],
            v_proj[:, 2 * VD + start : 2 * VD + start + 256],
            preferred_element_type=F32,
        )
        v_att[:, start : start + 256] += jnp.where(inside, mixed, 0.0)
    attended = v_att[...].astype(BF)
    for tile in range(5):
        v_tiles[15 + tile].wait()
        cols = slice(tile * TILE, (tile + 1) * TILE)
        v_hidden[:, cols] = (
            patch[:, cols]
            + jnp.dot(attended, ring[(15 + tile) % SLOTS], preferred_element_type=F32)
        ).astype(BF).astype(F32)
    merged = layer_norm(v_hidden[...], merge_gain[...])
    for block in range(SIDE):
        pieces[block, :, :, :PIECE] = merged[:, block * PIECE : (block + 1) * PIECE].astype(BF).reshape(
            SIDE, UNITS, PIECE
        )
        pieces[block, :, :, PIECE:] = jnp.zeros((SIDE, UNITS, PADDED - PIECE), BF)
    plane_copies = []
    for dx, dz in plane:
        xt = along(x, dx)
        plane_copies.append(
            push(
                pieces.at[xt], xbuf.at[x * SIDE + z],
                s_pl.at[dx * SIDE + dz], r_pl.at[dx * SIDE + dz],
                {"x": xt, "mp": along(z, dz)},
            )
        )
    xbuf[x * SIDE + z] = pieces[x]

    merge_w[1]()
    raw_load.wait()
    shard = y * SIDE + x
    gain = lang_gain[:, pl.ds(pl.multiple_of(shard * FB, FB), FB)]
    gain = jnp.transpose(jnp.broadcast_to(gain, (128, FB)))
    for tile in range(PW // 128):
        cols = slice(tile * 128, (tile + 1) * 128)
        w[section, y, :, cols] = (wraw[:, cols].astype(F32) * gain).astype(BF)
    own_out.wait()
    only(0, qkv_w[0])

    for block in range(SIDE):
        before = iota((256, COUNT), 0) + block * 256
        tri[block * 256 : (block + 1) * 256, :] = one_hot(before < iota((256, COUNT), 1))
    for copy in route_copies:
        copy.wait()
    known = rt[0]
    for source in range(1, SIDE * SIDE):
        known = known + rt[source]
    ry[y] = known
    ry_copies = [
        push(ry.at[y], ry.at[y], s_ry.at[dy], r_ry.at[dy], {"y": along(y, dy)})
        for dy in STEPS
    ]
    for copy in plane_copies:
        copy.wait()
    merge_w[2]()
    merge_w[3]()

    def product(dx):
        cols = pl.ds(pl.multiple_of(along(x, dx) * FB, FB), FB)
        total = None
        for patch_at in range(SIDE):
            piece = xbuf[:, patch_at].reshape(SIDE * SIDE * UNITS, PADDED)[:, :PIECE]
            weights = wmv[patch_at, :, :, cols].reshape(PIECE, FB)
            term = jnp.dot(piece, weights, preferred_element_type=F32)
            total = term if total is None else total + term
        return total

    m_copies = []
    for dx in STEPS:
        msend[dx] = product(dx).astype(BF)
        m_copies.append(
            push(msend.at[dx], mrecv.at[dx], s_mx.at[dx], r_mx.at[dx], {"x": along(x, dx)})
        )
    part[...] = product(0)

    for copy in ry_copies:
        copy.wait()
    target = ry[0] + ry[1] + ry[2] + ry[3]
    named = jnp.where(iota((16, COUNT), 0) == target, 1.0, 0.0)
    earlier = jnp.dot(named.astype(BF), tri[...], preferred_element_type=F32)
    position = jnp.sum(named * earlier, axis=0, keepdims=True).astype(jnp.int32)
    slots = (target - y * SIDE) * TOK + position
    for block in range(SIDE):
        wanted = iota((TOK, COUNT), 0) + block * TOK
        pick[block * TOK : (block + 1) * TOK, :] = one_hot(wanted == slots)
    line[...] = jnp.where((target >> 2) == y, (target & 3) * TOK + position + 1, 0)
    down = iota((256, COUNT), 0)
    chosen_rows = one_hot(iota((256, COUNT), 1) == (down >> 6) * 256 + x * 64 + (down & 63))

    def upright(values):
        wide = jnp.broadcast_to(values.astype(F32), (128, COUNT)).astype(BF)
        return lax.dot_general(
            chosen_rows, wide, (((1,), (1,)), ((), ())), preferred_element_type=F32
        )

    slot_line = line[...]
    gslot[...] = (
        16.0 * upright(slot_line >> 4) + upright(slot_line & 15)
    ).astype(jnp.int32) - 1

    only(0, qkv_w[1], out_w[0])
    for copy in m_copies:
        copy.wait()
    total = part[...]
    for dx in STEPS:
        total = total + mrecv[dx].astype(F32)
    ybuf[y] = total.astype(BF)
    y_copies = [
        push(ybuf.at[y], ybuf.at[y], s_my.at[dy], r_my.at[dy], {"y": along(y, dy)})
        for dy in STEPS
    ]
    grad_copies[0].wait()
    from_left = gbuf.at[behind(x, 1), pl.ds(0, HALF), :]
    grad_copies[1].wait()
    from_right = gbuf.at[along(x, 1), pl.ds(HALF, HALF), :]
    grad_copies = [
        push(from_left, from_left, s_g.at[0], r_g.at[0], {"x": along(x, 1)}),
        push(from_right, from_right, s_g.at[2], r_g.at[2], {"x": along(x, 3)}),
    ]
    present = jnp.dot(pick[...], jnp.ones((COUNT, 128), BF), preferred_element_type=F32)
    own_text.wait()
    for copy in text_copies:
        copy.wait()
    for copy in y_copies:
        copy.wait()
    picked = jnp.dot(
        pick[...], ybuf[...].reshape(COUNT, FB), preferred_element_type=F32
    ).astype(BF)
    for group in range(SIDE):
        for part_of in range(2):
            span = slice(group * TOK + part_of * HALF, group * TOK + (part_of + 1) * HALF)
            to = slice(group * HALF, (group + 1) * HALF)
            inside = slice(part_of * HALF, (part_of + 1) * HALF)
            for tile in range(FB // 128):
                cols = slice(tile * 128, (tile + 1) * 128)
                zbuf[part_of, z, to, cols] = jnp.where(
                    present[span, :] > 0.5, picked[span, cols], tbuf[group, inside, cols]
                )

    z_copies, f_copies, x_copies, a_copies, o_copies, e_copies = {}, {}, {}, {}, {}, []

    def spread(layer, part):
        z_copies[layer, part] = {
            dz: push(
                zbuf.at[part, z], zbuf.at[part, z],
                s_z.at[layer, part, dz], r_z.at[layer, part, dz], {"mp": along(z, dz)},
            )
            for dz in (1, 3)
        }

    def times(layer, part, dz):
        zs = behind(z, dz)
        wide = zbuf[part, zs].astype(F32)
        squared = jnp.sum(wide * wide, axis=1, keepdims=True)
        if dz:
            squares[part] += jnp.broadcast_to(squared, (rows, HD))
        else:
            squares[part] = jnp.broadcast_to(squared, (rows, HD))

        product = jnp.dot(
            zbuf[part, zs], w[layer, zs, :, :PW], preferred_element_type=F32
        )
        if dz:
            acc[part] += product
        else:
            acc[part] = product

    def passed(layer, part):
        copies = z_copies[layer, part]
        copies[1].wait()
        zs = behind(z, 1)
        f_copies[layer, part] = [
            push(
                zbuf.at[part, zs, left], zbuf.at[part, zs, left],
                s_z.at[layer, part, 0], r_z.at[layer, part, 0], {"mp": along(z, 1)},
            )
        ]
        copies[3].wait()
        zs = along(z, 1)
        f_copies[layer, part].append(
            push(
                zbuf.at[part, zs, right], zbuf.at[part, zs, right],
                s_z.at[layer, part, 2], r_z.at[layer, part, 2], {"mp": along(z, 3)},
            )
        )

    def own_part(layer, part):
        times(layer, part, 0)

    def project(layer, part):
        times(layer, part, 1)
        times(layer, part, 3)
        for copy in f_copies[layer, part]:
            copy.wait()
        times(layer, part, 2)
        lane = lax.broadcasted_iota(jnp.int32, (HALF, HD), 1)
        copies = []
        for dx in STEPS:
            xt = along(x, dx)
            span = pl.ds(pl.multiple_of(xt * HALF, HALF), HALF)
            psend[part, dx, :, :PW] = acc[part, span, :].astype(BF)
            sq = squares[part, span, :]
            high = sq.astype(BF)
            low = (sq - high.astype(F32)).astype(BF)
            psend[part, dx, :, PW:] = jnp.where(lane < 64, high, low)
            copies.append(
                push(
                    psend.at[part, dx], rbuf.at[part, dx],
                    s_x.at[layer, part, dx], r_x.at[layer, part, dx], {"x": xt},
                )
            )
        x_copies[layer, part] = copies

    def attend(layer, part):
        own = pl.ds(pl.multiple_of(x * HALF, HALF), HALF)
        total = acc[part, own, :]
        sq = squares[part, own, :][:, :1]
        for copy in x_copies[layer, part]:
            copy.wait()
        for dx in STEPS:
            total = total + rbuf[part, dx, :, :PW].astype(F32)
            tail = rbuf[part, dx, :, PW:].astype(F32)
            sq = sq + tail[:, :1] + tail[:, 64:65]
        projected = (total * lax.rsqrt(sq / D + EPSILON)).astype(BF)
        kv[part * HALF : (part + 1) * HALF, :] = projected[:, QW:]
        seen = (part + 1) * HALF
        keys = kv[:seen, :HD]
        values = kv[:seen, HD:]
        queries = jnp.concatenate(
            [projected[:, head * HD : (head + 1) * HD] for head in range(HEADS)], axis=0
        )
        at = iota((HALF, seen), 0) + part * HALF
        key_at = iota((HALF, seen), 1)
        allowed = jnp.where(
            (segments(at, lengths) == segments(key_at, lengths)) & (at >= key_at), 1.0, 0.0
        )
        allowed = jnp.concatenate([allowed] * HEADS, axis=0) > 0.5
        scores = lax.dot_general(
            queries, keys, (((1,), (1,)), ((), ())), preferred_element_type=F32
        ) * (1.0 / math.sqrt(HD))
        scores = jnp.where(allowed, scores, -1e30)
        top = jnp.max(scores, axis=1, keepdims=True)
        weights = jnp.exp(scores - top)
        weights = (weights / jnp.sum(weights, axis=1, keepdims=True)).astype(BF)
        mixed = jnp.dot(weights, values, preferred_element_type=F32).astype(BF)
        for head in range(HEADS):
            abuf[part, x, :, head * HD : (head + 1) * HD] = mixed[
                head * HALF : (head + 1) * HALF, :
            ]
        a_copies[layer, part] = [
            push(
                abuf.at[part, x], abuf.at[part, x],
                s_a.at[layer, part, dx], r_a.at[layer, part, dx], {"x": along(x, dx)},
            )
            for dx in STEPS
        ]

    def output(layer, part):
        for copy in a_copies[layer, part]:
            copy.wait()
        copies = {}

        def send(name, src, dst, dz):
            copies[name] = push(
                src, dst, s_o.at[layer, part, name], r_o.at[layer, part, name],
                {"mp": along(z, dz)},
            )

        for dz in (2, 1, 3, 0):
            zt = along(z, dz)

            osend[part, dz] = lax.dot_general(
                abuf[part].reshape(rows, QW), w[layer, zt, :, PW:],
                (((1,), (1,)), ((), ())), preferred_element_type=F32,
            ).astype(BF)

            if dz == 2:
                send(0, osend.at[part, 2, left], orel.at[part, 0], 1)
                send(1, osend.at[part, 2, right], orel.at[part, 1], 3)
            elif dz == 1:
                send(2, osend.at[part, 1, right], orec.at[part, 0, right], 1)
            elif dz == 3:
                send(3, osend.at[part, 3, left], orec.at[part, 1, left], 3)
        o_copies[layer, part] = copies, send

    def relay(layer, part):
        copies, send = o_copies[layer, part]
        copies[0].wait()
        osend[part, 1, left] = (
            osend[part, 1, left].astype(F32) + orel[part, 0].astype(F32)
        ).astype(BF)
        send(4, osend.at[part, 1, left], orec.at[part, 0, left], 1)
        copies[1].wait()
        osend[part, 3, right] = (
            osend[part, 3, right].astype(F32) + orel[part, 1].astype(F32)
        ).astype(BF)
        send(5, osend.at[part, 3, right], orec.at[part, 1, right], 3)

    def finish(layer, part):
        update = osend[part, 0].astype(F32)
        copies, _ = o_copies[layer, part]
        for name in (2, 3, 4, 5):
            copies[name].wait()
        for side in range(2):
            update = update + orec[part, side].astype(F32)
        fresh = (zbuf[part, z].astype(F32) + update).astype(BF)
        if layer == 0:
            zbuf[part, z] = fresh
            return
        osend[part, 0] = fresh
        for dx in STEPS:
            xt = along(x, dx)
            e_copies.append(
                push(
                    osend.at[part, 0, pl.ds(pl.multiple_of(xt * HALF, HALF), HALF), :],
                    obuf.at[x, part],
                    s_e.at[part, dx], r_e.at[part, dx], {"x": xt},
                )
            )
        obuf[x, part] = osend[part, 0, pl.ds(pl.multiple_of(x * HALF, HALF), HALF), :
        ]

    spread(0, 0)
    g_copies, gz_copies = [], []

    def ready_qkv(layer, part):
        only(0, qkv_w[2], out_w[1])
        only(1, last_q[0], qkv_w[3])

    def ready_out(layer, part):
        only(0, out_w[2])
        only(1, last_q[1], last_o[0], out_w[3])

    def ready_last(layer, part):
        only(1, last_q[2], last_o[1])
        only(0, last_q[3])

    def ready_end(layer, part):
        only(1, last_o[2])
        only(0, last_o[3])

    def choose(layer, part):
        own_grads.wait()
        for copy in grad_copies:
            copy.wait()
        for dy in (1, 3, 2, 0):
            yt = along(y, dy)
            wanted = gslot[pl.ds(pl.multiple_of(yt * 64, 64), 64), :1]
            chosen = one_hot(iota((64, SIDE * TOK), 1) == wanted)
            gsend[dy] = jnp.dot(
                chosen, gbuf[...].reshape(SIDE * TOK, width), preferred_element_type=F32
            ).astype(BF)
            if dy:
                g_copies.append(
                    push(gsend.at[dy], grec.at[dy], s_gy.at[dy], r_gy.at[dy], {"y": yt})
                )

    def hand(layer, part):
        for copy in g_copies:
            copy.wait()
        found = gsend[0].astype(F32)
        for dy in STEPS:
            found = found + grec[dy].astype(F32)
        gz[...] = found.astype(BF).reshape(SIDE, UNITS, width)
        for dz in STEPS:
            zt = along(z, dz)
            gz_copies.append(
                push(gz.at[zt], mz.at[z], s_gz.at[dz], r_gz.at[dz], {"mp": zt})
            )
        mz[z] = gz[z]

    for stage, layer, part_at in (
        (ready_qkv, 0, 0),
        (own_part, 0, 0),
        (passed, 0, 0),
        (spread, 0, 1),
        (project, 0, 0),
        (own_part, 0, 1),
        (attend, 0, 0),
        (passed, 0, 1),
        (project, 0, 1),
        (ready_out, 0, 0),
        (output, 0, 0),
        (attend, 0, 1),
        (relay, 0, 0),
        (output, 0, 1),
        (finish, 0, 0),
        (spread, 1, 0),
        (relay, 0, 1),
        (ready_last, 1, 0),
        (own_part, 1, 0),
        (finish, 0, 1),
        (passed, 1, 0),
        (spread, 1, 1),
        (project, 1, 0),
        (own_part, 1, 1),
        (attend, 1, 0),
        (choose, 1, 0),
        (passed, 1, 1),
        (project, 1, 1),
        (ready_end, 1, 0),
        (output, 1, 0),
        (attend, 1, 1),
        (relay, 1, 0),
        (output, 1, 1),
        (hand, 1, 0),
        (finish, 1, 0),
        (relay, 1, 1),
        (finish, 1, 1),
    ):
        stage(layer, part_at)

    for copy in gz_copies:
        copy.wait()
    for block in range(SIDE):
        mg[:, block * width : (block + 1) * width] = mz[block]
    for copy in e_copies:
        copy.wait()
    for block in range(SIDE):
        for part_of in range(2):
            out[part_of * HALF : (part_of + 1) * HALF, block * FB : (block + 1) * FB] = obuf[
                block, part_of
            ]
    merge_w[4]()
    only(0, qkv_w[4], out_w[4])
    only(1, last_q[4], last_o[4])


def shards(*arrays):
    vmem = pl.BlockSpec(memory_space=pltpu.VMEM)
    smem = pl.BlockSpec(memory_space=pltpu.SMEM)
    hbm = pl.BlockSpec(memory_space=pl.ANY)
    dma = pltpu.SemaphoreType.DMA
    rows = SIDE * HALF
    width = arrays[13].shape[1]
    half = arrays[6].shape[0] // 2
    stage = dma((2, 2, SIDE))
    four, plane = dma((SIDE,)), dma((SIDE * SIDE,))
    call = pl.pallas_call(
        whole_kernel,
        out_shape=(
            jax.ShapeDtypeStruct((TOK, SIDE * FB), BF),
            jax.ShapeDtypeStruct((UNITS, SIDE * width), BF),
        ),
        in_specs=[vmem, smem, vmem, hbm, hbm, vmem, hbm, smem, hbm, smem, vmem, hbm, hbm, hbm],
        out_specs=(vmem, vmem),
        scratch_shapes=[
            pltpu.VMEM((SLOTS, VD, TILE), BF),
            pltpu.VMEM((FB, PW), BF),
            pltpu.VMEM((SIDE, 2, half, SIDE * FB), BF),
            pltpu.VMEM((2, SIDE, FB, PW + QW), BF),
            pltpu.VMEM((PATCH, 3 * VD), BF),
            pltpu.VMEM((VH * PATCH, PATCH), F32),
            pltpu.VMEM((VH * PATCH, PATCH), BF),
            pltpu.VMEM((PATCH, VD), F32),
            pltpu.VMEM((PATCH, VD), F32),
            pltpu.VMEM((SIDE, SIDE, UNITS, PADDED), BF),
            pltpu.VMEM((SIDE * SIDE, SIDE, UNITS, PADDED), BF),
            pltpu.VMEM((256, FB), F32),
            pltpu.VMEM((SIDE, 256, FB), BF),
            pltpu.VMEM((SIDE, 256, FB), BF),
            pltpu.VMEM((SIDE, 256, FB), BF),
            pltpu.VMEM((SIDE, TOK, FB), BF),
            pltpu.VMEM((SIDE * TOK, COUNT), BF),
            pltpu.VMEM((1, COUNT), jnp.int32),
            pltpu.VMEM((SIDE * SIDE, 1, COUNT), jnp.int32),
            pltpu.VMEM((SIDE, 1, COUNT), jnp.int32),
            pltpu.VMEM((COUNT, COUNT), BF),
            pltpu.VMEM((1, COUNT), jnp.int32),
            pltpu.VMEM((256, 128), jnp.int32),
            pltpu.VMEM((2, SIDE, rows, FB), BF),
            pltpu.VMEM((2, rows, PW), F32),
            pltpu.VMEM((2, rows, HD), F32),
            pltpu.VMEM((TOK, 2 * HD), BF),
            pltpu.VMEM((2, SIDE, HALF, PT), BF),
            pltpu.VMEM((2, SIDE, HALF, PT), BF),
            pltpu.VMEM((2, SIDE, HALF, QW), BF),
            pltpu.VMEM((2, SIDE, rows, FB), BF),
            pltpu.VMEM((2, 2, rows, FB), BF),
            pltpu.VMEM((2, 2, rows // 2, FB), BF),
            pltpu.VMEM((SIDE, 2, HALF, FB), BF),
            pltpu.VMEM((SIDE, TOK, width), BF),
            pltpu.VMEM((SIDE, 64, width), BF),
            pltpu.VMEM((SIDE, 64, width), BF),
            pltpu.VMEM((SIDE, UNITS, width), BF),
            pltpu.VMEM((SIDE, UNITS, width), BF),
            dma((SLOTS,)), dma((5,)), dma((5, 8)), dma((5, 8)),
            plane, plane, four, four, plane, plane, four, four, four, four, four, four,
            stage, stage, stage, stage, stage, stage, dma((2, 2, 6)), dma((2, 2, 6)),
            dma((2, SIDE)), dma((2, SIDE)),
            four, four, four, four, four, four,
        ],
        compiler_params=pltpu.CompilerParams(
            collective_id=1, has_side_effects=True, vmem_limit_bytes=VMEM_LIMIT
        ),
        name="whole",
    )
    arrays = list(arrays)
    arrays[2] = arrays[2][None, :]
    arrays[5] = arrays[5][None, :]
    return call(*arrays)


def solution(mesh):
    grid = jax.sharding.Mesh(
        mesh.devices.reshape(2, SIDE, SIDE, SIDE), ("section", "y", "x", "mp")
    )
    every = ("section", "y", "x", "mp")
    home = P(("section", "y", "x"), "mp")
    in_specs = (
        P(every, None),
        P(every, None),
        P(),
        P(),
        P(),
        P(),
        P(("y", "x"), "mp"),
        P(every, None),
        home,
        P(("section", "y", "x"), None),
        P("section", None),
        P("section", ("y", "x"), "mp"),
        P("section", ("y", "x"), "mp"),
        home,
    )
    out_specs = (home, P(every, None))
    return jax.shard_map(shards, mesh=grid, in_specs=in_specs, out_specs=out_specs, check_vma=False)
```

```python
import functools
import math

import jax
import jax.numpy as jnp
from jax import lax
from jax.experimental import pallas as pl
from jax.experimental.pallas import tpu as pltpu
from jax.sharding import PartitionSpec as P

QH = 32
KVH = 4
HD = 128
VD = 1280
VH = 16
VHD = 80
SIDE = 4
TOK = 128
HALF = TOK // 2
STEPS = (1, 3, 2)
FB = 512
HEADS = QH // KVH
QW = HEADS * HD
PW = QW + 2 * HD
PT = PW + HD
D = 8192
PATCH = 64
UNITS = 16
PIECE = VD // SIDE
PADDED = 384
COUNT = 1024
TILE = 256
SLOTS = 6
EPSILON = 1e-06
VMEM_LIMIT = 62 * 1024 * 1024
BF = jnp.bfloat16
F32 = jnp.float32
MESH = pl.DeviceIdType.MESH


def layer_norm(values, norm_gain):
    centre = jnp.mean(values, axis=-1, keepdims=True)
    centred = values - centre
    variance = jnp.mean(centred * centred, axis=-1, keepdims=True)
    return centred * lax.rsqrt(variance + EPSILON) * norm_gain


def remote(src, dst, send_sem, recv_sem, where):
    return pltpu.make_async_remote_copy(
        src_ref=src, dst_ref=dst, send_sem=send_sem, recv_sem=recv_sem,
        device_id=where, device_id_type=MESH,
    )


def push(src, dst, send_sem, recv_sem, where):
    copy = remote(src, dst, send_sem, recv_sem, where)
    copy.start()
    return copy


def greet(partners):
    barrier = pltpu.get_barrier_semaphore()
    for where in partners:
        pl.semaphore_signal(barrier, inc=1, device_id=where, device_id_type=MESH)
    pl.semaphore_wait(barrier, len(partners))


def along(index, step):
    return lax.rem(index + step, SIDE)


def behind(index, step):
    return lax.rem(index + SIDE - step, SIDE)


def one_hot(condition):
    return jnp.where(condition, 1.0, 0.0).astype(BF)


def iota(shape, dimension):
    return lax.broadcasted_iota(jnp.int32, shape, dimension)


def segments(index, lengths):
    first = lengths[0, 0]
    second = first + lengths[0, 1]
    return jnp.where(index >= first, 1, 0) + jnp.where(index >= second, 1, 0)


def whole_kernel(
    patches, units, v_gain, v_qkv, v_out, merge_gain, w_merge, routes, text, lengths,
    lang_gain, w_qkv, wo_t, grads,
    out, mg,
    ring, wraw, wmv, w, v_proj, v_scores, v_weights, v_att, v_hidden, pieces, xbuf, part, msend, mrecv, ybuf, tbuf, pick,
    placed, rt, ry, tri, line, gslot,
    zbuf, acc, squares, kv, psend, rbuf, abuf, osend, orec, orel, obuf,
    gbuf, gsend, grec, gz, mz,
    v_sem, l_sem, s_w, r_w, s_rt, r_rt, s_ry, r_ry, s_pl, r_pl, s_mx, r_mx, s_my, r_my, s_t, r_t,
    s_z, r_z, s_x, r_x, s_a, r_a, s_o, r_o, s_e, r_e,
    s_g, r_g, s_gy, r_gy, s_gz, r_gz,
):
    section = lax.axis_index("section")
    x = lax.axis_index("x")
    y = lax.axis_index("y")
    z = lax.axis_index("mp")
    twin = {"section": 1 - section}
    rows = SIDE * HALF
    width = grads.shape[1]
    half = wmv.shape[2]
    plane = [(dx, dz) for dx in range(SIDE) for dz in range(SIDE) if dx or dz]
    left = slice(0, rows // 2)
    right = slice(rows // 2, rows)

    own_merge = pltpu.make_async_copy(
        w_merge.at[pl.ds(pl.multiple_of(section * half, half), half), :],
        wmv.at[y, section], l_sem.at[0],
    )
    own_merge.start()
    v_tiles = [
        pltpu.make_async_copy(
            (v_qkv if tile < 15 else v_out).at[:, pl.ds((tile if tile < 15 else tile - 15) * TILE, TILE)],
            ring.at[tile % SLOTS], v_sem.at[tile % SLOTS],
        )
        for tile in range(20)
    ]
    for tile in range(SLOTS):
        v_tiles[tile].start()
    raw_load = pltpu.make_async_copy(w_qkv.at[0], wraw, l_sem.at[1])
    raw_load.start()
    own_out = pltpu.make_async_copy(
        wo_t.at[0], w.at[section, y, :, pl.ds(PW, QW)], l_sem.at[2]
    )
    own_out.start()
    own_text = pltpu.make_async_copy(
        text.at[:, pl.ds(pl.multiple_of(x * FB, FB), FB)], tbuf.at[x], l_sem.at[3]
    )
    own_text.start()
    own_grads = pltpu.make_async_copy(grads, gbuf.at[x], l_sem.at[4])
    own_grads.start()

    lane = iota((1, COUNT), 1)
    base = ((y * SIDE + x) * SIDE + z) * UNITS
    row = jnp.zeros((1, COUNT), jnp.int32)
    for unit in range(UNITS):
        row = jnp.where(lane == base + unit, routes[unit, 0], row)
    placed[...] = row
    rt[x * SIDE + z] = row

    greet(
        [{"x": along(x, dx), "mp": along(z, dz)} for dx, dz in plane]
        + [{"y": along(y, dy)} for dy in STEPS]
        + [twin]
    )

    def shared(number, block, low, high):
        def own_copy(dy):
            return remote(
                block(y), block(y), s_w.at[number, dy], r_w.at[number, dy], {"y": along(y, dy)}
            )

        def up_copy():
            ref = low(behind(y, 1))
            return remote(ref, ref, s_w.at[number, 0], r_w.at[number, 0], {"y": along(y, 1)})

        def down_copy():
            ref = high(along(y, 1))
            return remote(ref, ref, s_w.at[number, 2], r_w.at[number, 2], {"y": along(y, 3)})

        def twin_copy(source):
            return remote(
                block(source), block(source), s_w.at[number, SIDE + source],
                r_w.at[number, SIDE + source], twin,
            )

        def begin():
            own_copy(1).start()
            own_copy(3).start()
            twin_copy(y).start()

        def middle():
            own_copy(1).wait()
            up_copy().start()
            own_copy(3).wait()
            down_copy().start()
            twin_copy(behind(y, 1)).start()
            twin_copy(along(y, 1)).start()

        def end():
            up_copy().wait()
            down_copy().wait()
            twin_copy(along(y, 2)).start()

        def taken():
            for source in range(SIDE):
                twin_copy(source).wait_recv()

        def given():
            for source in range(SIDE):
                twin_copy(source).wait_send()

        return begin, middle, end, taken, given

    mid = wmv.shape[3] // 2
    merge_w = shared(
        0,
        lambda ys: wmv.at[ys, section],
        lambda ys: wmv.at[ys, section, :, pl.ds(0, mid)],
        lambda ys: wmv.at[ys, section, :, pl.ds(mid, mid)],
    )

    def layer_shard(number, layer, first, amount):
        cols = pl.ds(first, amount)
        return shared(
            number,
            lambda ys: w.at[layer, ys, :, cols],
            lambda ys: w.at[layer, ys, pl.ds(0, FB // 2), cols],
            lambda ys: w.at[layer, ys, pl.ds(FB // 2, FB // 2), cols],
        )

    qkv_w = layer_shard(1, 0, 0, PW)
    out_w = layer_shard(2, 0, PW, QW)
    last_q = layer_shard(3, 1, 0, PW)
    last_o = layer_shard(4, 1, PW, QW)

    def only(at, *actions):
        @pl.when(section == at)
        def _():
            for action in actions:
                action()

    own_merge.wait()
    merge_w[0]()
    route_copies = [
        push(
            placed, rt.at[x * SIDE + z], s_rt.at[dx * SIDE + dz], r_rt.at[dx * SIDE + dz],
            {"x": along(x, dx), "mp": along(z, dz)},
        )
        for dx, dz in plane
    ]
    text_copies = []
    for dx in STEPS:
        xt = along(x, dx)
        text_copies.append(
            push(
                text.at[:, pl.ds(pl.multiple_of(xt * FB, FB), FB)], tbuf.at[x],
                s_t.at[dx], r_t.at[dx], {"x": xt},
            )
        )
    grad_copies = [
        push(grads, gbuf.at[x], s_g.at[dx], r_g.at[dx], {"x": along(x, dx)}) for dx in (1, 3)
    ]

    order = iota((PATCH, PATCH), 0)
    swap = one_hot(iota((PATCH, PATCH), 1) == (order & 15) * SIDE + (order >> 4))
    patch = jnp.dot(swap, patches[...], preferred_element_type=F32)
    normed = layer_norm(patch, v_gain[...].reshape(1, VD)).astype(BF)
    for tile in range(15):
        v_tiles[tile].wait()
        v_proj[:, tile * TILE : (tile + 1) * TILE] = jnp.dot(
            normed, ring[tile % SLOTS], preferred_element_type=F32
        ).astype(BF)
        if tile + SLOTS < 20:
            v_tiles[tile + SLOTS].start()

    windows = []
    for head in range(VH):
        start = min(head * VHD // 128 * 128, VD - 256)
        lanes = iota((PATCH, 256), 1) + start
        windows.append((start, (lanes >= head * VHD) & (lanes < (head + 1) * VHD)))
    for head, (start, inside) in enumerate(windows):
        query = v_proj[:, start : start + 256].astype(F32)
        query = jnp.where(inside, query, 0.0).astype(BF)
        key = v_proj[:, VD + start : VD + start + 256]
        v_scores[head * PATCH : (head + 1) * PATCH, :] = lax.dot_general(
            query, key, (((1,), (1,)), ((), ())), preferred_element_type=F32
        )
    image_q = segments(iota((VH * PATCH, PATCH), 0) & 15, units)
    image_k = segments(iota((VH * PATCH, PATCH), 1) & 15, units)
    scores = jnp.where(image_q == image_k, v_scores[...] / math.sqrt(VHD), -1e30)
    top = jnp.max(scores, axis=1, keepdims=True)
    weights = jnp.exp(scores - top)
    v_weights[...] = (weights / jnp.sum(weights, axis=1, keepdims=True)).astype(BF)
    v_att[...] = jnp.zeros((PATCH, VD), F32)
    for head, (start, inside) in enumerate(windows):
        mixed = jnp.dot(
            v_weights[head * PATCH : (head + 1) * PATCH, :],
            v_proj[:, 2 * VD + start : 2 * VD + start + 256],
            preferred_element_type=F32,
        )
        v_att[:, start : start + 256] += jnp.where(inside, mixed, 0.0)
    attended = v_att[...].astype(BF)
    for tile in range(5):
        v_tiles[15 + tile].wait()
        cols = slice(tile * TILE, (tile + 1) * TILE)
        v_hidden[:, cols] = (
            patch[:, cols]
            + jnp.dot(attended, ring[(15 + tile) % SLOTS], preferred_element_type=F32)
        ).astype(BF).astype(F32)
    merged = layer_norm(v_hidden[...], merge_gain[...].reshape(1, VD))
    for block in range(SIDE):
        pieces[block, :, :, :PIECE] = merged[:, block * PIECE : (block + 1) * PIECE].astype(BF).reshape(
            SIDE, UNITS, PIECE
        )
        pieces[block, :, :, PIECE:] = jnp.zeros((SIDE, UNITS, PADDED - PIECE), BF)
    plane_copies = []
    for dx, dz in plane:
        xt = along(x, dx)
        plane_copies.append(
            push(
                pieces.at[xt], xbuf.at[x * SIDE + z],
                s_pl.at[dx * SIDE + dz], r_pl.at[dx * SIDE + dz],
                {"x": xt, "mp": along(z, dz)},
            )
        )
    xbuf[x * SIDE + z] = pieces[x]

    merge_w[1]()
    raw_load.wait()
    shard = y * SIDE + x
    gain = lang_gain[:, pl.ds(pl.multiple_of(shard * FB, FB), FB)]
    gain = jnp.transpose(jnp.broadcast_to(gain, (128, FB)))
    for tile in range(PW // 128):
        cols = slice(tile * 128, (tile + 1) * 128)
        w[section, y, :, cols] = (wraw[:, cols].astype(F32) * gain).astype(BF)
    own_out.wait()
    only(0, qkv_w[0])

    for block in range(SIDE):
        before = iota((256, COUNT), 0) + block * 256
        tri[block * 256 : (block + 1) * 256, :] = one_hot(before < iota((256, COUNT), 1))
    for copy in route_copies:
        copy.wait()
    known = rt[0]
    for source in range(1, SIDE * SIDE):
        known = known + rt[source]
    ry[y] = known
    ry_copies = [
        push(ry.at[y], ry.at[y], s_ry.at[dy], r_ry.at[dy], {"y": along(y, dy)})
        for dy in STEPS
    ]
    for copy in plane_copies:
        copy.wait()
    merge_w[2]()
    merge_w[3]()

    def product(dx):
        cols = pl.ds(pl.multiple_of(along(x, dx) * FB, FB), FB)
        total = None
        for patch_at in range(SIDE):
            piece = xbuf[:, patch_at].reshape(SIDE * SIDE * UNITS, PADDED)[:, :PIECE]
            weights = wmv[patch_at, :, :, cols].reshape(PIECE, FB)
            term = jnp.dot(piece, weights, preferred_element_type=F32)
            total = term if total is None else total + term
        return total

    m_copies = []
    for dx in STEPS:
        msend[dx] = product(dx).astype(BF)
        m_copies.append(
            push(msend.at[dx], mrecv.at[dx], s_mx.at[dx], r_mx.at[dx], {"x": along(x, dx)})
        )
    part[...] = product(0)

    for copy in ry_copies:
        copy.wait()
    target = ry[0] + ry[1] + ry[2] + ry[3]
    named = jnp.where(iota((16, COUNT), 0) == target, 1.0, 0.0)
    earlier = jnp.dot(named.astype(BF), tri[...], preferred_element_type=F32)
    position = jnp.sum(named * earlier, axis=0, keepdims=True).astype(jnp.int32)
    slots = (target - y * SIDE) * TOK + position
    for block in range(SIDE):
        wanted = iota((TOK, COUNT), 0) + block * TOK
        pick[block * TOK : (block + 1) * TOK, :] = one_hot(wanted == slots)
    line[...] = jnp.where((target >> 2) == y, (target & 3) * TOK + position + 1, 0)
    down = iota((256, COUNT), 0)
    chosen_rows = one_hot(iota((256, COUNT), 1) == (down >> 6) * 256 + x * 64 + (down & 63))

    def upright(values):
        wide = jnp.broadcast_to(values.astype(F32), (128, COUNT)).astype(BF)
        return lax.dot_general(
            chosen_rows, wide, (((1,), (1,)), ((), ())), preferred_element_type=F32
        )

    slot_line = line[...]
    gslot[...] = (
        16.0 * upright(slot_line >> 4) + upright(slot_line & 15)
    ).astype(jnp.int32) - 1

    only(0, qkv_w[1])
    for copy in m_copies:
        copy.wait()
    total = part[...]
    for dx in STEPS:
        total = total + mrecv[dx].astype(F32)
    ybuf[y] = total.astype(BF)
    y_copies = [
        push(ybuf.at[y], ybuf.at[y], s_my.at[dy], r_my.at[dy], {"y": along(y, dy)})
        for dy in STEPS
    ]
    grad_copies[0].wait()
    from_left = gbuf.at[behind(x, 1), pl.ds(0, HALF), :]
    grad_copies[1].wait()
    from_right = gbuf.at[along(x, 1), pl.ds(HALF, HALF), :]
    grad_copies = [
        push(from_left, from_left, s_g.at[0], r_g.at[0], {"x": along(x, 1)}),
        push(from_right, from_right, s_g.at[2], r_g.at[2], {"x": along(x, 3)}),
    ]
    present = jnp.dot(pick[...], jnp.ones((COUNT, 128), BF), preferred_element_type=F32)
    own_text.wait()
    for copy in text_copies:
        copy.wait()
    for copy in y_copies:
        copy.wait()
    only(0, out_w[0])
    picked = jnp.dot(
        pick[...], ybuf[...].reshape(COUNT, FB), preferred_element_type=F32
    ).astype(BF)
    for group in range(SIDE):
        for part_of in range(2):
            span = slice(group * TOK + part_of * HALF, group * TOK + (part_of + 1) * HALF)
            to = slice(group * HALF, (group + 1) * HALF)
            inside = slice(part_of * HALF, (part_of + 1) * HALF)
            for tile in range(FB // 128):
                cols = slice(tile * 128, (tile + 1) * 128)
                zbuf[part_of, z, to, cols] = jnp.where(
                    present[span, :] > 0.5, picked[span, cols], tbuf[group, inside, cols]
                )

    z_copies, f_copies, x_copies, a_copies, o_copies, e_copies = {}, {}, {}, {}, {}, []

    def spread(layer, part):
        z_copies[layer, part] = {
            dz: push(
                zbuf.at[part, z], zbuf.at[part, z],
                s_z.at[layer, part, dz], r_z.at[layer, part, dz], {"mp": along(z, dz)},
            )
            for dz in (1, 3)
        }

    def times(layer, part, dz):
        zs = behind(z, dz)
        wide = zbuf[part, zs].astype(F32)
        squared = jnp.sum(wide * wide, axis=1, keepdims=True)
        if dz:
            squares[part] += jnp.broadcast_to(squared, (rows, HD))
        else:
            squares[part] = jnp.broadcast_to(squared, (rows, HD))

        product = jnp.dot(
            zbuf[part, zs], w[layer, zs, :, :PW], preferred_element_type=F32
        )
        if dz:
            acc[part] += product
        else:
            acc[part] = product

    def passed(layer, part):
        copies = z_copies[layer, part]
        copies[1].wait()
        zs = behind(z, 1)
        f_copies[layer, part] = [
            push(
                zbuf.at[part, zs, left], zbuf.at[part, zs, left],
                s_z.at[layer, part, 0], r_z.at[layer, part, 0], {"mp": along(z, 1)},
            )
        ]
        copies[3].wait()
        zs = along(z, 1)
        f_copies[layer, part].append(
            push(
                zbuf.at[part, zs, right], zbuf.at[part, zs, right],
                s_z.at[layer, part, 2], r_z.at[layer, part, 2], {"mp": along(z, 3)},
            )
        )

    def own_part(layer, part):
        times(layer, part, 0)

    def project(layer, part):
        times(layer, part, 1)
        times(layer, part, 3)
        for copy in f_copies[layer, part]:
            copy.wait()
        times(layer, part, 2)
        lane = lax.broadcasted_iota(jnp.int32, (HALF, HD), 1)
        copies = []
        for dx in STEPS:
            xt = along(x, dx)
            span = pl.ds(pl.multiple_of(xt * HALF, HALF), HALF)
            psend[part, dx, :, :PW] = acc[part, span, :].astype(BF)
            sq = squares[part, span, :]
            high = sq.astype(BF)
            low = (sq - high.astype(F32)).astype(BF)
            psend[part, dx, :, PW:] = jnp.where(lane < 64, high, low)
            copies.append(
                push(
                    psend.at[part, dx], rbuf.at[part, dx],
                    s_x.at[layer, part, dx], r_x.at[layer, part, dx], {"x": xt},
                )
            )
        x_copies[layer, part] = copies

    def attend(layer, part):
        own = pl.ds(pl.multiple_of(x * HALF, HALF), HALF)
        total = acc[part, own, :]
        sq = squares[part, own, :][:, :1]
        for copy in x_copies[layer, part]:
            copy.wait()
        for dx in STEPS:
            total = total + rbuf[part, dx, :, :PW].astype(F32)
            tail = rbuf[part, dx, :, PW:].astype(F32)
            sq = sq + tail[:, :1] + tail[:, 64:65]
        projected = (total * lax.rsqrt(sq / D + EPSILON)).astype(BF)
        kv[part * HALF : (part + 1) * HALF, :] = projected[:, QW:]
        seen = (part + 1) * HALF
        keys = kv[:seen, :HD]
        values = kv[:seen, HD:]
        queries = jnp.concatenate(
            [projected[:, head * HD : (head + 1) * HD] for head in range(HEADS)], axis=0
        )
        at = iota((HALF, seen), 0) + part * HALF
        key_at = iota((HALF, seen), 1)
        allowed = jnp.where(
            (segments(at, lengths) == segments(key_at, lengths)) & (at >= key_at), 1.0, 0.0
        )
        allowed = jnp.concatenate([allowed] * HEADS, axis=0) > 0.5
        scores = lax.dot_general(
            queries, keys, (((1,), (1,)), ((), ())), preferred_element_type=F32
        ) * (1.0 / math.sqrt(HD))
        scores = jnp.where(allowed, scores, -1e30)
        top = jnp.max(scores, axis=1, keepdims=True)
        weights = jnp.exp(scores - top)
        weights = (weights / jnp.sum(weights, axis=1, keepdims=True)).astype(BF)
        mixed = jnp.dot(weights, values, preferred_element_type=F32).astype(BF)
        for head in range(HEADS):
            abuf[part, x, :, head * HD : (head + 1) * HD] = mixed[
                head * HALF : (head + 1) * HALF, :
            ]
        a_copies[layer, part] = [
            push(
                abuf.at[part, x], abuf.at[part, x],
                s_a.at[layer, part, dx], r_a.at[layer, part, dx], {"x": along(x, dx)},
            )
            for dx in STEPS
        ]

    def output(layer, part):
        for copy in a_copies[layer, part]:
            copy.wait()
        copies = {}

        def send(name, src, dst, dz):
            copies[name] = push(
                src, dst, s_o.at[layer, part, name], r_o.at[layer, part, name],
                {"mp": along(z, dz)},
            )

        for dz in (2, 1, 3, 0):
            zt = along(z, dz)

            osend[part, dz] = lax.dot_general(
                abuf[part].reshape(rows, QW), w[layer, zt, :, PW:],
                (((1,), (1,)), ((), ())), preferred_element_type=F32,
            ).astype(BF)

            if dz == 2:
                send(0, osend.at[part, 2, left], orel.at[part, 0], 1)
                send(1, osend.at[part, 2, right], orel.at[part, 1], 3)
            elif dz == 1:
                send(2, osend.at[part, 1, right], orec.at[part, 0, right], 1)
            elif dz == 3:
                send(3, osend.at[part, 3, left], orec.at[part, 1, left], 3)
        o_copies[layer, part] = copies, send

    def relay(layer, part):
        copies, send = o_copies[layer, part]
        copies[0].wait()
        osend[part, 1, left] = (
            osend[part, 1, left].astype(F32) + orel[part, 0].astype(F32)
        ).astype(BF)
        send(4, osend.at[part, 1, left], orec.at[part, 0, left], 1)
        copies[1].wait()
        osend[part, 3, right] = (
            osend[part, 3, right].astype(F32) + orel[part, 1].astype(F32)
        ).astype(BF)
        send(5, osend.at[part, 3, right], orec.at[part, 1, right], 3)

    def finish(layer, part):
        update = osend[part, 0].astype(F32)
        copies, _ = o_copies[layer, part]
        for name in (2, 3, 4, 5):
            copies[name].wait()
        for side in range(2):
            update = update + orec[part, side].astype(F32)
        fresh = (zbuf[part, z].astype(F32) + update).astype(BF)
        if layer == 0:
            zbuf[part, z] = fresh
            return
        osend[part, 0] = fresh
        for dx in STEPS:
            xt = along(x, dx)
            e_copies.append(
                push(
                    osend.at[part, 0, pl.ds(pl.multiple_of(xt * HALF, HALF), HALF), :],
                    obuf.at[x, part],
                    s_e.at[part, dx], r_e.at[part, dx], {"x": xt},
                )
            )
        obuf[x, part] = osend[part, 0, pl.ds(pl.multiple_of(x * HALF, HALF), HALF), :
        ]

    spread(0, 0)
    g_copies, gz_copies = [], []

    def ready_qkv(layer, part):
        only(0, qkv_w[2])
        only(1, qkv_w[3])

    def ready_out(layer, part):
        only(0, out_w[2])
        only(1, last_q[1], last_o[0], out_w[3])

    def pass_out(layer, part):
        only(0, out_w[1])
        only(1, last_q[0])

    def ready_last(layer, part):
        only(1, last_q[2], last_o[1])
        only(0, last_q[3])

    def ready_end(layer, part):
        only(1, last_o[2])
        only(0, last_o[3])

    def choose(layer, part):
        own_grads.wait()
        for copy in grad_copies:
            copy.wait()
        for dy in (1, 3, 2, 0):
            yt = along(y, dy)
            wanted = gslot[pl.ds(pl.multiple_of(yt * 64, 64), 64), :1]
            chosen = one_hot(iota((64, SIDE * TOK), 1) == wanted)
            gsend[dy] = jnp.dot(
                chosen, gbuf[...].reshape(SIDE * TOK, width), preferred_element_type=F32
            ).astype(BF)
            if dy:
                g_copies.append(
                    push(gsend.at[dy], grec.at[dy], s_gy.at[dy], r_gy.at[dy], {"y": yt})
                )

    def hand(layer, part):
        for copy in g_copies:
            copy.wait()
        found = gsend[0].astype(F32)
        for dy in STEPS:
            found = found + grec[dy].astype(F32)
        gz[...] = found.astype(BF).reshape(SIDE, UNITS, width)
        for dz in STEPS:
            zt = along(z, dz)
            gz_copies.append(
                push(gz.at[zt], mz.at[z], s_gz.at[dz], r_gz.at[dz], {"mp": zt})
            )
        mz[z] = gz[z]

    for stage, layer, part_at in (
        (ready_qkv, 0, 0),
        (own_part, 0, 0),
        (passed, 0, 0),
        (spread, 0, 1),
        (project, 0, 0),
        (pass_out, 0, 0),
        (own_part, 0, 1),
        (attend, 0, 0),
        (passed, 0, 1),
        (project, 0, 1),
        (ready_out, 0, 0),
        (output, 0, 0),
        (attend, 0, 1),
        (relay, 0, 0),
        (output, 0, 1),
        (finish, 0, 0),
        (spread, 1, 0),
        (relay, 0, 1),
        (ready_last, 1, 0),
        (own_part, 1, 0),
        (finish, 0, 1),
        (passed, 1, 0),
        (spread, 1, 1),
        (project, 1, 0),
        (own_part, 1, 1),
        (attend, 1, 0),
        (choose, 1, 0),
        (passed, 1, 1),
        (project, 1, 1),
        (ready_end, 1, 0),
        (output, 1, 0),
        (attend, 1, 1),
        (relay, 1, 0),
        (output, 1, 1),
        (hand, 1, 0),
        (finish, 1, 0),
        (relay, 1, 1),
        (finish, 1, 1),
    ):
        stage(layer, part_at)

    for copy in gz_copies:
        copy.wait()
    for block in range(SIDE):
        mg[:, block * width : (block + 1) * width] = mz[block]
    for copy in e_copies:
        copy.wait()
    for block in range(SIDE):
        for part_of in range(2):
            out[part_of * HALF : (part_of + 1) * HALF, block * FB : (block + 1) * FB] = obuf[
                block, part_of
            ]
    merge_w[4]()
    only(0, qkv_w[4], out_w[4])
    only(1, last_q[4], last_o[4])


def shards(*arrays):
    vmem = pl.BlockSpec(memory_space=pltpu.VMEM)
    smem = pl.BlockSpec(memory_space=pltpu.SMEM)
    hbm = pl.BlockSpec(memory_space=pl.ANY)
    dma = pltpu.SemaphoreType.DMA
    rows = SIDE * HALF
    width = arrays[13].shape[1]
    half = arrays[6].shape[0] // 2
    stage = dma((2, 2, SIDE))
    four, plane = dma((SIDE,)), dma((SIDE * SIDE,))
    call = pl.pallas_call(
        whole_kernel,
        out_shape=(
            jax.ShapeDtypeStruct((TOK, SIDE * FB), BF),
            jax.ShapeDtypeStruct((UNITS, SIDE * width), BF),
        ),
        in_specs=[vmem, smem, vmem, hbm, hbm, vmem, hbm, smem, hbm, smem, vmem, hbm, hbm, hbm],
        out_specs=(vmem, vmem),
        scratch_shapes=[
            pltpu.VMEM((SLOTS, VD, TILE), BF),
            pltpu.VMEM((FB, PW), BF),
            pltpu.VMEM((SIDE, 2, half, SIDE * FB), BF),
            pltpu.VMEM((2, SIDE, FB, PW + QW), BF),
            pltpu.VMEM((PATCH, 3 * VD), BF),
            pltpu.VMEM((VH * PATCH, PATCH), F32),
            pltpu.VMEM((VH * PATCH, PATCH), BF),
            pltpu.VMEM((PATCH, VD), F32),
            pltpu.VMEM((PATCH, VD), F32),
            pltpu.VMEM((SIDE, SIDE, UNITS, PADDED), BF),
            pltpu.VMEM((SIDE * SIDE, SIDE, UNITS, PADDED), BF),
            pltpu.VMEM((256, FB), F32),
            pltpu.VMEM((SIDE, 256, FB), BF),
            pltpu.VMEM((SIDE, 256, FB), BF),
            pltpu.VMEM((SIDE, 256, FB), BF),
            pltpu.VMEM((SIDE, TOK, FB), BF),
            pltpu.VMEM((SIDE * TOK, COUNT), BF),
            pltpu.VMEM((1, COUNT), jnp.int32),
            pltpu.VMEM((SIDE * SIDE, 1, COUNT), jnp.int32),
            pltpu.VMEM((SIDE, 1, COUNT), jnp.int32),
            pltpu.VMEM((COUNT, COUNT), BF),
            pltpu.VMEM((1, COUNT), jnp.int32),
            pltpu.VMEM((256, 128), jnp.int32),
            pltpu.VMEM((2, SIDE, rows, FB), BF),
            pltpu.VMEM((2, rows, PW), F32),
            pltpu.VMEM((2, rows, HD), F32),
            pltpu.VMEM((TOK, 2 * HD), BF),
            pltpu.VMEM((2, SIDE, HALF, PT), BF),
            pltpu.VMEM((2, SIDE, HALF, PT), BF),
            pltpu.VMEM((2, SIDE, HALF, QW), BF),
            pltpu.VMEM((2, SIDE, rows, FB), BF),
            pltpu.VMEM((2, 2, rows, FB), BF),
            pltpu.VMEM((2, 2, rows // 2, FB), BF),
            pltpu.VMEM((SIDE, 2, HALF, FB), BF),
            pltpu.VMEM((SIDE, TOK, width), BF),
            pltpu.VMEM((SIDE, 64, width), BF),
            pltpu.VMEM((SIDE, 64, width), BF),
            pltpu.VMEM((SIDE, UNITS, width), BF),
            pltpu.VMEM((SIDE, UNITS, width), BF),
            dma((SLOTS,)), dma((5,)), dma((5, 8)), dma((5, 8)),
            plane, plane, four, four, plane, plane, four, four, four, four, four, four,
            stage, stage, stage, stage, stage, stage, dma((2, 2, 6)), dma((2, 2, 6)),
            dma((2, SIDE)), dma((2, SIDE)),
            four, four, four, four, four, four,
        ],
        compiler_params=pltpu.CompilerParams(
            collective_id=1, has_side_effects=True, vmem_limit_bytes=VMEM_LIMIT
        ),
        name="whole",
    )
    return call(*arrays)


def solution(mesh):
    grid = jax.sharding.Mesh(
        mesh.devices.reshape(2, SIDE, SIDE, SIDE), ("section", "y", "x", "mp")
    )
    every = ("section", "y", "x", "mp")
    home = P(("section", "y", "x"), "mp")
    in_specs = (
        P(every, None),
        P(every, None),
        P(),
        P(),
        P(),
        P(),
        P(("y", "x"), "mp"),
        P(every, None),
        home,
        P(("section", "y", "x"), None),
        P("section", None),
        P("section", ("y", "x"), "mp"),
        P("section", ("y", "x"), "mp"),
        home,
    )
    out_specs = (home, P(every, None))
    return jax.shard_map(shards, mesh=grid, in_specs=in_specs, out_specs=out_specs, check_vma=False)
```

```python
import functools
import math

import jax
import jax.numpy as jnp
from jax import lax
from jax.experimental import pallas as pl
from jax.experimental.pallas import tpu as pltpu
from jax.sharding import PartitionSpec as P

QH = 32
KVH = 4
HD = 128
VD = 1280
VH = 16
VHD = 80
SIDE = 4
TOK = 128
HALF = TOK // 2
STEPS = (1, 3, 2)
FB = 512
HEADS = QH // KVH
QW = HEADS * HD
PW = QW + 2 * HD
PT = PW + HD
D = 8192
PATCH = 64
UNITS = 16
PIECE = VD // SIDE
PADDED = 384
COUNT = 1024
TILE = 256
SLOTS = 6
EPSILON = 1e-06
VMEM_LIMIT = 62 * 1024 * 1024
BF = jnp.bfloat16
F32 = jnp.float32
MESH = pl.DeviceIdType.MESH


def layer_norm(values, norm_gain):
    centre = jnp.mean(values, axis=-1, keepdims=True)
    centred = values - centre
    variance = jnp.mean(centred * centred, axis=-1, keepdims=True)
    return centred * lax.rsqrt(variance + EPSILON) * norm_gain


def remote(src, dst, send_sem, recv_sem, where):
    return pltpu.make_async_remote_copy(
        src_ref=src, dst_ref=dst, send_sem=send_sem, recv_sem=recv_sem,
        device_id=where, device_id_type=MESH,
    )


def push(src, dst, send_sem, recv_sem, where):
    copy = remote(src, dst, send_sem, recv_sem, where)
    copy.start()
    return copy


def greet(partners):
    barrier = pltpu.get_barrier_semaphore()
    for where in partners:
        pl.semaphore_signal(barrier, inc=1, device_id=where, device_id_type=MESH)
    pl.semaphore_wait(barrier, len(partners))


def along(index, step):
    return lax.rem(index + step, SIDE)


def behind(index, step):
    return lax.rem(index + SIDE - step, SIDE)


def one_hot(condition):
    return jnp.where(condition, 1.0, 0.0).astype(BF)


def iota(shape, dimension):
    return lax.broadcasted_iota(jnp.int32, shape, dimension)


def segments(index, lengths):
    first = lengths[0, 0]
    second = first + lengths[0, 1]
    return jnp.where(index >= first, 1, 0) + jnp.where(index >= second, 1, 0)


def whole_kernel(
    patches, units, v_gain, v_qkv, v_out, merge_gain, w_merge, routes, text, lengths,
    lang_gain, w_qkv, wo_t, grads,
    out, mg,
    ring, wraw, wmv, w, v_proj, v_scores, v_weights, v_att, v_hidden, pieces, xbuf, part, msend, mrecv, ybuf, tbuf, pick,
    placed, rt, ry, tri, line, gslot,
    zbuf, acc, squares, kv, psend, rbuf, abuf, osend, orec, orel, obuf,
    gbuf, gsend, grec, gz, mz,
    v_sem, l_sem, s_w, r_w, s_rt, r_rt, s_ry, r_ry, s_pl, r_pl, s_mx, r_mx, s_my, r_my, s_t, r_t,
    s_z, r_z, s_x, r_x, s_a, r_a, s_o, r_o, s_e, r_e,
    s_g, r_g, s_gy, r_gy, s_gz, r_gz,
):
    section = lax.axis_index("section")
    x = lax.axis_index("x")
    y = lax.axis_index("y")
    z = lax.axis_index("mp")
    twin = {"section": 1 - section}
    rows = SIDE * HALF
    width = grads.shape[1]
    half = wmv.shape[2]
    plane = [(dx, dz) for dx in range(SIDE) for dz in range(SIDE) if dx or dz]
    left = slice(0, rows // 2)
    right = slice(rows // 2, rows)

    own_merge = pltpu.make_async_copy(
        w_merge.at[pl.ds(pl.multiple_of(section * half, half), half), :],
        wmv.at[y, section], l_sem.at[0],
    )
    own_merge.start()
    v_tiles = [
        pltpu.make_async_copy(
            (v_qkv if tile < 15 else v_out).at[:, pl.ds((tile if tile < 15 else tile - 15) * TILE, TILE)],
            ring.at[tile % SLOTS], v_sem.at[tile % SLOTS],
        )
        for tile in range(20)
    ]
    for tile in range(SLOTS):
        v_tiles[tile].start()
    raw_load = pltpu.make_async_copy(w_qkv.at[0], wraw, l_sem.at[1])
    raw_load.start()
    own_out = pltpu.make_async_copy(
        wo_t.at[0], w.at[section, y, :, pl.ds(PW, QW)], l_sem.at[2]
    )
    own_out.start()
    own_text = pltpu.make_async_copy(
        text.at[:, pl.ds(pl.multiple_of(x * FB, FB), FB)], tbuf.at[x], l_sem.at[3]
    )
    own_text.start()
    own_grads = pltpu.make_async_copy(grads, gbuf.at[x], l_sem.at[4])
    own_grads.start()

    lane = iota((1, COUNT), 1)
    base = ((y * SIDE + x) * SIDE + z) * UNITS
    row = jnp.zeros((1, COUNT), jnp.int32)
    for unit in range(UNITS):
        row = jnp.where(lane == base + unit, routes[unit, 0], row)
    placed[...] = row
    rt[x * SIDE + z] = row

    greet(
        [{"x": along(x, dx), "mp": along(z, dz)} for dx, dz in plane]
        + [{"y": along(y, dy)} for dy in STEPS]
        + [twin]
    )

    def shared(number, block, low, high):
        def own_copy(dy):
            return remote(
                block(y), block(y), s_w.at[number, dy], r_w.at[number, dy], {"y": along(y, dy)}
            )

        def up_copy():
            ref = low(behind(y, 1))
            return remote(ref, ref, s_w.at[number, 0], r_w.at[number, 0], {"y": along(y, 1)})

        def down_copy():
            ref = high(along(y, 1))
            return remote(ref, ref, s_w.at[number, 2], r_w.at[number, 2], {"y": along(y, 3)})

        def twin_copy(source):
            return remote(
                block(source), block(source), s_w.at[number, SIDE + source],
                r_w.at[number, SIDE + source], twin,
            )

        def begin():
            own_copy(1).start()
            own_copy(3).start()
            twin_copy(y).start()

        def middle():
            own_copy(1).wait()
            up_copy().start()
            own_copy(3).wait()
            down_copy().start()
            twin_copy(behind(y, 1)).start()
            twin_copy(along(y, 1)).start()

        def end():
            up_copy().wait()
            down_copy().wait()
            twin_copy(along(y, 2)).start()

        def taken():
            for source in range(SIDE):
                twin_copy(source).wait_recv()

        def given():
            for source in range(SIDE):
                twin_copy(source).wait_send()

        return begin, middle, end, taken, given

    mid = wmv.shape[3] // 2
    merge_w = shared(
        0,
        lambda ys: wmv.at[ys, section],
        lambda ys: wmv.at[ys, section, :, pl.ds(0, mid)],
        lambda ys: wmv.at[ys, section, :, pl.ds(mid, mid)],
    )

    def layer_shard(number, layer, first, amount):
        cols = pl.ds(first, amount)
        return shared(
            number,
            lambda ys: w.at[layer, ys, :, cols],
            lambda ys: w.at[layer, ys, pl.ds(0, FB // 2), cols],
            lambda ys: w.at[layer, ys, pl.ds(FB // 2, FB // 2), cols],
        )

    qkv_w = layer_shard(1, 0, 0, PW)
    out_w = layer_shard(2, 0, PW, QW)
    last_q = layer_shard(3, 1, 0, PW)
    last_o = layer_shard(4, 1, PW, QW)

    def only(at, *actions):
        @pl.when(section == at)
        def _():
            for action in actions:
                action()

    own_merge.wait()
    merge_w[0]()
    route_copies = [
        push(
            placed, rt.at[x * SIDE + z], s_rt.at[dx * SIDE + dz], r_rt.at[dx * SIDE + dz],
            {"x": along(x, dx), "mp": along(z, dz)},
        )
        for dx, dz in plane
    ]
    text_copies = []
    for dx in STEPS:
        xt = along(x, dx)
        text_copies.append(
            push(
                text.at[:, pl.ds(pl.multiple_of(xt * FB, FB), FB)], tbuf.at[x],
                s_t.at[dx], r_t.at[dx], {"x": xt},
            )
        )

    order = iota((PATCH, PATCH), 0)
    swap = one_hot(iota((PATCH, PATCH), 1) == (order & 15) * SIDE + (order >> 4))
    patch = jnp.dot(swap, patches[...], preferred_element_type=F32)
    normed = layer_norm(patch, v_gain[...].reshape(1, VD)).astype(BF)
    for tile in range(15):
        v_tiles[tile].wait()
        v_proj[:, tile * TILE : (tile + 1) * TILE] = jnp.dot(
            normed, ring[tile % SLOTS], preferred_element_type=F32
        ).astype(BF)
        if tile + SLOTS < 20:
            v_tiles[tile + SLOTS].start()

    windows = []
    for head in range(VH):
        start = min(head * VHD // 128 * 128, VD - 256)
        lanes = iota((PATCH, 256), 1) + start
        windows.append((start, (lanes >= head * VHD) & (lanes < (head + 1) * VHD)))
    for head, (start, inside) in enumerate(windows):
        query = v_proj[:, start : start + 256].astype(F32)
        query = jnp.where(inside, query, 0.0).astype(BF)
        key = v_proj[:, VD + start : VD + start + 256]
        v_scores[head * PATCH : (head + 1) * PATCH, :] = lax.dot_general(
            query, key, (((1,), (1,)), ((), ())), preferred_element_type=F32
        )
    image_q = segments(iota((VH * PATCH, PATCH), 0) & 15, units)
    image_k = segments(iota((VH * PATCH, PATCH), 1) & 15, units)
    scores = jnp.where(image_q == image_k, v_scores[...] / math.sqrt(VHD), -1e30)
    top = jnp.max(scores, axis=1, keepdims=True)
    weights = jnp.exp(scores - top)
    v_weights[...] = (weights / jnp.sum(weights, axis=1, keepdims=True)).astype(BF)
    v_att[...] = jnp.zeros((PATCH, VD), F32)
    for head, (start, inside) in enumerate(windows):
        mixed = jnp.dot(
            v_weights[head * PATCH : (head + 1) * PATCH, :],
            v_proj[:, 2 * VD + start : 2 * VD + start + 256],
            preferred_element_type=F32,
        )
        v_att[:, start : start + 256] += jnp.where(inside, mixed, 0.0)
    attended = v_att[...].astype(BF)
    for tile in range(5):
        v_tiles[15 + tile].wait()
        cols = slice(tile * TILE, (tile + 1) * TILE)
        v_hidden[:, cols] = (
            patch[:, cols]
            + jnp.dot(attended, ring[(15 + tile) % SLOTS], preferred_element_type=F32)
        ).astype(BF).astype(F32)
    merged = layer_norm(v_hidden[...], merge_gain[...].reshape(1, VD))
    for block in range(SIDE):
        pieces[block, :, :, :PIECE] = merged[:, block * PIECE : (block + 1) * PIECE].astype(BF).reshape(
            SIDE, UNITS, PIECE
        )
        pieces[block, :, :, PIECE:] = jnp.zeros((SIDE, UNITS, PADDED - PIECE), BF)
    plane_copies = []
    for dx, dz in plane:
        xt = along(x, dx)
        plane_copies.append(
            push(
                pieces.at[xt], xbuf.at[x * SIDE + z],
                s_pl.at[dx * SIDE + dz], r_pl.at[dx * SIDE + dz],
                {"x": xt, "mp": along(z, dz)},
            )
        )
    xbuf[x * SIDE + z] = pieces[x]

    merge_w[1]()
    raw_load.wait()
    shard = y * SIDE + x
    gain = lang_gain[:, pl.ds(pl.multiple_of(shard * FB, FB), FB)]
    gain = jnp.transpose(jnp.broadcast_to(gain, (128, FB)))
    for tile in range(PW // 128):
        cols = slice(tile * 128, (tile + 1) * 128)
        w[section, y, :, cols] = (wraw[:, cols].astype(F32) * gain).astype(BF)
    own_out.wait()
    only(0, qkv_w[0])

    for block in range(SIDE):
        before = iota((256, COUNT), 0) + block * 256
        tri[block * 256 : (block + 1) * 256, :] = one_hot(before < iota((256, COUNT), 1))
    for copy in route_copies:
        copy.wait()
    known = rt[0]
    for source in range(1, SIDE * SIDE):
        known = known + rt[source]
    ry[y] = known
    ry_copies = [
        push(ry.at[y], ry.at[y], s_ry.at[dy], r_ry.at[dy], {"y": along(y, dy)})
        for dy in STEPS
    ]
    for copy in plane_copies:
        copy.wait()
    merge_w[2]()
    merge_w[3]()

    def product(dx):
        cols = pl.ds(pl.multiple_of(along(x, dx) * FB, FB), FB)
        total = None
        for patch_at in range(SIDE):
            piece = xbuf[:, patch_at].reshape(SIDE * SIDE * UNITS, PADDED)[:, :PIECE]
            weights = wmv[patch_at, :, :, cols].reshape(PIECE, FB)
            term = jnp.dot(piece, weights, preferred_element_type=F32)
            total = term if total is None else total + term
        return total

    m_copies = []
    for dx in STEPS:
        msend[dx] = product(dx).astype(BF)
        m_copies.append(
            push(msend.at[dx], mrecv.at[dx], s_mx.at[dx], r_mx.at[dx], {"x": along(x, dx)})
        )
    part[...] = product(0)

    for copy in ry_copies:
        copy.wait()
    target = ry[0] + ry[1] + ry[2] + ry[3]
    named = jnp.where(iota((16, COUNT), 0) == target, 1.0, 0.0)
    earlier = jnp.dot(named.astype(BF), tri[...], preferred_element_type=F32)
    position = jnp.sum(named * earlier, axis=0, keepdims=True).astype(jnp.int32)
    slots = (target - y * SIDE) * TOK + position
    for block in range(SIDE):
        wanted = iota((TOK, COUNT), 0) + block * TOK
        pick[block * TOK : (block + 1) * TOK, :] = one_hot(wanted == slots)
    line[...] = jnp.where((target >> 2) == y, (target & 3) * TOK + position + 1, 0)
    down = iota((256, COUNT), 0)
    chosen_rows = one_hot(iota((256, COUNT), 1) == (down >> 6) * 256 + x * 64 + (down & 63))

    def upright(values):
        wide = jnp.broadcast_to(values.astype(F32), (128, COUNT)).astype(BF)
        return lax.dot_general(
            chosen_rows, wide, (((1,), (1,)), ((), ())), preferred_element_type=F32
        )

    slot_line = line[...]
    gslot[...] = (
        16.0 * upright(slot_line >> 4) + upright(slot_line & 15)
    ).astype(jnp.int32) - 1

    only(0, qkv_w[1])
    for copy in m_copies:
        copy.wait()
    grad_copies = [
        push(grads, gbuf.at[x], s_g.at[dx], r_g.at[dx], {"x": along(x, dx)}) for dx in (1, 3)
    ]
    total = part[...]
    for dx in STEPS:
        total = total + mrecv[dx].astype(F32)
    ybuf[y] = total.astype(BF)
    y_copies = [
        push(ybuf.at[y], ybuf.at[y], s_my.at[dy], r_my.at[dy], {"y": along(y, dy)})
        for dy in STEPS
    ]
    present = jnp.dot(pick[...], jnp.ones((COUNT, 128), BF), preferred_element_type=F32)
    own_text.wait()
    for copy in text_copies:
        copy.wait()
    for copy in y_copies:
        copy.wait()
    only(0, out_w[0])
    picked = jnp.dot(
        pick[...], ybuf[...].reshape(COUNT, FB), preferred_element_type=F32
    ).astype(BF)
    for group in range(SIDE):
        for part_of in range(2):
            span = slice(group * TOK + part_of * HALF, group * TOK + (part_of + 1) * HALF)
            to = slice(group * HALF, (group + 1) * HALF)
            inside = slice(part_of * HALF, (part_of + 1) * HALF)
            for tile in range(FB // 128):
                cols = slice(tile * 128, (tile + 1) * 128)
                zbuf[part_of, z, to, cols] = jnp.where(
                    present[span, :] > 0.5, picked[span, cols], tbuf[group, inside, cols]
                )

    z_copies, f_copies, x_copies, a_copies, o_copies, e_copies = {}, {}, {}, {}, {}, []

    def spread(layer, part):
        z_copies[layer, part] = {
            dz: push(
                zbuf.at[part, z], zbuf.at[part, z],
                s_z.at[layer, part, dz], r_z.at[layer, part, dz], {"mp": along(z, dz)},
            )
            for dz in (1, 3)
        }

    def times(layer, part, dz):
        zs = behind(z, dz)
        wide = zbuf[part, zs].astype(F32)
        squared = jnp.sum(wide * wide, axis=1, keepdims=True)
        if dz:
            squares[part] += jnp.broadcast_to(squared, (rows, HD))
        else:
            squares[part] = jnp.broadcast_to(squared, (rows, HD))

        product = jnp.dot(
            zbuf[part, zs], w[layer, zs, :, :PW], preferred_element_type=F32
        )
        if dz:
            acc[part] += product
        else:
            acc[part] = product

    def passed(layer, part):
        copies = z_copies[layer, part]
        copies[1].wait()
        zs = behind(z, 1)
        f_copies[layer, part] = [
            push(
                zbuf.at[part, zs, left], zbuf.at[part, zs, left],
                s_z.at[layer, part, 0], r_z.at[layer, part, 0], {"mp": along(z, 1)},
            )
        ]
        copies[3].wait()
        zs = along(z, 1)
        f_copies[layer, part].append(
            push(
                zbuf.at[part, zs, right], zbuf.at[part, zs, right],
                s_z.at[layer, part, 2], r_z.at[layer, part, 2], {"mp": along(z, 3)},
            )
        )

    def own_part(layer, part):
        times(layer, part, 0)

    def project(layer, part):
        times(layer, part, 1)
        times(layer, part, 3)
        for copy in f_copies[layer, part]:
            copy.wait()
        times(layer, part, 2)
        lane = lax.broadcasted_iota(jnp.int32, (HALF, HD), 1)
        copies = []
        for dx in STEPS:
            xt = along(x, dx)
            span = pl.ds(pl.multiple_of(xt * HALF, HALF), HALF)
            psend[part, dx, :, :PW] = acc[part, span, :].astype(BF)
            sq = squares[part, span, :]
            high = sq.astype(BF)
            low = (sq - high.astype(F32)).astype(BF)
            psend[part, dx, :, PW:] = jnp.where(lane < 64, high, low)
            copies.append(
                push(
                    psend.at[part, dx], rbuf.at[part, dx],
                    s_x.at[layer, part, dx], r_x.at[layer, part, dx], {"x": xt},
                )
            )
        x_copies[layer, part] = copies

    def attend(layer, part):
        own = pl.ds(pl.multiple_of(x * HALF, HALF), HALF)
        total = acc[part, own, :]
        sq = squares[part, own, :][:, :1]
        for copy in x_copies[layer, part]:
            copy.wait()
        for dx in STEPS:
            total = total + rbuf[part, dx, :, :PW].astype(F32)
            tail = rbuf[part, dx, :, PW:].astype(F32)
            sq = sq + tail[:, :1] + tail[:, 64:65]
        projected = (total * lax.rsqrt(sq / D + EPSILON)).astype(BF)
        kv[part * HALF : (part + 1) * HALF, :] = projected[:, QW:]
        seen = (part + 1) * HALF
        keys = kv[:seen, :HD]
        values = kv[:seen, HD:]
        queries = jnp.concatenate(
            [projected[:, head * HD : (head + 1) * HD] for head in range(HEADS)], axis=0
        )
        at = iota((HALF, seen), 0) + part * HALF
        key_at = iota((HALF, seen), 1)
        allowed = jnp.where(
            (segments(at, lengths) == segments(key_at, lengths)) & (at >= key_at), 1.0, 0.0
        )
        allowed = jnp.concatenate([allowed] * HEADS, axis=0) > 0.5
        scores = lax.dot_general(
            queries, keys, (((1,), (1,)), ((), ())), preferred_element_type=F32
        ) * (1.0 / math.sqrt(HD))
        scores = jnp.where(allowed, scores, -1e30)
        top = jnp.max(scores, axis=1, keepdims=True)
        weights = jnp.exp(scores - top)
        weights = (weights / jnp.sum(weights, axis=1, keepdims=True)).astype(BF)
        mixed = jnp.dot(weights, values, preferred_element_type=F32).astype(BF)
        for head in range(HEADS):
            abuf[part, x, :, head * HD : (head + 1) * HD] = mixed[
                head * HALF : (head + 1) * HALF, :
            ]
        a_copies[layer, part] = [
            push(
                abuf.at[part, x], abuf.at[part, x],
                s_a.at[layer, part, dx], r_a.at[layer, part, dx], {"x": along(x, dx)},
            )
            for dx in STEPS
        ]

    def output(layer, part):
        for copy in a_copies[layer, part]:
            copy.wait()
        copies = {}

        def send(name, src, dst, dz):
            copies[name] = push(
                src, dst, s_o.at[layer, part, name], r_o.at[layer, part, name],
                {"mp": along(z, dz)},
            )

        for dz in (2, 1, 3, 0):
            zt = along(z, dz)

            osend[part, dz] = lax.dot_general(
                abuf[part].reshape(rows, QW), w[layer, zt, :, PW:],
                (((1,), (1,)), ((), ())), preferred_element_type=F32,
            ).astype(BF)

            if dz == 2:
                send(0, osend.at[part, 2, left], orel.at[part, 0], 1)
                send(1, osend.at[part, 2, right], orel.at[part, 1], 3)
            elif dz == 1:
                send(2, osend.at[part, 1, right], orec.at[part, 0, right], 1)
            elif dz == 3:
                send(3, osend.at[part, 3, left], orec.at[part, 1, left], 3)
        o_copies[layer, part] = copies, send

    def relay(layer, part):
        copies, send = o_copies[layer, part]
        copies[0].wait()
        osend[part, 1, left] = (
            osend[part, 1, left].astype(F32) + orel[part, 0].astype(F32)
        ).astype(BF)
        send(4, osend.at[part, 1, left], orec.at[part, 0, left], 1)
        copies[1].wait()
        osend[part, 3, right] = (
            osend[part, 3, right].astype(F32) + orel[part, 1].astype(F32)
        ).astype(BF)
        send(5, osend.at[part, 3, right], orec.at[part, 1, right], 3)

    def finish(layer, part):
        update = osend[part, 0].astype(F32)
        copies, _ = o_copies[layer, part]
        for name in (2, 3, 4, 5):
            copies[name].wait()
        for side in range(2):
            update = update + orec[part, side].astype(F32)
        fresh = (zbuf[part, z].astype(F32) + update).astype(BF)
        if layer == 0:
            zbuf[part, z] = fresh
            return
        osend[part, 0] = fresh
        for dx in STEPS:
            xt = along(x, dx)
            e_copies.append(
                push(
                    osend.at[part, 0, pl.ds(pl.multiple_of(xt * HALF, HALF), HALF), :],
                    obuf.at[x, part],
                    s_e.at[part, dx], r_e.at[part, dx], {"x": xt},
                )
            )
        obuf[x, part] = osend[part, 0, pl.ds(pl.multiple_of(x * HALF, HALF), HALF), :
        ]

    spread(0, 0)
    grad_copies[0].wait()
    from_left = gbuf.at[behind(x, 1), pl.ds(0, HALF), :]
    grad_copies[1].wait()
    from_right = gbuf.at[along(x, 1), pl.ds(HALF, HALF), :]
    grad_copies = [
        push(from_left, from_left, s_g.at[0], r_g.at[0], {"x": along(x, 1)}),
        push(from_right, from_right, s_g.at[2], r_g.at[2], {"x": along(x, 3)}),
    ]
    g_copies, gz_copies = [], []

    def ready_qkv(layer, part):
        only(0, qkv_w[2])
        only(1, qkv_w[3])

    def ready_out(layer, part):
        only(0, out_w[2])
        only(1, last_q[1], last_o[0], out_w[3])

    def pass_out(layer, part):
        only(0, out_w[1])
        only(1, last_q[0])

    def ready_last(layer, part):
        only(1, last_q[2], last_o[1])
        only(0, last_q[3])

    def ready_end(layer, part):
        only(1, last_o[2])
        only(0, last_o[3])

    def choose(layer, part):
        own_grads.wait()
        for copy in grad_copies:
            copy.wait()
        for dy in (1, 3, 2, 0):
            yt = along(y, dy)
            wanted = gslot[pl.ds(pl.multiple_of(yt * 64, 64), 64), :1]
            chosen = one_hot(iota((64, SIDE * TOK), 1) == wanted)
            gsend[dy] = jnp.dot(
                chosen, gbuf[...].reshape(SIDE * TOK, width), preferred_element_type=F32
            ).astype(BF)
            if dy:
                g_copies.append(
                    push(gsend.at[dy], grec.at[dy], s_gy.at[dy], r_gy.at[dy], {"y": yt})
                )

    def hand(layer, part):
        for copy in g_copies:
            copy.wait()
        found = gsend[0].astype(F32)
        for dy in STEPS:
            found = found + grec[dy].astype(F32)
        gz[...] = found.astype(BF).reshape(SIDE, UNITS, width)
        for dz in STEPS:
            zt = along(z, dz)
            gz_copies.append(
                push(gz.at[zt], mz.at[z], s_gz.at[dz], r_gz.at[dz], {"mp": zt})
            )
        mz[z] = gz[z]

    for stage, layer, part_at in (
        (ready_qkv, 0, 0),
        (own_part, 0, 0),
        (passed, 0, 0),
        (spread, 0, 1),
        (project, 0, 0),
        (pass_out, 0, 0),
        (own_part, 0, 1),
        (attend, 0, 0),
        (passed, 0, 1),
        (project, 0, 1),
        (ready_out, 0, 0),
        (output, 0, 0),
        (attend, 0, 1),
        (relay, 0, 0),
        (output, 0, 1),
        (finish, 0, 0),
        (spread, 1, 0),
        (relay, 0, 1),
        (ready_last, 1, 0),
        (own_part, 1, 0),
        (passed, 1, 0),
        (finish, 0, 1),
        (spread, 1, 1),
        (project, 1, 0),
        (own_part, 1, 1),
        (attend, 1, 0),
        (choose, 1, 0),
        (passed, 1, 1),
        (project, 1, 1),
        (ready_end, 1, 0),
        (output, 1, 0),
        (attend, 1, 1),
        (relay, 1, 0),
        (output, 1, 1),
        (hand, 1, 0),
        (finish, 1, 0),
        (relay, 1, 1),
        (finish, 1, 1),
    ):
        stage(layer, part_at)

    for copy in gz_copies:
        copy.wait()
    for block in range(SIDE):
        mg[:, block * width : (block + 1) * width] = mz[block]
    for copy in e_copies:
        copy.wait()
    for block in range(SIDE):
        for part_of in range(2):
            out[part_of * HALF : (part_of + 1) * HALF, block * FB : (block + 1) * FB] = obuf[
                block, part_of
            ]
    merge_w[4]()
    only(0, qkv_w[4], out_w[4])
    only(1, last_q[4], last_o[4])


def shards(*arrays):
    vmem = pl.BlockSpec(memory_space=pltpu.VMEM)
    smem = pl.BlockSpec(memory_space=pltpu.SMEM)
    hbm = pl.BlockSpec(memory_space=pl.ANY)
    dma = pltpu.SemaphoreType.DMA
    rows = SIDE * HALF
    width = arrays[13].shape[1]
    half = arrays[6].shape[0] // 2
    stage = dma((2, 2, SIDE))
    four, plane = dma((SIDE,)), dma((SIDE * SIDE,))
    call = pl.pallas_call(
        whole_kernel,
        out_shape=(
            jax.ShapeDtypeStruct((TOK, SIDE * FB), BF),
            jax.ShapeDtypeStruct((UNITS, SIDE * width), BF),
        ),
        in_specs=[vmem, smem, vmem, hbm, hbm, vmem, hbm, smem, hbm, smem, vmem, hbm, hbm, hbm],
        out_specs=(vmem, vmem),
        scratch_shapes=[
            pltpu.VMEM((SLOTS, VD, TILE), BF),
            pltpu.VMEM((FB, PW), BF),
            pltpu.VMEM((SIDE, 2, half, SIDE * FB), BF),
            pltpu.VMEM((2, SIDE, FB, PW + QW), BF),
            pltpu.VMEM((PATCH, 3 * VD), BF),
            pltpu.VMEM((VH * PATCH, PATCH), F32),
            pltpu.VMEM((VH * PATCH, PATCH), BF),
            pltpu.VMEM((PATCH, VD), F32),
            pltpu.VMEM((PATCH, VD), F32),
            pltpu.VMEM((SIDE, SIDE, UNITS, PADDED), BF),
            pltpu.VMEM((SIDE * SIDE, SIDE, UNITS, PADDED), BF),
            pltpu.VMEM((256, FB), F32),
            pltpu.VMEM((SIDE, 256, FB), BF),
            pltpu.VMEM((SIDE, 256, FB), BF),
            pltpu.VMEM((SIDE, 256, FB), BF),
            pltpu.VMEM((SIDE, TOK, FB), BF),
            pltpu.VMEM((SIDE * TOK, COUNT), BF),
            pltpu.VMEM((1, COUNT), jnp.int32),
            pltpu.VMEM((SIDE * SIDE, 1, COUNT), jnp.int32),
            pltpu.VMEM((SIDE, 1, COUNT), jnp.int32),
            pltpu.VMEM((COUNT, COUNT), BF),
            pltpu.VMEM((1, COUNT), jnp.int32),
            pltpu.VMEM((256, 128), jnp.int32),
            pltpu.VMEM((2, SIDE, rows, FB), BF),
            pltpu.VMEM((2, rows, PW), F32),
            pltpu.VMEM((2, rows, HD), F32),
            pltpu.VMEM((TOK, 2 * HD), BF),
            pltpu.VMEM((2, SIDE, HALF, PT), BF),
            pltpu.VMEM((2, SIDE, HALF, PT), BF),
            pltpu.VMEM((2, SIDE, HALF, QW), BF),
            pltpu.VMEM((2, SIDE, rows, FB), BF),
            pltpu.VMEM((2, 2, rows, FB), BF),
            pltpu.VMEM((2, 2, rows // 2, FB), BF),
            pltpu.VMEM((SIDE, 2, HALF, FB), BF),
            pltpu.VMEM((SIDE, TOK, width), BF),
            pltpu.VMEM((SIDE, 64, width), BF),
            pltpu.VMEM((SIDE, 64, width), BF),
            pltpu.VMEM((SIDE, UNITS, width), BF),
            pltpu.VMEM((SIDE, UNITS, width), BF),
            dma((SLOTS,)), dma((5,)), dma((5, 8)), dma((5, 8)),
            plane, plane, four, four, plane, plane, four, four, four, four, four, four,
            stage, stage, stage, stage, stage, stage, dma((2, 2, 6)), dma((2, 2, 6)),
            dma((2, SIDE)), dma((2, SIDE)),
            four, four, four, four, four, four,
        ],
        compiler_params=pltpu.CompilerParams(
            collective_id=1, has_side_effects=True, vmem_limit_bytes=VMEM_LIMIT
        ),
        name="whole",
    )
    return call(*arrays)


def solution(mesh):
    grid = jax.sharding.Mesh(
        mesh.devices.reshape(2, SIDE, SIDE, SIDE), ("section", "y", "x", "mp")
    )
    every = ("section", "y", "x", "mp")
    home = P(("section", "y", "x"), "mp")
    in_specs = (
        P(every, None),
        P(every, None),
        P(),
        P(),
        P(),
        P(),
        P(("y", "x"), "mp"),
        P(every, None),
        home,
        P(("section", "y", "x"), None),
        P("section", None),
        P("section", ("y", "x"), "mp"),
        P("section", ("y", "x"), "mp"),
        home,
    )
    out_specs = (home, P(every, None))
    return jax.shard_map(shards, mesh=grid, in_specs=in_specs, out_specs=out_specs, check_vma=False)
```

```python
import functools
import math

import jax
import jax.numpy as jnp
from jax import lax
from jax.experimental import pallas as pl
from jax.experimental.pallas import tpu as pltpu
from jax.sharding import PartitionSpec as P

QH = 32
KVH = 4
HD = 128
VD = 1280
VH = 16
VHD = 80
SIDE = 4
TOK = 128
HALF = TOK // 2
STEPS = (1, 3, 2)
FB = 512
HEADS = QH // KVH
QW = HEADS * HD
PW = QW + 2 * HD
PT = PW + HD
D = 8192
PATCH = 64
UNITS = 16
PIECE = VD // SIDE
PADDED = 384
COUNT = 1024
TILE = 256
SLOTS = 6
EPSILON = 1e-06
VMEM_LIMIT = 62 * 1024 * 1024
BF = jnp.bfloat16
F32 = jnp.float32
MESH = pl.DeviceIdType.MESH


def layer_norm(values, norm_gain):
    centre = jnp.mean(values, axis=-1, keepdims=True)
    centred = values - centre
    variance = jnp.mean(centred * centred, axis=-1, keepdims=True)
    return centred * lax.rsqrt(variance + EPSILON) * norm_gain


def remote(src, dst, send_sem, recv_sem, where):
    return pltpu.make_async_remote_copy(
        src_ref=src, dst_ref=dst, send_sem=send_sem, recv_sem=recv_sem,
        device_id=where, device_id_type=MESH,
    )


def push(src, dst, send_sem, recv_sem, where):
    copy = remote(src, dst, send_sem, recv_sem, where)
    copy.start()
    return copy


def greet(partners):
    barrier = pltpu.get_barrier_semaphore()
    for where in partners:
        pl.semaphore_signal(barrier, inc=1, device_id=where, device_id_type=MESH)
    pl.semaphore_wait(barrier, len(partners))


def along(index, step):
    return lax.rem(index + step, SIDE)


def behind(index, step):
    return lax.rem(index + SIDE - step, SIDE)


def one_hot(condition):
    return jnp.where(condition, 1.0, 0.0).astype(BF)


def iota(shape, dimension):
    return lax.broadcasted_iota(jnp.int32, shape, dimension)


def segments(index, lengths):
    first = lengths[0, 0]
    second = first + lengths[0, 1]
    return jnp.where(index >= first, 1, 0) + jnp.where(index >= second, 1, 0)


def whole_kernel(
    patches, units, v_gain, v_qkv, v_out, merge_gain, w_merge, routes, text, lengths,
    lang_gain, w_qkv, wo_t, grads,
    out, mg,
    ring, wraw, wmv, w, v_proj, v_scores, v_weights, v_att, v_hidden, pieces, xbuf, part, msend, mrecv, ybuf, tbuf, pick,
    placed, rt, ry, tri, line, gslot,
    zbuf, acc, squares, kv, psend, rbuf, abuf, osend, orec, orel, obuf,
    gbuf, gsend, grec, gz, mz,
    v_sem, l_sem, s_w, r_w, s_rt, r_rt, s_ry, r_ry, s_pl, r_pl, s_mx, r_mx, s_my, r_my, s_t, r_t,
    s_z, r_z, s_x, r_x, s_a, r_a, s_o, r_o, s_e, r_e,
    s_g, r_g, s_gy, r_gy, s_gz, r_gz,
):
    section = lax.axis_index("section")
    x = lax.axis_index("x")
    y = lax.axis_index("y")
    z = lax.axis_index("mp")
    twin = {"section": 1 - section}
    rows = SIDE * HALF
    width = grads.shape[1]
    half = wmv.shape[2]
    plane = [(dx, dz) for dx in range(SIDE) for dz in range(SIDE) if dx or dz]
    left = slice(0, rows // 2)
    right = slice(rows // 2, rows)

    own_merge = pltpu.make_async_copy(
        w_merge.at[pl.ds(pl.multiple_of(section * half, half), half), :],
        wmv.at[y, section], l_sem.at[0],
    )
    own_merge.start()
    v_tiles = [
        pltpu.make_async_copy(
            (v_qkv if tile < 15 else v_out).at[:, pl.ds((tile if tile < 15 else tile - 15) * TILE, TILE)],
            ring.at[tile % SLOTS], v_sem.at[tile % SLOTS],
        )
        for tile in range(20)
    ]
    for tile in range(SLOTS):
        v_tiles[tile].start()
    raw_load = pltpu.make_async_copy(w_qkv.at[0], wraw, l_sem.at[1])
    raw_load.start()
    own_out = pltpu.make_async_copy(
        wo_t.at[0], w.at[section, y, :, pl.ds(PW, QW)], l_sem.at[2]
    )
    own_out.start()
    own_text = pltpu.make_async_copy(
        text.at[:, pl.ds(pl.multiple_of(x * FB, FB), FB)], tbuf.at[x], l_sem.at[3]
    )
    own_text.start()
    own_grads = pltpu.make_async_copy(grads, gbuf.at[x], l_sem.at[4])
    own_grads.start()

    lane = iota((1, COUNT), 1)
    base = ((y * SIDE + x) * SIDE + z) * UNITS
    row = jnp.zeros((1, COUNT), jnp.int32)
    for unit in range(UNITS):
        row = jnp.where(lane == base + unit, routes[0, unit], row)
    placed[...] = row
    rt[x * SIDE + z] = row

    greet(
        [{"x": along(x, dx), "mp": along(z, dz)} for dx, dz in plane]
        + [{"y": along(y, dy)} for dy in STEPS]
        + [twin]
    )

    def shared(number, block, low, high):
        def own_copy(dy):
            return remote(
                block(y), block(y), s_w.at[number, dy], r_w.at[number, dy], {"y": along(y, dy)}
            )

        def up_copy():
            ref = low(behind(y, 1))
            return remote(ref, ref, s_w.at[number, 0], r_w.at[number, 0], {"y": along(y, 1)})

        def down_copy():
            ref = high(along(y, 1))
            return remote(ref, ref, s_w.at[number, 2], r_w.at[number, 2], {"y": along(y, 3)})

        def twin_copy(source):
            return remote(
                block(source), block(source), s_w.at[number, SIDE + source],
                r_w.at[number, SIDE + source], twin,
            )

        def begin():
            own_copy(1).start()
            own_copy(3).start()
            twin_copy(y).start()

        def middle():
            own_copy(1).wait()
            up_copy().start()
            own_copy(3).wait()
            down_copy().start()
            twin_copy(behind(y, 1)).start()
            twin_copy(along(y, 1)).start()

        def end():
            up_copy().wait()
            down_copy().wait()
            twin_copy(along(y, 2)).start()

        def taken():
            for source in range(SIDE):
                twin_copy(source).wait_recv()

        def given():
            for source in range(SIDE):
                twin_copy(source).wait_send()

        return begin, middle, end, taken, given

    mid = wmv.shape[3] // 2
    merge_w = shared(
        0,
        lambda ys: wmv.at[ys, section],
        lambda ys: wmv.at[ys, section, :, pl.ds(0, mid)],
        lambda ys: wmv.at[ys, section, :, pl.ds(mid, mid)],
    )

    def layer_shard(number, layer, first, amount):
        cols = pl.ds(first, amount)
        return shared(
            number,
            lambda ys: w.at[layer, ys, :, cols],
            lambda ys: w.at[layer, ys, pl.ds(0, FB // 2), cols],
            lambda ys: w.at[layer, ys, pl.ds(FB // 2, FB // 2), cols],
        )

    qkv_w = layer_shard(1, 0, 0, PW)
    out_w = layer_shard(2, 0, PW, QW)
    last_q = layer_shard(3, 1, 0, PW)
    last_o = layer_shard(4, 1, PW, QW)

    def only(at, *actions):
        @pl.when(section == at)
        def _():
            for action in actions:
                action()

    own_merge.wait()
    merge_w[0]()
    route_copies = [
        push(
            placed, rt.at[x * SIDE + z], s_rt.at[dx * SIDE + dz], r_rt.at[dx * SIDE + dz],
            {"x": along(x, dx), "mp": along(z, dz)},
        )
        for dx, dz in plane
    ]
    text_copies = []
    for dx in STEPS:
        xt = along(x, dx)
        text_copies.append(
            push(
                text.at[:, pl.ds(pl.multiple_of(xt * FB, FB), FB)], tbuf.at[x],
                s_t.at[dx], r_t.at[dx], {"x": xt},
            )
        )

    order = iota((PATCH, PATCH), 0)
    swap = one_hot(iota((PATCH, PATCH), 1) == (order & 15) * SIDE + (order >> 4))
    patch = jnp.dot(swap, patches[...], preferred_element_type=F32)
    normed = layer_norm(patch, v_gain[...].reshape(1, VD)).astype(BF)
    for tile in range(15):
        v_tiles[tile].wait()
        v_proj[:, tile * TILE : (tile + 1) * TILE] = jnp.dot(
            normed, ring[tile % SLOTS], preferred_element_type=F32
        ).astype(BF)
        if tile + SLOTS < 20:
            v_tiles[tile + SLOTS].start()

    windows = []
    for head in range(VH):
        start = min(head * VHD // 128 * 128, VD - 256)
        lanes = iota((PATCH, 256), 1) + start
        windows.append((start, (lanes >= head * VHD) & (lanes < (head + 1) * VHD)))
    for head, (start, inside) in enumerate(windows):
        query = v_proj[:, start : start + 256].astype(F32)
        query = jnp.where(inside, query, 0.0).astype(BF)
        key = v_proj[:, VD + start : VD + start + 256]
        v_scores[head * PATCH : (head + 1) * PATCH, :] = lax.dot_general(
            query, key, (((1,), (1,)), ((), ())), preferred_element_type=F32
        )
    image_q = segments(iota((VH * PATCH, PATCH), 0) & 15, units)
    image_k = segments(iota((VH * PATCH, PATCH), 1) & 15, units)
    scores = jnp.where(image_q == image_k, v_scores[...] / math.sqrt(VHD), -1e30)
    top = jnp.max(scores, axis=1, keepdims=True)
    weights = jnp.exp(scores - top)
    v_weights[...] = (weights / jnp.sum(weights, axis=1, keepdims=True)).astype(BF)
    v_att[...] = jnp.zeros((PATCH, VD), F32)
    for head, (start, inside) in enumerate(windows):
        mixed = jnp.dot(
            v_weights[head * PATCH : (head + 1) * PATCH, :],
            v_proj[:, 2 * VD + start : 2 * VD + start + 256],
            preferred_element_type=F32,
        )
        v_att[:, start : start + 256] += jnp.where(inside, mixed, 0.0)
    attended = v_att[...].astype(BF)
    for tile in range(5):
        v_tiles[15 + tile].wait()
        cols = slice(tile * TILE, (tile + 1) * TILE)
        v_hidden[:, cols] = (
            patch[:, cols]
            + jnp.dot(attended, ring[(15 + tile) % SLOTS], preferred_element_type=F32)
        ).astype(BF).astype(F32)
    merged = layer_norm(v_hidden[...], merge_gain[...].reshape(1, VD))
    for block in range(SIDE):
        pieces[block, :, :, :PIECE] = merged[:, block * PIECE : (block + 1) * PIECE].astype(BF).reshape(
            SIDE, UNITS, PIECE
        )
        pieces[block, :, :, PIECE:] = jnp.zeros((SIDE, UNITS, PADDED - PIECE), BF)
    plane_copies = []
    for dx, dz in plane:
        xt = along(x, dx)
        plane_copies.append(
            push(
                pieces.at[xt], xbuf.at[x * SIDE + z],
                s_pl.at[dx * SIDE + dz], r_pl.at[dx * SIDE + dz],
                {"x": xt, "mp": along(z, dz)},
            )
        )
    xbuf[x * SIDE + z] = pieces[x]

    merge_w[1]()
    raw_load.wait()
    shard = y * SIDE + x
    gain = lang_gain[:, pl.ds(pl.multiple_of(shard * FB, FB), FB)]
    gain = jnp.transpose(jnp.broadcast_to(gain, (128, FB)))
    for tile in range(PW // 128):
        cols = slice(tile * 128, (tile + 1) * 128)
        w[section, y, :, cols] = (wraw[:, cols].astype(F32) * gain).astype(BF)
    own_out.wait()
    only(0, qkv_w[0])

    for block in range(SIDE):
        before = iota((256, COUNT), 0) + block * 256
        tri[block * 256 : (block + 1) * 256, :] = one_hot(before < iota((256, COUNT), 1))
    for copy in route_copies:
        copy.wait()
    known = rt[0]
    for source in range(1, SIDE * SIDE):
        known = known + rt[source]
    ry[y] = known
    ry_copies = [
        push(ry.at[y], ry.at[y], s_ry.at[dy], r_ry.at[dy], {"y": along(y, dy)})
        for dy in STEPS
    ]
    for copy in plane_copies:
        copy.wait()
    merge_w[2]()
    merge_w[3]()

    def product(dx):
        cols = pl.ds(pl.multiple_of(along(x, dx) * FB, FB), FB)
        total = None
        for patch_at in range(SIDE):
            piece = xbuf[:, patch_at].reshape(SIDE * SIDE * UNITS, PADDED)[:, :PIECE]
            weights = wmv[patch_at, :, :, cols].reshape(PIECE, FB)
            term = jnp.dot(piece, weights, preferred_element_type=F32)
            total = term if total is None else total + term
        return total

    m_copies = []
    for dx in STEPS:
        msend[dx] = product(dx).astype(BF)
        m_copies.append(
            push(msend.at[dx], mrecv.at[dx], s_mx.at[dx], r_mx.at[dx], {"x": along(x, dx)})
        )
    part[...] = product(0)

    for copy in ry_copies:
        copy.wait()
    target = ry[0] + ry[1] + ry[2] + ry[3]
    named = jnp.where(iota((16, COUNT), 0) == target, 1.0, 0.0)
    earlier = jnp.dot(named.astype(BF), tri[...], preferred_element_type=F32)
    position = jnp.sum(named * earlier, axis=0, keepdims=True).astype(jnp.int32)
    slots = (target - y * SIDE) * TOK + position
    for block in range(SIDE):
        wanted = iota((TOK, COUNT), 0) + block * TOK
        pick[block * TOK : (block + 1) * TOK, :] = one_hot(wanted == slots)
    line[...] = jnp.where((target >> 2) == y, (target & 3) * TOK + position + 1, 0)
    down = iota((256, COUNT), 0)
    chosen_rows = one_hot(iota((256, COUNT), 1) == (down >> 6) * 256 + x * 64 + (down & 63))

    def upright(values):
        wide = jnp.broadcast_to(values.astype(F32), (128, COUNT)).astype(BF)
        return lax.dot_general(
            chosen_rows, wide, (((1,), (1,)), ((), ())), preferred_element_type=F32
        )

    slot_line = line[...]
    gslot[...] = (
        16.0 * upright(slot_line >> 4) + upright(slot_line & 15)
    ).astype(jnp.int32) - 1

    only(0, qkv_w[1])
    for copy in m_copies:
        copy.wait()
    grad_copies = [
        push(grads, gbuf.at[x], s_g.at[dx], r_g.at[dx], {"x": along(x, dx)}) for dx in (1, 3)
    ]
    total = part[...]
    for dx in STEPS:
        total = total + mrecv[dx].astype(F32)
    ybuf[y] = total.astype(BF)
    y_copies = [
        push(ybuf.at[y], ybuf.at[y], s_my.at[dy], r_my.at[dy], {"y": along(y, dy)})
        for dy in STEPS
    ]
    present = jnp.dot(pick[...], jnp.ones((COUNT, 128), BF), preferred_element_type=F32)
    own_text.wait()
    for copy in text_copies:
        copy.wait()
    for copy in y_copies:
        copy.wait()
    only(0, out_w[0])
    picked = jnp.dot(
        pick[...], ybuf[...].reshape(COUNT, FB), preferred_element_type=F32
    ).astype(BF)
    for group in range(SIDE):
        for part_of in range(2):
            span = slice(group * TOK + part_of * HALF, group * TOK + (part_of + 1) * HALF)
            to = slice(group * HALF, (group + 1) * HALF)
            inside = slice(part_of * HALF, (part_of + 1) * HALF)
            for tile in range(FB // 128):
                cols = slice(tile * 128, (tile + 1) * 128)
                zbuf[part_of, z, to, cols] = jnp.where(
                    present[span, :] > 0.5, picked[span, cols], tbuf[group, inside, cols]
                )

    z_copies, f_copies, x_copies, a_copies, o_copies, e_copies = {}, {}, {}, {}, {}, []

    def spread(layer, part):
        z_copies[layer, part] = {
            dz: push(
                zbuf.at[part, z], zbuf.at[part, z],
                s_z.at[layer, part, dz], r_z.at[layer, part, dz], {"mp": along(z, dz)},
            )
            for dz in (1, 3)
        }

    def times(layer, part, dz):
        zs = behind(z, dz)
        wide = zbuf[part, zs].astype(F32)
        squared = jnp.sum(wide * wide, axis=1, keepdims=True)
        if dz:
            squares[part] += jnp.broadcast_to(squared, (rows, HD))
        else:
            squares[part] = jnp.broadcast_to(squared, (rows, HD))

        product = jnp.dot(
            zbuf[part, zs], w[layer, zs, :, :PW], preferred_element_type=F32
        )
        if dz:
            acc[part] += product
        else:
            acc[part] = product

    def passed(layer, part):
        copies = z_copies[layer, part]
        copies[1].wait()
        zs = behind(z, 1)
        f_copies[layer, part] = [
            push(
                zbuf.at[part, zs, left], zbuf.at[part, zs, left],
                s_z.at[layer, part, 0], r_z.at[layer, part, 0], {"mp": along(z, 1)},
            )
        ]
        copies[3].wait()
        zs = along(z, 1)
        f_copies[layer, part].append(
            push(
                zbuf.at[part, zs, right], zbuf.at[part, zs, right],
                s_z.at[layer, part, 2], r_z.at[layer, part, 2], {"mp": along(z, 3)},
            )
        )

    def own_part(layer, part):
        times(layer, part, 0)

    def project(layer, part):
        times(layer, part, 1)
        times(layer, part, 3)
        for copy in f_copies[layer, part]:
            copy.wait()
        times(layer, part, 2)
        lane = lax.broadcasted_iota(jnp.int32, (HALF, HD), 1)
        copies = []
        for dx in STEPS:
            xt = along(x, dx)
            span = pl.ds(pl.multiple_of(xt * HALF, HALF), HALF)
            psend[part, dx, :, :PW] = acc[part, span, :].astype(BF)
            sq = squares[part, span, :]
            high = sq.astype(BF)
            low = (sq - high.astype(F32)).astype(BF)
            psend[part, dx, :, PW:] = jnp.where(lane < 64, high, low)
            copies.append(
                push(
                    psend.at[part, dx], rbuf.at[part, dx],
                    s_x.at[layer, part, dx], r_x.at[layer, part, dx], {"x": xt},
                )
            )
        x_copies[layer, part] = copies

    def attend(layer, part):
        own = pl.ds(pl.multiple_of(x * HALF, HALF), HALF)
        total = acc[part, own, :]
        sq = squares[part, own, :][:, :1]
        for copy in x_copies[layer, part]:
            copy.wait()
        for dx in STEPS:
            total = total + rbuf[part, dx, :, :PW].astype(F32)
            tail = rbuf[part, dx, :, PW:].astype(F32)
            sq = sq + tail[:, :1] + tail[:, 64:65]
        projected = (total * lax.rsqrt(sq / D + EPSILON)).astype(BF)
        kv[part * HALF : (part + 1) * HALF, :] = projected[:, QW:]
        seen = (part + 1) * HALF
        keys = kv[:seen, :HD]
        values = kv[:seen, HD:]
        queries = jnp.concatenate(
            [projected[:, head * HD : (head + 1) * HD] for head in range(HEADS)], axis=0
        )
        at = iota((HALF, seen), 0) + part * HALF
        key_at = iota((HALF, seen), 1)
        allowed = jnp.where(
            (segments(at, lengths) == segments(key_at, lengths)) & (at >= key_at), 1.0, 0.0
        )
        allowed = jnp.concatenate([allowed] * HEADS, axis=0) > 0.5
        scores = lax.dot_general(
            queries, keys, (((1,), (1,)), ((), ())), preferred_element_type=F32
        ) * (1.0 / math.sqrt(HD))
        scores = jnp.where(allowed, scores, -1e30)
        top = jnp.max(scores, axis=1, keepdims=True)
        weights = jnp.exp(scores - top)
        weights = (weights / jnp.sum(weights, axis=1, keepdims=True)).astype(BF)
        mixed = jnp.dot(weights, values, preferred_element_type=F32).astype(BF)
        for head in range(HEADS):
            abuf[part, x, :, head * HD : (head + 1) * HD] = mixed[
                head * HALF : (head + 1) * HALF, :
            ]
        a_copies[layer, part] = [
            push(
                abuf.at[part, x], abuf.at[part, x],
                s_a.at[layer, part, dx], r_a.at[layer, part, dx], {"x": along(x, dx)},
            )
            for dx in STEPS
        ]

    def output(layer, part):
        for copy in a_copies[layer, part]:
            copy.wait()
        copies = {}

        def send(name, src, dst, dz):
            copies[name] = push(
                src, dst, s_o.at[layer, part, name], r_o.at[layer, part, name],
                {"mp": along(z, dz)},
            )

        for dz in (2, 1, 3, 0):
            zt = along(z, dz)

            osend[part, dz] = lax.dot_general(
                abuf[part].reshape(rows, QW), w[layer, zt, :, PW:],
                (((1,), (1,)), ((), ())), preferred_element_type=F32,
            ).astype(BF)

            if dz == 2:
                send(0, osend.at[part, 2, left], orel.at[part, 0], 1)
                send(1, osend.at[part, 2, right], orel.at[part, 1], 3)
            elif dz == 1:
                send(2, osend.at[part, 1, right], orec.at[part, 0, right], 1)
            elif dz == 3:
                send(3, osend.at[part, 3, left], orec.at[part, 1, left], 3)
        o_copies[layer, part] = copies, send

    def relay(layer, part):
        copies, send = o_copies[layer, part]
        copies[0].wait()
        osend[part, 1, left] = (
            osend[part, 1, left].astype(F32) + orel[part, 0].astype(F32)
        ).astype(BF)
        send(4, osend.at[part, 1, left], orec.at[part, 0, left], 1)
        copies[1].wait()
        osend[part, 3, right] = (
            osend[part, 3, right].astype(F32) + orel[part, 1].astype(F32)
        ).astype(BF)
        send(5, osend.at[part, 3, right], orec.at[part, 1, right], 3)

    def finish(layer, part):
        update = osend[part, 0].astype(F32)
        copies, _ = o_copies[layer, part]
        for name in (2, 3, 4, 5):
            copies[name].wait()
        for side in range(2):
            update = update + orec[part, side].astype(F32)
        fresh = (zbuf[part, z].astype(F32) + update).astype(BF)
        if layer == 0:
            zbuf[part, z] = fresh
            return
        osend[part, 0] = fresh
        for dx in STEPS:
            xt = along(x, dx)
            e_copies.append(
                push(
                    osend.at[part, 0, pl.ds(pl.multiple_of(xt * HALF, HALF), HALF), :],
                    obuf.at[x, part],
                    s_e.at[part, dx], r_e.at[part, dx], {"x": xt},
                )
            )
        obuf[x, part] = osend[part, 0, pl.ds(pl.multiple_of(x * HALF, HALF), HALF), :
        ]

    spread(0, 0)
    grad_copies[0].wait()
    from_left = gbuf.at[behind(x, 1), pl.ds(0, HALF), :]
    grad_copies[1].wait()
    from_right = gbuf.at[along(x, 1), pl.ds(HALF, HALF), :]
    grad_copies = [
        push(from_left, from_left, s_g.at[0], r_g.at[0], {"x": along(x, 1)}),
        push(from_right, from_right, s_g.at[2], r_g.at[2], {"x": along(x, 3)}),
    ]
    g_copies, gz_copies = [], []

    def ready_qkv(layer, part):
        only(0, qkv_w[2])
        only(1, qkv_w[3])

    def ready_out(layer, part):
        only(0, out_w[2])
        only(1, last_q[1], last_o[0], out_w[3])

    def pass_out(layer, part):
        only(0, out_w[1])
        only(1, last_q[0])

    def ready_last(layer, part):
        only(1, last_q[2], last_o[1])
        only(0, last_q[3])

    def ready_end(layer, part):
        only(1, last_o[2])
        only(0, last_o[3])

    def choose(layer, part):
        own_grads.wait()
        for copy in grad_copies:
            copy.wait()
        for dy in (1, 3, 2, 0):
            yt = along(y, dy)
            wanted = gslot[pl.ds(pl.multiple_of(yt * 64, 64), 64), :1]
            chosen = one_hot(iota((64, SIDE * TOK), 1) == wanted)
            gsend[dy] = jnp.dot(
                chosen, gbuf[...].reshape(SIDE * TOK, width), preferred_element_type=F32
            ).astype(BF)
            if dy:
                g_copies.append(
                    push(gsend.at[dy], grec.at[dy], s_gy.at[dy], r_gy.at[dy], {"y": yt})
                )

    def hand(layer, part):
        for copy in g_copies:
            copy.wait()
        found = gsend[0].astype(F32)
        for dy in STEPS:
            found = found + grec[dy].astype(F32)
        gz[...] = found.astype(BF).reshape(SIDE, UNITS, width)
        for dz in STEPS:
            zt = along(z, dz)
            gz_copies.append(
                push(gz.at[zt], mz.at[z], s_gz.at[dz], r_gz.at[dz], {"mp": zt})
            )
        mz[z] = gz[z]

    for stage, layer, part_at in (
        (ready_qkv, 0, 0),
        (own_part, 0, 0),
        (passed, 0, 0),
        (spread, 0, 1),
        (project, 0, 0),
        (pass_out, 0, 0),
        (own_part, 0, 1),
        (attend, 0, 0),
        (passed, 0, 1),
        (project, 0, 1),
        (ready_out, 0, 0),
        (output, 0, 0),
        (attend, 0, 1),
        (relay, 0, 0),
        (output, 0, 1),
        (finish, 0, 0),
        (spread, 1, 0),
        (relay, 0, 1),
        (ready_last, 1, 0),
        (own_part, 1, 0),
        (passed, 1, 0),
        (finish, 0, 1),
        (spread, 1, 1),
        (project, 1, 0),
        (own_part, 1, 1),
        (attend, 1, 0),
        (choose, 1, 0),
        (passed, 1, 1),
        (project, 1, 1),
        (ready_end, 1, 0),
        (output, 1, 0),
        (attend, 1, 1),
        (relay, 1, 0),
        (output, 1, 1),
        (hand, 1, 0),
        (finish, 1, 0),
        (relay, 1, 1),
        (finish, 1, 1),
    ):
        stage(layer, part_at)

    for copy in gz_copies:
        copy.wait()
    for block in range(SIDE):
        mg[:, block * width : (block + 1) * width] = mz[block]
    for copy in e_copies:
        copy.wait()
    for block in range(SIDE):
        for part_of in range(2):
            out[part_of * HALF : (part_of + 1) * HALF, block * FB : (block + 1) * FB] = obuf[
                block, part_of
            ]
    merge_w[4]()
    only(0, qkv_w[4], out_w[4])
    only(1, last_q[4], last_o[4])


def shards(*arrays):
    vmem = pl.BlockSpec(memory_space=pltpu.VMEM)
    smem = pl.BlockSpec(memory_space=pltpu.SMEM)
    hbm = pl.BlockSpec(memory_space=pl.ANY)
    dma = pltpu.SemaphoreType.DMA
    rows = SIDE * HALF
    width = arrays[13].shape[1]
    half = arrays[6].shape[0] // 2
    stage = dma((2, 2, SIDE))
    four, plane = dma((SIDE,)), dma((SIDE * SIDE,))
    call = pl.pallas_call(
        whole_kernel,
        out_shape=(
            jax.ShapeDtypeStruct((TOK, SIDE * FB), BF),
            jax.ShapeDtypeStruct((UNITS, SIDE * width), BF),
        ),
        in_specs=[vmem, smem, vmem, hbm, hbm, vmem, hbm, smem, hbm, smem, vmem, hbm, hbm, hbm],
        out_specs=(vmem, vmem),
        scratch_shapes=[
            pltpu.VMEM((SLOTS, VD, TILE), BF),
            pltpu.VMEM((FB, PW), BF),
            pltpu.VMEM((SIDE, 2, half, SIDE * FB), BF),
            pltpu.VMEM((2, SIDE, FB, PW + QW), BF),
            pltpu.VMEM((PATCH, 3 * VD), BF),
            pltpu.VMEM((VH * PATCH, PATCH), F32),
            pltpu.VMEM((VH * PATCH, PATCH), BF),
            pltpu.VMEM((PATCH, VD), F32),
            pltpu.VMEM((PATCH, VD), F32),
            pltpu.VMEM((SIDE, SIDE, UNITS, PADDED), BF),
            pltpu.VMEM((SIDE * SIDE, SIDE, UNITS, PADDED), BF),
            pltpu.VMEM((256, FB), F32),
            pltpu.VMEM((SIDE, 256, FB), BF),
            pltpu.VMEM((SIDE, 256, FB), BF),
            pltpu.VMEM((SIDE, 256, FB), BF),
            pltpu.VMEM((SIDE, TOK, FB), BF),
            pltpu.VMEM((SIDE * TOK, COUNT), BF),
            pltpu.VMEM((1, COUNT), jnp.int32),
            pltpu.VMEM((SIDE * SIDE, 1, COUNT), jnp.int32),
            pltpu.VMEM((SIDE, 1, COUNT), jnp.int32),
            pltpu.VMEM((COUNT, COUNT), BF),
            pltpu.VMEM((1, COUNT), jnp.int32),
            pltpu.VMEM((256, 128), jnp.int32),
            pltpu.VMEM((2, SIDE, rows, FB), BF),
            pltpu.VMEM((2, rows, PW), F32),
            pltpu.VMEM((2, rows, HD), F32),
            pltpu.VMEM((TOK, 2 * HD), BF),
            pltpu.VMEM((2, SIDE, HALF, PT), BF),
            pltpu.VMEM((2, SIDE, HALF, PT), BF),
            pltpu.VMEM((2, SIDE, HALF, QW), BF),
            pltpu.VMEM((2, SIDE, rows, FB), BF),
            pltpu.VMEM((2, 2, rows, FB), BF),
            pltpu.VMEM((2, 2, rows // 2, FB), BF),
            pltpu.VMEM((SIDE, 2, HALF, FB), BF),
            pltpu.VMEM((SIDE, TOK, width), BF),
            pltpu.VMEM((SIDE, 64, width), BF),
            pltpu.VMEM((SIDE, 64, width), BF),
            pltpu.VMEM((SIDE, UNITS, width), BF),
            pltpu.VMEM((SIDE, UNITS, width), BF),
            dma((SLOTS,)), dma((5,)), dma((5, 8)), dma((5, 8)),
            plane, plane, four, four, plane, plane, four, four, four, four, four, four,
            stage, stage, stage, stage, stage, stage, dma((2, 2, 6)), dma((2, 2, 6)),
            dma((2, SIDE)), dma((2, SIDE)),
            four, four, four, four, four, four,
        ],
        compiler_params=pltpu.CompilerParams(
            collective_id=1, has_side_effects=True, vmem_limit_bytes=VMEM_LIMIT
        ),
        name="whole",
    )
    arrays = list(arrays)
    arrays[7] = arrays[7].reshape(1, UNITS)
    return call(*arrays)


def solution(mesh):
    grid = jax.sharding.Mesh(
        mesh.devices.reshape(2, SIDE, SIDE, SIDE), ("section", "y", "x", "mp")
    )
    every = ("section", "y", "x", "mp")
    home = P(("section", "y", "x"), "mp")
    in_specs = (
        P(every, None),
        P(every, None),
        P(),
        P(),
        P(),
        P(),
        P(("y", "x"), "mp"),
        P(every, None),
        home,
        P(("section", "y", "x"), None),
        P("section", None),
        P("section", ("y", "x"), "mp"),
        P("section", ("y", "x"), "mp"),
        home,
    )
    out_specs = (home, P(every, None))
    return jax.shard_map(shards, mesh=grid, in_specs=in_specs, out_specs=out_specs, check_vma=False)
```
